128 devices in a mesh: gx: 4 (over x), gy: 4 (over z), gz: 8 (over y, core).
Axes of the slice: x: 4, y: 4, z: 4, core: 2. Of those that a mesh axis runs over, the one named last changes fastest.
Arguments:
- element_load: float32 [36, 36, 72, 128], P('gx', 'gy', 'gz'), may hold values from -90 to 90
- local_matrix: float32 [4, 4, 8, 729, 729], P('gx', 'gy', 'gz'), may hold values from -10 to 61, as said below
- dirichlet_inverse: float32 [4, 4, 8, 343, 343], P('gx', 'gy', 'gz'), as said below
- neumann_inverse: float32 [4, 4, 8, 729, 729], P('gx', 'gy', 'gz'), as said below
- coarse_basis: float32 [4, 4, 8, 20, 729], P('gx', 'gy', 'gz'), as said below
Outputs:
- solution: float32 [36, 36, 72, 128], P('gx', 'gy', 'gz')
- residual: float32 [36, 36, 72, 128], P('gx', 'gy', 'gz')
The draws below stay inside these ranges and needn't reach their ends.
Inputs may be any that keep to these rules, and one draw needn't show every extreme that they name: `local_matrix`: block (a, b, c) is the symmetric positive definite stiffness matrix of subdomain (a, b, c) in the node order of the steps: cellwise conductivities on the couplings of neighbouring nodes plus a lumped reaction term. `dirichlet_inverse`: block (a, b, c) is the inverse, computed in float32, of local_matrix's block restricted to the inner nodes. `neumann_inverse`: block (a, b, c) is the node-by-node block of the inverse, computed in float32, of the saddle-point matrix [[A, Cm^T], [Cm, 0]], with A local_matrix's block and Cm the 20 x 729 primal constraints in the order of the coarse numbering: the value at each of the 8 corners, then the mean over the 7 inner nodes of each of the 12 edges. `coarse_basis`: block (a, b, c) is the constraint-by-node block of that same saddle-point inverse.
All inputs are finite; a program needn't handle non-finite values.
Results may differ from the reference program's by a relative error of at most 0.0014.
Values sent between devices are 32-bit elements; how exact they have to be, the bound alone decides.
A program may use at most 128 MiB of HBM per device.

```python
import jax
import jax.numpy as jnp
import numpy as np
from jax import lax

CELLS = 8
PRIMAL = 20
RHS = 128
ITERS = 2
N_GX = 4
N_GY = 4
N_GZ = 8


REACTION = 0.004


def conductivity(key):
    shape = (N_GX * N_GY * N_GZ, CELLS, CELLS, CELLS)
    subkey = jax.random.fold_in(key, 7)
    logs = jax.random.uniform(subkey, shape, jnp.float32, np.log(0.3), np.log(3.0))
    return jnp.exp(logs)


def stiffness_of(kappa):
    node_side = CELLS + 1
    node_count = node_side ** 3
    index = jnp.arange(node_count, dtype=jnp.int32).reshape(node_side, node_side, node_side)
    padded = jnp.pad(kappa, 1)
    part_x = padded[1:-1, :, :]
    weight_x = (part_x[:, :-1, :-1] + part_x[:, 1:, :-1] + part_x[:, :-1, 1:] + part_x[:, 1:, 1:]) / 4.0
    part_y = padded[:, 1:-1, :]
    weight_y = (part_y[:-1, :, :-1] + part_y[1:, :, :-1] + part_y[:-1, :, 1:] + part_y[1:, :, 1:]) / 4.0
    part_z = padded[:, :, 1:-1]
    weight_z = (part_z[:-1, :-1, :] + part_z[1:, :-1, :] + part_z[:-1, 1:, :] + part_z[1:, 1:, :]) / 4.0
    pairs = ((weight_x, index[:-1, :, :], index[1:, :, :]), (weight_y, index[:, :-1, :], index[:, 1:, :]), (weight_z, index[:, :, :-1], index[:, :, 1:]))
    matrix = jnp.zeros((node_count, node_count), jnp.float32)
    for weights, lower, upper in pairs:
        weights = weights.reshape(-1)
        lower = lower.reshape(-1)
        upper = upper.reshape(-1)
        matrix = matrix.at[lower, lower].add(weights).at[upper, upper].add(weights)
        matrix = matrix.at[lower, upper].add(-weights).at[upper, lower].add(-weights)
    cell_pad = jnp.pad(jnp.ones((CELLS, CELLS, CELLS), jnp.float32), 1)
    adjacent = jnp.zeros((node_side, node_side, node_side), jnp.float32)
    for shift_x in (0, 1):
        for shift_y in (0, 1):
            for shift_z in (0, 1):
                adjacent = adjacent + cell_pad[shift_x:shift_x + node_side, shift_y:shift_y + node_side, shift_z:shift_z + node_side]
    return matrix + jnp.diag(REACTION * adjacent.reshape(-1) / 8.0)


def constraint_table():
    node_side = CELLS + 1
    node_count = node_side ** 3
    top_index = node_side - 1
    table = np.zeros((20, node_count), np.float32)

    def node_at(first_i, second_j, third_k):
        return (first_i * node_side + second_j) * node_side + third_k
    row = 0
    for sx in (0, 1):
        for sy in (0, 1):
            for sz in (0, 1):
                table[row, node_at(sx * top_index, sy * top_index, sz * top_index)] = 1.0
                row += 1
    for sy in (0, 1):
        for sz in (0, 1):
            for place in range(1, top_index):
                table[row, node_at(place, sy * top_index, sz * top_index)] = 1.0 / (top_index - 1)
            row += 1
    for sx in (0, 1):
        for sz in (0, 1):
            for place in range(1, top_index):
                table[row, node_at(sx * top_index, place, sz * top_index)] = 1.0 / (top_index - 1)
            row += 1
    for sx in (0, 1):
        for sy in (0, 1):
            for place in range(1, top_index):
                table[row, node_at(sx * top_index, sy * top_index, place)] = 1.0 / (top_index - 1)
            row += 1
    return table


def all_stiffness(key):
    return jax.vmap(stiffness_of)(conductivity(key))


def saddle_inverse(matrix):
    table = jnp.asarray(constraint_table())
    zeros_block = jnp.zeros((table.shape[0], table.shape[0]), jnp.float32)
    saddle = jnp.concatenate([jnp.concatenate([matrix, table.T], axis=1), jnp.concatenate([table, zeros_block], axis=1)], axis=0)
    return jnp.linalg.inv(saddle)


def draw_local_matrix(key, part):
    node_count = (CELLS + 1) ** 3
    return all_stiffness(key).reshape(N_GX, N_GY, N_GZ, node_count, node_count)


def draw_dirichlet_inverse(key, part):
    node_side = CELLS + 1
    inner_count = (CELLS - 1) ** 3
    matrices = all_stiffness(key)
    shaped = matrices.reshape(-1, node_side, node_side, node_side, node_side, node_side, node_side)
    inner = shaped[:, 1:-1, 1:-1, 1:-1, 1:-1, 1:-1, 1:-1].reshape(-1, inner_count, inner_count)
    inverse = jnp.linalg.inv(inner)
    inverse = 0.5 * (inverse + jnp.swapaxes(inverse, 1, 2))
    return inverse.reshape(N_GX, N_GY, N_GZ, inner_count, inner_count)


def draw_neumann_inverse(key, part):
    node_count = (CELLS + 1) ** 3
    inverse = jax.vmap(saddle_inverse)(all_stiffness(key))
    top_block = inverse[:, :node_count, :node_count]
    top_block = 0.5 * (top_block + jnp.swapaxes(top_block, 1, 2))
    return top_block.reshape(N_GX, N_GY, N_GZ, node_count, node_count)


def draw_coarse_basis(key, part):
    node_count = (CELLS + 1) ** 3
    inverse = jax.vmap(saddle_inverse)(all_stiffness(key))
    lower_block = inverse[:, node_count:, :node_count]
    upper_block = jnp.swapaxes(inverse[:, :node_count, node_count:], 1, 2)
    basis = 0.5 * (lower_block + upper_block)
    return basis.reshape(N_GX, N_GY, N_GZ, 20, node_count)


def draw_element_load(key, part):
    node_side = CELLS + 1
    devices = N_GX * N_GY * N_GZ
    noise = jax.random.normal(jax.random.fold_in(key, 31), (N_GX, node_side, N_GY, node_side, N_GZ, node_side, RHS), jnp.float32)
    noise = jnp.clip(noise, -4.0, 4.0)
    column_scale = jnp.exp(jax.random.uniform(jax.random.fold_in(key, 37), (RHS,), jnp.float32, np.log(0.3), np.log(3.0)))
    linear = jnp.arange(N_GX, dtype=jnp.float32)[:, None, None, None, None, None, None] * (N_GY * N_GZ) + jnp.arange(N_GY, dtype=jnp.float32)[None, None, :, None, None, None, None] * N_GZ + jnp.arange(N_GZ, dtype=jnp.float32)[None, None, None, None, :, None, None]
    fraction = linear / max(devices - 1, 1)
    values = noise * column_scale * jnp.exp(fraction * np.log(3.0))
    values = jnp.clip(values, -90.0, 90.0)
    return values.reshape(N_GX * node_side, N_GY * node_side, N_GZ * node_side, RHS)


def setup_inputs(seed: int = 0) -> dict:
    key_of = jax.random.split(jax.random.key(seed), 6)
    element_load = draw_element_load(jax.random.fold_in(key_of[5], 71), 0)
    local_matrix = draw_local_matrix(jax.random.fold_in(key_of[5], 71), 0)
    dirichlet_inverse = draw_dirichlet_inverse(jax.random.fold_in(key_of[5], 71), 0)
    neumann_inverse = draw_neumann_inverse(jax.random.fold_in(key_of[5], 71), 0)
    coarse_basis = draw_coarse_basis(jax.random.fold_in(key_of[5], 71), 0)
    return dict(element_load=element_load, local_matrix=local_matrix, dirichlet_inverse=dirichlet_inverse, neumann_inverse=neumann_inverse, coarse_basis=coarse_basis)


def coarse_ids(along_x, along_y, along_z, count_x, count_y, count_z):
    total = count_x * count_y * count_z

    def vertex(shift_x, shift_y, shift_z):
        return ((along_x + shift_x) % count_x * count_y + (along_y + shift_y) % count_y) * count_z + (along_z + shift_z) % count_z
    listed = [vertex(sx, sy, sz) for sx in (0, 1) for sy in (0, 1) for sz in (0, 1)]
    listed += [total + vertex(0, sy, sz) for sy in (0, 1) for sz in (0, 1)]
    listed += [2 * total + vertex(sx, 0, sz) for sx in (0, 1) for sz in (0, 1)]
    listed += [3 * total + vertex(sx, sy, 0) for sx in (0, 1) for sy in (0, 1)]
    return jnp.stack(listed, axis=-1).astype(jnp.int32)

def node_weights(node_side):
    places = jnp.arange(node_side, dtype=jnp.int32)
    on_rim = ((places == 0) | (places == node_side - 1)).astype(jnp.int32)
    rims = on_rim[:, None, None] + on_rim[None, :, None] + on_rim[None, None, :]
    copies = (1.0 + on_rim[:, None, None].astype(jnp.float32)) * (1.0 + on_rim[None, :, None].astype(jnp.float32)) * (1.0 + on_rim[None, None, :].astype(jnp.float32))
    share = (1.0 / copies)[..., None]
    border = jnp.where(rims[..., None] > 0, share, jnp.zeros_like(share))
    return (share, border)

def fold_axis(field, block_axis, node_axis):
    moved = jnp.moveaxis(field, (block_axis, node_axis), (0, 1))
    from_low = jnp.roll(moved[:, -1], 1, axis=0)
    from_high = jnp.roll(moved[:, 0], -1, axis=0)
    moved = moved.at[:, 0].add(from_low)
    moved = moved.at[:, -1].add(from_high)
    return jnp.moveaxis(moved, (0, 1), (block_axis, node_axis))

def assemble(field):
    for block_axis, node_axis in ((0, 3), (1, 4), (2, 5)):
        field = fold_axis(field, block_axis, node_axis)
    return field

def reference(element_load, local_matrix, dirichlet_inverse, neumann_inverse, coarse_basis):
    highest = lax.Precision.HIGHEST
    node_side = CELLS + 1
    node_count = node_side ** 3
    inner_side = node_side - 2
    inner_count = inner_side ** 3
    rhs_count = element_load.shape[-1]
    devices = N_GX * N_GY * N_GZ
    coarse_count = 4 * devices
    cube_shape = (N_GX, N_GY, N_GZ, node_side, node_side, node_side, rhs_count)
    inner_shape = (N_GX, N_GY, N_GZ, inner_side, inner_side, inner_side, rhs_count)

    def to_blocks(field):
        return field.reshape(N_GX, node_side, N_GY, node_side, N_GZ, node_side, rhs_count).transpose(0, 2, 4, 1, 3, 5, 6)

    def from_blocks(field):
        return field.transpose(0, 3, 1, 4, 2, 5, 6).reshape(N_GX * node_side, N_GY * node_side, N_GZ * node_side, rhs_count)
    stiffness = local_matrix.reshape(devices, node_count, node_count)
    stiff_cols = stiffness.reshape(devices, node_count, node_side, node_side, node_side)[:, :, 1:-1, 1:-1, 1:-1].reshape(devices, node_count, inner_count)
    stiff_rows = stiffness.reshape(devices, node_side, node_side, node_side, node_count)[:, 1:-1, 1:-1, 1:-1].reshape(devices, inner_count, node_count)
    interior_inverse = dirichlet_inverse.reshape(devices, inner_count, inner_count)
    neumann = neumann_inverse.reshape(devices, node_count, node_count)
    basis = coarse_basis.reshape(devices, PRIMAL, node_count)
    share, border = node_weights(node_side)
    grid_shape = (N_GX, N_GY, N_GZ)
    along_x = jnp.broadcast_to(jnp.arange(N_GX, dtype=jnp.int32)[:, None, None], grid_shape)
    along_y = jnp.broadcast_to(jnp.arange(N_GY, dtype=jnp.int32)[None, :, None], grid_shape)
    along_z = jnp.broadcast_to(jnp.arange(N_GZ, dtype=jnp.int32)[None, None, :], grid_shape)
    numbers = coarse_ids(along_x, along_y, along_z, N_GX, N_GY, N_GZ).reshape(devices, PRIMAL)
    indicator = (numbers[:, :, None] == jnp.arange(coarse_count, dtype=jnp.int32)[None, None, :]).astype(jnp.float32)

    def product(matrix, flat):
        return jnp.einsum('zmn,znk->zmk', matrix, flat, precision=highest)
    stiff_basis = jnp.einsum('znm,zqm->znq', stiffness, basis, precision=highest)
    coarse_local = jnp.einsum('zpn,znq->zpq', basis, stiff_basis, precision=highest)
    partial_rows = jnp.einsum('zpm,zpq->zmq', indicator, coarse_local, precision=highest)
    coarse_matrix = jnp.einsum('zmq,zqn->mn', partial_rows, indicator, precision=highest)
    factor = jnp.linalg.cholesky(coarse_matrix)

    def dot_all(left, right):
        return jnp.sum(left * right * share, axis=(0, 1, 2, 3, 4, 5))

    def apply_operator(field):
        return assemble(product(stiffness, field.reshape(devices, node_count, rhs_count)).reshape(cube_shape))

    def precondition(current):
        inner_part = current[:, :, :, 1:-1, 1:-1, 1:-1].reshape(devices, inner_count, rhs_count)
        start = product(interior_inverse, inner_part)
        spill = product(stiff_cols, start).reshape(cube_shape)
        first_residual = current - assemble(spill)
        weighted = (border * first_residual).reshape(devices, node_count, rhs_count)
        local_part = product(neumann, weighted)
        primal_load = product(basis, weighted)
        coarse_rhs = jnp.einsum('zpm,zpk->mk', indicator, primal_load, precision=highest)
        coarse_values = jax.scipy.linalg.cho_solve((factor, True), coarse_rhs)
        primal_values = jnp.einsum('zpm,mk->zpk', indicator, coarse_values, precision=highest)
        combined = local_part + jnp.einsum('zpn,zpk->znk', basis, primal_values, precision=highest)
        surface = assemble(border * combined.reshape(cube_shape))
        inner_new = start - product(interior_inverse, product(stiff_rows, surface.reshape(devices, node_count, rhs_count)))
        padded = jnp.pad(inner_new.reshape(inner_shape), ((0, 0), (0, 0), (0, 0), (1, 1), (1, 1), (1, 1), (0, 0)))
        return surface + padded
    right_side = assemble(to_blocks(element_load))
    solution = jnp.zeros(cube_shape, jnp.float32)
    residual = right_side
    precond_now = precondition(residual)
    direction = precond_now
    energy = dot_all(residual, precond_now)
    for iteration in range(ITERS):
        mapped = apply_operator(direction)
        step_size = energy / dot_all(direction, mapped)
        solution = solution + step_size * direction
        residual = residual - step_size * mapped
        if iteration + 1 < ITERS:
            precond_now = precondition(residual)
            energy_next = dot_all(residual, precond_now)
            direction = precond_now + energy_next / energy * direction
            energy = energy_next
    return (from_blocks(solution), from_blocks(residual))
```

```python
import functools

import jax
import jax.numpy as jnp
import numpy as np
from jax import lax
from jax.experimental import pallas as pl
from jax.experimental.pallas import tpu as pltpu
from jax.sharding import PartitionSpec as P

MESH = pl.DeviceIdType.MESH
F32, BF16 = jnp.float32, jnp.bfloat16
GX, GY, GZ = 4, 4, 8
M = 9
NODES, NB, NI, RHS = 729, 392, 343, 128
ORDER = (1, 3, 5, 7, 2, 6, 0, 4)
VM = pl.BlockSpec(memory_space=pltpu.VMEM)

_g = np.indices((M, M, M)).reshape(3, -1)
_rim = ((_g == 0) | (_g == M - 1)).sum(0)
B_IDS, I_IDS = np.where(_rim > 0)[0], np.where(_rim == 0)[0]
B_POS = {int(n): r for r, n in enumerate(B_IDS)}


def one_hot(rows, cols, shape):
    out = np.zeros(shape, np.float32)
    out[rows, cols] = 1.0
    return out


PB = one_hot(np.arange(len(B_IDS)), B_IDS, (NB, NODES))
PI = one_hot(np.arange(NI), I_IDS, (NI, NODES))
WEIGHT = np.zeros((NB, 1), np.float32)
WEIGHT[: len(B_IDS), 0] = 1.0 / 2.0 ** _rim[B_IDS]
WEIGHT = np.broadcast_to(WEIGHT, (NB, RHS)).copy()

DIRS = sorted(
    ((x, y, z) for x in (-1, 0, 1) for y in (-1, 0, 1) for z in (-1, 0, 1) if (x, y, z) != (0, 0, 0)),
    key=lambda d: (sum(map(abs, d)), d),
)
SIZE = {1: 88, 2: 16, 3: 8}
OFFS, _at = {}, 0
for _d in DIRS:
    OFFS[_d] = (_at, SIZE[sum(map(abs, _d))])
    _at += OFFS[_d][1]
NS = _at
PK = np.zeros((NS, NB), np.float32)
for _d in DIRS:
    _sel = [[0] if v == -1 else [M - 1] if v == 1 else list(range(M)) for v in _d]
    for _r, (_i, _j, _k) in enumerate((i, j, k) for i in _sel[0] for j in _sel[1] for k in _sel[2]):
        PK[OFFS[_d][0] + _r, B_POS[(_i * M + _j) * M + _k]] = 1.0

CORNERS = [(x, y, z) for x in (0, 1) for y in (0, 1) for z in (0, 1)]
PRIM = [(0, o) for o in CORNERS]
PRIM += [(1, (0, y, z)) for y in (0, 1) for z in (0, 1)]
PRIM += [(2, (x, 0, z)) for x in (0, 1) for z in (0, 1)]
PRIM += [(3, (x, y, 0)) for x in (0, 1) for y in (0, 1)]
S64 = one_hot([CORNERS.index(o) * 8 + t for t, o in PRIM], np.arange(20), (64, 24))
TILE = np.tile(np.eye(24, dtype=np.float32), (1, 8))
TMASK = (np.arange(64)[:, None] // 8 == np.arange(192)[None, :] // 24).astype(np.float32)
SPREAD = np.zeros((192, 128), np.float32)
for _c, _o1 in enumerate(CORNERS):
    for _q, (_t, _o2) in enumerate(PRIM):
        _f = [b - a + 1 for a, b in zip(_o1, _o2)]
        SPREAD[_c * 24 + _q, _t * 27 + (_f[0] * 3 + _f[1]) * 3 + _f[2]] = 1.0


def coarse_slots():
    m = np.arange(512)
    c, a, b, t = np.array(ORDER)[m // 64], m // 16 % 4, m // 4 % 4, m % 4
    da = (a[None, :] - a[:, None] + 1) % GX
    db = (b[None, :] - b[:, None] + 1) % GY
    dc = (c[None, :] - c[:, None] + 1) % GZ
    slot = t[None, :] * 27 + (da * 3 + db) * 3 + dc
    return np.where((da < 3) & (db < 3) & (dc < 3), slot, -1).astype(np.int32)


SLOTS = coarse_slots()


def dot(a, b, ca=1, cb=0):
    return lax.dot_general(
        a, b, (((ca,), (cb,)), ((), ())), precision=lax.Precision.HIGHEST, preferred_element_type=F32
    )


def pieces(x):
    h = x.astype(BF16)
    r = x - h.astype(F32)
    m = r.astype(BF16)
    return h, m, (r - m.astype(F32)).astype(BF16)


def pick(sel, x, ca=1, cb=0):
    out = None
    for p in pieces(x):
        d = lax.dot_general(sel, p, (((ca,), (cb,)), ((), ())), preferred_element_type=F32)
        out = d if out is None else out + d
    return out


def pick_cols(x, sel):
    out = None
    for p in pieces(x):
        d = lax.dot_general(p, sel, (((1,), (1,)), ((), ())), preferred_element_type=F32)
        out = d if out is None else out + d
    return out


def here():
    return lax.axis_index("gx"), lax.axis_index("gy"), lax.axis_index("gz")


def at(d):
    x, y, z = here()
    return (lax.rem(x + d[0] + GX, GX), lax.rem(y + d[1] + GY, GY), lax.rem(z + d[2] + GZ, GZ))


PLANE = [(x, y, 0) for x in range(GX) for y in range(GY) if (x, y) != (0, 0)]
LINE = [(0, 0, z) for z in range(1, GZ)]
_norm = lambda d: (d[0] % GX, d[1] % GY, d[2] % GZ)
PARTNERS = sorted({_norm(d) for d in DIRS + PLANE + LINE})


def barrier():
    sem = pltpu.get_barrier_semaphore()
    for d in PARTNERS:
        pl.semaphore_signal(sem, inc=1, device_id=at(d), device_id_type=MESH)
    pl.semaphore_wait(sem, len(PARTNERS))


def remote(src, dst, sems, k, d):
    return pltpu.make_async_remote_copy(
        src_ref=src, dst_ref=dst, send_sem=sems.at[2 * k], recv_sem=sems.at[2 * k + 1], device_id=at(d), device_id_type=MESH
    )


def exchange_start(send, recv, sems, k):
    for d in DIRS:
        o, n = OFFS[d]
        o2, _ = OFFS[tuple(-v for v in d)]
        remote(send.at[pl.ds(o, n)], recv.at[pl.ds(o2, n)], sems, k, d).start()


def bulk_wait(send, recv, sems, k):
    c = remote(send, recv, sems, k, (1, 0, 0))
    c.wait_recv()
    c.wait_send()


def owner_start(send, recv, sems, k):
    for c, o in enumerate(CORNERS):
        if c:
            remote(send.at[pl.ds(8 * c, 8)], recv.at[pl.ds(8 * c, 8)], sems, k, o).start()


def owner_finish(send, recv, sems, k):
    bulk_wait(send.at[pl.ds(8, 56)], recv.at[pl.ds(8, 56)], sems, k)
    out = send[pl.ds(0, 8), :]
    for c in range(1, 8):
        out = out + recv[pl.ds(8 * c, 8), :]
    return out


def gather_start(val, plane, sems, k):
    x, y, _ = here()
    ab = x * GY + y
    odd = lax.rem(y, 2) == 1
    plane[ab] = jnp.where(jnp.full((8, 128), odd), pltpu.roll(val, 4, 0), val)
    for d in PLANE:
        remote(plane.at[ab], plane.at[ab], sems, k, d).start()


def gather_turn(plane, full, sems, k):
    bulk_wait(plane.at[pl.ds(0, 15)], plane.at[pl.ds(0, 15)], sems, k)
    _, _, z = here()
    h = z // 2
    pos = lax.rem(z, 2) * h + (1 - lax.rem(z, 2)) * (6 - 2 * lax.rem(h, 2) + h // 2)
    rows = [plane[2 * i] + plane[2 * i + 1] for i in range(8)]
    mine = pl.ds(pl.multiple_of(pos * 64, 64), 64)
    full[mine, :] = jnp.concatenate(rows, axis=0)
    for d in LINE:
        remote(full.at[mine], full.at[mine], sems, k + 1, d).start()


def gather_finish(full, sems, k):
    bulk_wait(full.at[pl.ds(0, 448)], full.at[pl.ds(0, 448)], sems, k + 1)


def reduce_start(val, plane, sems, k):
    x, y, _ = here()
    ab = x * GY + y
    plane[ab] = val
    for d in PLANE:
        remote(plane.at[ab], plane.at[ab], sems, k, d).start()


def reduce_turn(plane, line, sems, k):
    bulk_wait(plane.at[pl.ds(0, 15)], plane.at[pl.ds(0, 15)], sems, k)
    _, _, z = here()
    line[z] = jnp.sum(plane[...], axis=0)
    for d in LINE:
        remote(line.at[z], line.at[z], sems, k + 1, d).start()


def reduce_finish(line, sems, k):
    bulk_wait(line.at[pl.ds(0, 7)], line.at[pl.ds(0, 7)], sems, k + 1)
    return jnp.sum(line[...], axis=0)


def prepare(load_ref, a_ref, di_ref, n_ref, phi_ref, pb_ref, pi_ref, s64_ref, tile_ref, tmask_ref, spread_ref,
            cl_ref, s_ref, nbb_ref, x_ref, p24_ref, start_ref, li_ref, k0_ref, k64_ref, flat):
    for i in range(M):
        for j in range(M):
            flat[pl.ds((i * M + j) * M, M), :] = load_ref[i, j]
    pb, pi = pb_ref[...], pi_ref[...]
    load = flat[...]
    lb, li = pick(pb, load), pick(pi, load)
    di = di_ref[...]
    start = dot(di, li)
    ab = pick(pb, a_ref[...])
    abb, abi = pick_cols(ab, pb), pick_cols(ab, pi)
    x = dot(di, abi, 1, 1)
    s = abb - dot(abi, x)
    cl_ref[:, 0:RHS] = lb - dot(abi, start)
    cl_ref[:, RHS : 2 * RHS] = lb
    s_ref[...] = s
    x_ref[...] = x
    start_ref[...] = start
    li_ref[...] = li
    k0_ref[...] = jnp.broadcast_to(jnp.sum(li * start, axis=0, keepdims=True), (8, RHS))
    nbb_ref[...] = pick_cols(pick(pb, n_ref[...]), pb)
    phi = pick_cols(phi_ref[...], pb)
    p24 = jnp.concatenate([phi, jnp.zeros((4, NB), F32)], axis=0)
    p24_ref[...] = p24
    k24 = dot(dot(p24, s), p24, 1, 1)
    k64 = dot(dot(s64_ref[...], k24), tile_ref[...]) * tmask_ref[...]
    k64_ref[...] = dot(k64, spread_ref[...])


def first(cl_ref, k64_ref, nbb_ref, p24_ref, pk_ref, wt_ref, s64_ref, asm_ref, w_ref, kall_ref, gall_ref,
          send, recv, ksend, krecv, hsend, hrecv, kplane, hplane, sems):
    barrier()
    ksend[...] = k64_ref[...]
    owner_start(ksend, krecv, sems, 0)
    pk = pk_ref[...]
    cl = cl_ref[...]
    send[...] = pick(pk, cl)
    exchange_start(send, recv, sems, 1)
    gather_start(owner_finish(ksend, krecv, sems, 0), kplane, sems, 2)
    bulk_wait(send, recv, sems, 1)
    asm = cl + pick(pk, recv[...], 0, 0)
    asm_ref[...] = asm
    f = wt_ref[...] * asm[:, 0:RHS]
    hsend[...] = dot(s64_ref[...], dot(p24_ref[...], f))
    owner_start(hsend, hrecv, sems, 4)
    gather_turn(kplane, kall_ref, sems, 2)
    w_ref[...] = dot(nbb_ref[...], f)
    gather_start(owner_finish(hsend, hrecv, sems, 4), hplane, sems, 5)
    gather_finish(kall_ref, sems, 2)
    gather_turn(hplane, gall_ref, sems, 5)
    gather_finish(gall_ref, sems, 5)


def sweep(ref, n, steps):
    lane = lax.broadcasted_iota(jnp.int32, (n, 128), 1)
    sub = lax.broadcasted_iota(jnp.int32, (n, 128), 0)
    base = lane // n * n

    def body(k, carry):
        idx = base + k
        for j in range(ref.shape[0]):
            x = ref[j]
            row = ref[j, pl.ds(k, 1), :]
            col = jnp.take_along_axis(x, idx, axis=1, mode="promise_in_bounds")
            piv = jnp.take_along_axis(jnp.broadcast_to(row, (8, 128)), idx[0:8], axis=1, mode="promise_in_bounds")[0:1]
            inv = 1.0 / piv
            scaled = row * inv
            oncol = lane == idx
            new = jnp.where(oncol, -col * inv, x - col * scaled)
            ref[j] = jnp.where(sub == k, jnp.where(oncol, inv, scaled), new)
        return carry

    lax.fori_loop(0, steps, body, 0)


def coarse(kall_ref, slots_ref, w24_ref, kc, xo, x2, xf):
    kall = kall_ref[...]
    for j in range(4):
        cut = pl.ds(128 * j, 128)
        idx = slots_ref[:, cut]
        v = jnp.take_along_axis(kall, jnp.maximum(idx, 0), axis=1, mode="promise_in_bounds")
        kc[:, cut] = jnp.where(idx >= 0, v, 0.0)
    low = lax.broadcasted_iota(jnp.int32, (64, 128), 1) < 64
    for j in range(2):
        cut = pl.ds(128 * j, 128)
        xo[j] = jnp.where(low, kc[pl.ds(128 * j, 64), cut], kc[pl.ds(128 * j + 64, 64), cut])
    sweep(xo, 64, 64)
    group = lax.broadcasted_iota(jnp.int32, (64, 256), 1) // 64
    both = jnp.concatenate([xo[0], xo[1]], axis=1)
    inv_o = jnp.concatenate([jnp.where(group == g, both, 0.0) for g in range(4)], axis=0)
    koe = kc[pl.ds(0, 256), pl.ds(256, 256)]
    m = dot(inv_o, koe)
    se = kc[pl.ds(256, 256), pl.ds(256, 256)] - dot(koe, m, 0, 0)
    x2[0] = jnp.where(low, se[0:64, 0:128], se[64:128, 0:128])
    sweep(x2, 64, 64)
    inv_2 = jnp.concatenate([jnp.where(low, x2[0], 0.0), jnp.where(low, 0.0, x2[0])], axis=0)
    k2f = se[0:128, 128:256]
    m2 = dot(inv_2, k2f)
    xf[0] = se[128:256, 128:256] - dot(k2f, m2, 0, 0)
    sweep(xf, 128, 128)
    x, y, z = here()
    p = lax.broadcasted_iota(jnp.int32, (24, 512), 0)
    col = lax.broadcasted_iota(jnp.int32, (24, 512), 1)
    want = jnp.full((24, 512), -1, jnp.int32)
    for q, (t, o) in enumerate(PRIM):
        cx, cy, cz = at(o)
        h = cz // 2
        pos = lax.rem(cz, 2) * h + (1 - lax.rem(cz, 2)) * (6 - 2 * lax.rem(h, 2) + h // 2)
        want = jnp.where(p == q, pos * 64 + (cx * GY + cy) * 4 + t, want)
    sel = (want == col).astype(F32)
    so = sel[:, 0:256]
    s_e = sel[:, 256:512] - dot(so, m)
    s_2 = s_e[:, 0:128]
    wf = dot(s_e[:, 128:256] - dot(s_2, m2), xf[0])
    w2 = dot(s_2, inv_2) - dot(wf, m2, 1, 1)
    we = jnp.concatenate([w2, wf], axis=1)
    w24_ref[:, 256:512] = we
    w24_ref[:, 0:256] = dot(so, inv_o) - dot(we, m, 1, 1)


def second(cl_ref, asm_ref, w_ref, gall_ref, w24_ref, s_ref, nbb_ref, p24_ref, k0_ref, pk_ref, wt_ref, s64_ref,
           z1_ref, z2_ref, at1_ref, at2_ref, sums_ref,
           send, recv, hsend, hrecv, hplane, gfull, rplane, rline, sems):
    barrier()
    pk, wt, p24 = pk_ref[...], wt_ref[...], p24_ref[...]
    c = cl_ref[:, 0:RHS]
    s = s_ref[...]

    def swap_start(k, v):
        send[k] = pick(pk, v)
        exchange_start(send.at[k], recv.at[k], sems, k)

    def swap_finish(k, v):
        bulk_wait(send.at[k], recv.at[k], sems, k)
        return v + pick(pk, recv[k], 0, 0)

    def apply_coarse(w, g):
        y = dot(w24_ref[...], g)
        return wt * (w + dot(p24, y, 0, 0))

    u = apply_coarse(w_ref[...], gall_ref[...])
    swap_start(0, u)
    z1 = swap_finish(0, u)
    t1 = dot(s, z1)
    swap_start(1, t1)
    z1_ref[...] = z1
    k0 = k0_ref[...]
    part = lambda a, b: jnp.sum(a * b, axis=0, keepdims=True)
    zero = jnp.zeros((5, RHS), F32)
    reduce_start(jnp.concatenate([k0[0:1], part(c, z1), part(z1, t1), zero], axis=0), rplane.at[0], sems, 4)
    at1 = swap_finish(1, t1)
    at1_ref[...] = at1
    f = wt * at1
    hsend[...] = dot(s64_ref[...], dot(p24, f))
    owner_start(hsend, hrecv, sems, 6)
    w = dot(nbb_ref[...], f)
    reduce_turn(rplane.at[0], rline.at[0], sems, 4)
    gather_start(owner_finish(hsend, hrecv, sems, 6), hplane, sems, 7)
    gather_turn(hplane, gfull, sems, 7)
    sums = reduce_finish(rline.at[0], sems, 4)
    k0s = sums[0:1]
    g0 = k0s + sums[1:2]
    s1 = g0 / (k0s + sums[2:3])
    gather_finish(gfull, sems, 7)
    u = apply_coarse(w, gfull[...])
    swap_start(2, u)
    z2 = swap_finish(2, u)
    t2 = dot(s, z2)
    swap_start(3, t2)
    z2_ref[...] = z2
    zp, tp, cp = z1 - s1 * z2, t1 - s1 * t2, c - s1 * t1
    zero = jnp.zeros((6, RHS), F32)
    reduce_start(jnp.concatenate([part(cp, zp), part(zp, tp), zero], axis=0), rplane.at[1], sems, 9)
    at2_ref[...] = swap_finish(3, t2)
    reduce_turn(rplane.at[1], rline.at[1], sems, 9)
    last = reduce_finish(rline.at[1], sems, 9)
    rest = 1.0 - s1
    g1 = rest * rest * k0s + last[0:1]
    beta = g1 / g0
    s2 = g1 / (rest * rest * k0s + last[1:2] - beta * g1 / s1)
    sums_ref[...] = jnp.concatenate([s1, beta, s2, jnp.zeros((5, RHS), F32)], axis=0)


def finish(sums_ref, z1_ref, z2_ref, at1_ref, at2_ref, asm_ref, x_ref, start_ref, li_ref, pb_ref, pi_ref, sol_ref, res_ref, flat):
    s1, beta, s2 = sums_ref[0:1, :], sums_ref[1:2, :], sums_ref[2:3, :]
    rest = 1.0 - s1
    z1, at1 = z1_ref[...], at1_ref[...]
    xb = s1 * z1 + s2 * ((z1 - s1 * z2_ref[...]) + beta * z1)
    xi = (s1 + s2 * (rest + beta)) * start_ref[...] - dot(x_ref[...], xb)
    kappa = rest * (1.0 - s2) - s2 * beta
    ac = asm_ref[:, 0:RHS]
    ae = asm_ref[:, RHS : 2 * RHS] - ac
    rb = kappa * ae + (ac - s1 * at1) - s2 * ((at1 - s1 * at2_ref[...]) + beta * at1)
    ri = kappa * li_ref[...]
    pb, pi = pb_ref[...], pi_ref[...]
    both = pick(pb, jnp.concatenate([xb, rb], axis=1), 0, 0) + pick(pi, jnp.concatenate([xi, ri], axis=1), 0, 0)
    flat[...] = both
    for i in range(M):
        for j in range(M):
            rows = pl.ds((i * M + j) * M, M)
            sol_ref[i, j] = flat[rows, 0:RHS]
            res_ref[i, j] = flat[rows, RHS : 2 * RHS]


def call(kernel, out_shapes, scratch=(), collective=None):
    params = dict(vmem_limit_bytes=60 * 2**20)
    if collective is not None:
        params |= dict(collective_id=collective, has_side_effects=True)
    outs = [jax.ShapeDtypeStruct(s, F32) for s in out_shapes]

    def run(*args):
        return pl.pallas_call(
            kernel, out_shape=outs, in_specs=[VM] * len(args), out_specs=[VM] * len(outs),
            scratch_shapes=list(scratch), compiler_params=pltpu.CompilerParams(**params), name=kernel.__name__,
        )(*args)

    return run


def local(load, a, di, n, phi):
    a, n = a.reshape(NODES, NODES), n.reshape(NODES, NODES)
    di, phi = di.reshape(NI, NI), phi.reshape(20, NODES)
    pb, pi, pk = (jnp.asarray(v, BF16) for v in (PB, PI, PK))
    wt, s64 = jnp.asarray(WEIGHT), jnp.asarray(S64)
    V = lambda *s: pltpu.VMEM(s, F32)
    cl, s, nbb, x, p24, start, li, k0, k64 = call(
        prepare,
        [(NB, 2 * RHS), (NB, NB), (NB, NB), (NI, NB), (24, NB), (NI, RHS), (NI, RHS), (8, RHS), (64, 128)],
        [V(NODES, RHS)],
    )(load, a, di, n, phi, pb, pi, s64, jnp.asarray(TILE), jnp.asarray(TMASK), jnp.asarray(SPREAD))
    asm, w, kall, gall = call(
        first,
        [(NB, 2 * RHS), (NB, RHS), (512, 128), (512, 128)],
        [V(NS, 2 * RHS), V(NS, 2 * RHS), V(64, 128), V(64, 128), V(64, 128), V(64, 128), V(16, 8, 128), V(16, 8, 128),
         pltpu.SemaphoreType.DMA((14,))],
        0,
    )(cl, k64, nbb, p24, pk, wt, s64)
    (w24,) = call(coarse, [(24, 512)], [V(512, 512), V(2, 64, 128), V(1, 64, 128), V(1, 128, 128)])(kall, jnp.asarray(SLOTS))
    z1, z2, at1, at2, sums = call(
        second,
        [(NB, RHS)] * 4 + [(8, RHS)],
        [V(4, NS, RHS), V(4, NS, RHS), V(64, 128), V(64, 128), V(16, 8, 128), V(512, 128), V(2, 16, 8, 128), V(2, 8, 8, 128),
         pltpu.SemaphoreType.DMA((22,))],
        1,
    )(cl, asm, w, gall, w24, s, nbb, p24, k0, pk, wt, s64)
    return tuple(
        call(finish, [(M, M, M, RHS)] * 2, [V(NODES, 2 * RHS)])(sums, z1, z2, at1, at2, asm, x, start, li, pb, pi)
    )


def solution(mesh):
    spec4, spec5 = P("gx", "gy", "gz", None), P("gx", "gy", "gz", None, None)
    return jax.shard_map(
        local, mesh=mesh, in_specs=(spec4, spec5, spec5, spec5, spec5), out_specs=(spec4, spec4), check_vma=False
    )
```

```python
import functools

import jax
import jax.numpy as jnp
import numpy as np
from jax import lax
from jax.experimental import pallas as pl
from jax.experimental.pallas import tpu as pltpu
from jax.sharding import PartitionSpec as P

MESH = pl.DeviceIdType.MESH
F32, BF16 = jnp.float32, jnp.bfloat16
GX, GY, GZ = 4, 4, 8
M = 9
NODES, NB, NI, RHS = 729, 392, 343, 128
ORDER = (1, 3, 5, 7, 2, 6, 0, 4)
VM = pl.BlockSpec(memory_space=pltpu.VMEM)

_g = np.indices((M, M, M)).reshape(3, -1)
_rim = ((_g == 0) | (_g == M - 1)).sum(0)
B_IDS, I_IDS = np.where(_rim > 0)[0], np.where(_rim == 0)[0]
B_POS = {int(n): r for r, n in enumerate(B_IDS)}


def one_hot(rows, cols, shape):
    out = np.zeros(shape, np.float32)
    out[rows, cols] = 1.0
    return out


B_COL = np.full((NB, 1), -1, np.int32)
B_COL[: len(B_IDS), 0] = B_IDS
I_COL = I_IDS.astype(np.int32)[:, None]
RUNS, _r = [], 0
while _r < len(B_IDS):
    _e = _r + 1
    while _e < len(B_IDS) and B_IDS[_e] == B_IDS[_e - 1] + 1:
        _e += 1
    RUNS.append((_r, int(B_IDS[_r]), _e - _r))
    _r = _e
WEIGHT = np.zeros((NB, 1), np.float32)
WEIGHT[: len(B_IDS), 0] = 1.0 / 2.0 ** _rim[B_IDS]
WEIGHT = np.broadcast_to(WEIGHT, (NB, RHS)).copy()

DIRS = sorted(
    ((x, y, z) for x in (-1, 0, 1) for y in (-1, 0, 1) for z in (-1, 0, 1) if (x, y, z) != (0, 0, 0)),
    key=lambda d: (sum(map(abs, d)), d),
)
SIZE = {1: 88, 2: 16, 3: 8}
OFFS, _at = {}, 0
for _d in DIRS:
    OFFS[_d] = (_at, SIZE[sum(map(abs, _d))])
    _at += OFFS[_d][1]
NS = _at
K_COL = np.full((NS, 1), -1, np.int32)
for _d in DIRS:
    _sel = [[0] if v == -1 else [M - 1] if v == 1 else list(range(M)) for v in _d]
    for _r, (_i, _j, _k) in enumerate((i, j, k) for i in _sel[0] for j in _sel[1] for k in _sel[2]):
        K_COL[OFFS[_d][0] + _r, 0] = B_POS[(_i * M + _j) * M + _k]

CORNERS = [(x, y, z) for x in (0, 1) for y in (0, 1) for z in (0, 1)]
PRIM = [(0, o) for o in CORNERS]
PRIM += [(1, (0, y, z)) for y in (0, 1) for z in (0, 1)]
PRIM += [(2, (x, 0, z)) for x in (0, 1) for z in (0, 1)]
PRIM += [(3, (x, y, 0)) for x in (0, 1) for y in (0, 1)]
S64 = one_hot([CORNERS.index(o) * 8 + t for t, o in PRIM], np.arange(20), (64, 24))
TILE = np.tile(np.eye(24, dtype=np.float32), (1, 8))
TMASK = (np.arange(64)[:, None] // 8 == np.arange(192)[None, :] // 24).astype(np.float32)
SPREAD = np.zeros((192, 128), np.float32)
for _c, _o1 in enumerate(CORNERS):
    for _q, (_t, _o2) in enumerate(PRIM):
        _f = [b - a + 1 for a, b in zip(_o1, _o2)]
        SPREAD[_c * 24 + _q, _t * 27 + (_f[0] * 3 + _f[1]) * 3 + _f[2]] = 1.0


def dot(a, b, ca=1, cb=0):
    return lax.dot_general(
        a, b, (((ca,), (cb,)), ((), ())), precision=lax.Precision.HIGHEST, preferred_element_type=F32
    )


def pieces(x):
    h = x.astype(BF16)
    r = x - h.astype(F32)
    m = r.astype(BF16)
    return h, m, (r - m.astype(F32)).astype(BF16)


def pick(sel, x, ca=1, cb=0):
    out = None
    for p in pieces(x):
        d = lax.dot_general(sel, p, (((ca,), (cb,)), ((), ())), preferred_element_type=F32)
        out = d if out is None else out + d
    return out


def pick_cols(x, sel):
    out = None
    for p in pieces(x):
        d = lax.dot_general(p, sel, (((1,), (1,)), ((), ())), preferred_element_type=F32)
        out = d if out is None else out + d
    return out


def here():
    return lax.axis_index("gx"), lax.axis_index("gy"), lax.axis_index("gz")


def at(d):
    x, y, z = here()
    return (lax.rem(x + d[0] + GX, GX), lax.rem(y + d[1] + GY, GY), lax.rem(z + d[2] + GZ, GZ))


PLANE = [(x, y, 0) for x in range(GX) for y in range(GY) if (x, y) != (0, 0)]
LINE = [(0, 0, z) for z in range(1, GZ)]
_norm = lambda d: (d[0] % GX, d[1] % GY, d[2] % GZ)
PARTNERS = sorted({_norm(d) for d in DIRS + PLANE + LINE})


def remote(src, dst, sems, k, d):
    return pltpu.make_async_remote_copy(
        src_ref=src, dst_ref=dst, send_sem=sems.at[2 * k], recv_sem=sems.at[2 * k + 1], device_id=at(d), device_id_type=MESH
    )


def exchange_start(send, recv, sems, k):
    for d in DIRS:
        o, n = OFFS[d]
        o2, _ = OFFS[tuple(-v for v in d)]
        remote(send.at[pl.ds(o, n)], recv.at[pl.ds(o2, n)], sems, k, d).start()


def bulk_wait(send, recv, sems, k):
    c = remote(send, recv, sems, k, (1, 0, 0))
    c.wait_recv()
    c.wait_send()


def owner_start(send, recv, sems, k):
    for c, o in enumerate(CORNERS):
        if c:
            remote(send.at[pl.ds(8 * c, 8)], recv.at[pl.ds(8 * c, 8)], sems, k, o).start()


def owner_finish(send, recv, sems, k):
    bulk_wait(send.at[pl.ds(8, 56)], recv.at[pl.ds(8, 56)], sems, k)
    out = send[pl.ds(0, 8), :]
    for c in range(1, 8):
        out = out + recv[pl.ds(8 * c, 8), :]
    return out


def gather_start(val, plane, sems, k):
    x, y, _ = here()
    ab = x * GY + y
    odd = lax.rem(y, 2) == 1
    plane[ab] = jnp.where(jnp.full((8, 128), odd), pltpu.roll(val, 4, 0), val)
    for d in PLANE:
        remote(plane.at[ab], plane.at[ab], sems, k, d).start()


def gather_turn(plane, full, sems, k):
    bulk_wait(plane.at[pl.ds(0, 15)], plane.at[pl.ds(0, 15)], sems, k)
    _, _, z = here()
    pos = place(z)
    rows = [plane[2 * i] + plane[2 * i + 1] for i in range(8)]
    mine = pl.ds(pl.multiple_of(pos * 64, 64), 64)
    full[mine, :] = jnp.concatenate(rows, axis=0)
    for d in LINE:
        remote(full.at[mine], full.at[mine], sems, k + 1, d).start()


def gather_finish(full, sems, k):
    bulk_wait(full.at[pl.ds(0, 448)], full.at[pl.ds(0, 448)], sems, k + 1)


def reduce_start(val, plane, sems, k):
    x, y, _ = here()
    ab = x * GY + y
    plane[ab] = val
    for d in PLANE:
        remote(plane.at[ab], plane.at[ab], sems, k, d).start()


def reduce_turn(plane, line, sems, k):
    bulk_wait(plane.at[pl.ds(0, 15)], plane.at[pl.ds(0, 15)], sems, k)
    _, _, z = here()
    line[z] = jnp.sum(plane[...], axis=0)
    for d in LINE:
        remote(line.at[z], line.at[z], sems, k + 1, d).start()


def reduce_finish(line, sems, k):
    bulk_wait(line.at[pl.ds(0, 7)], line.at[pl.ds(0, 7)], sems, k + 1)
    return jnp.sum(line[...], axis=0)


def choose(ids_ref, n):
    ids = ids_ref[...]
    return (lax.broadcasted_iota(jnp.int32, (ids.shape[0], n), 1) == ids).astype(F32).astype(BF16)


def place(z):
    h = z // 2
    return lax.rem(z, 2) * h + (1 - lax.rem(z, 2)) * (6 - 2 * lax.rem(h, 2) + h // 2)


def coords(m):
    pos = m >> 6
    c = jnp.where(pos < 4, 2 * pos + 1, jnp.where(pos < 6, 4 * pos - 14, 4 * pos - 24))
    return (m >> 4) & 3, (m >> 2) & 3, c, m & 3


def build_coarse(kall_ref, kc):
    kall = kall_ref[...]
    ra, rb, rc, _ = coords(lax.broadcasted_iota(jnp.int32, (512, 128), 0))
    for j in range(4):
        ca, cb, cc, ct = coords(lax.broadcasted_iota(jnp.int32, (1, 128), 1) + 128 * j)
        da, db, dc = (ca + 1 - ra) & 3, (cb + 1 - rb) & 3, (cc + 1 - rc) & 7
        hit = (da < 3) & (db < 3) & (dc < 3)
        slot = jnp.where(hit, ct * 27 + da * 9 + db * 3 + dc, 0)
        v = jnp.take_along_axis(kall, slot, axis=1, mode="promise_in_bounds")
        kc[:, pl.ds(128 * j, 128)] = jnp.where(hit, v, 0.0)


def sweep(ref, n):
    lane = lax.broadcasted_iota(jnp.int32, (n, 128), 1)
    base = lane // n * n
    take = lambda v, idx: jnp.take_along_axis(v, idx, axis=1, mode="promise_in_bounds")

    def body(i, carry):
        k = 2 * i
        i0, i1 = base + k, base + k + 1
        s0, s1 = i0[0:8], i1[0:8]
        for j in range(ref.shape[0]):
            x = ref[j]
            r0 = jnp.broadcast_to(ref[j, pl.ds(k, 1), :], (8, 128))
            r1 = jnp.broadcast_to(ref[j, pl.ds(k + 1, 1), :], (8, 128))
            c0, c1 = take(x, i0), take(x, i1)
            p, q, r = take(r0, s0), take(r0, s1), take(r1, s1)
            d = 1.0 / (p * r - q * q)
            b00, b01, b11 = r * d, -q * d, p * d
            on0, on1 = lane[0:8] == s0, lane[0:8] == s1
            n0 = jnp.where(on0, b00, jnp.where(on1, b01, b00 * r0 + b01 * r1))
            n1 = jnp.where(on0, b01, jnp.where(on1, b11, b01 * r0 + b11 * r1))
            left = jnp.where((lane == i0) | (lane == i1), 0.0, x)
            ref[j] = left - c0 * n0[0:1] - c1 * n1[0:1]
            ref[j, pl.ds(k, 1), :] = n0[0:1]
            ref[j, pl.ds(k + 1, 1), :] = n1[0:1]
        return carry

    lax.fori_loop(0, n // 2, body, 0)


def program(load_h, a_h, di_h, n_h, phi_h, bcol, icol, kcol, wt_ref, s64_ref, tile_ref, tmask_ref, spread_ref,
            sol_ref, res_ref,
            load_v, arows, nrows, di_v, phi_v, flat, out, send, recv, ssend, srecv,
            ksend, krecv, hsend, hrecv, kplane, gplane, kfull, gfull, rplane, rline, kc, xo, x2, xf, sems, dsems):
    sem = pltpu.get_barrier_semaphore()
    for d in PARTNERS:
        pl.semaphore_signal(sem, inc=1, device_id=at(d), device_id_type=MESH)

    def rows_copies(src, dst, q):
        return [pltpu.make_async_copy(src.at[pl.ds(n, c)], dst.at[pl.ds(r, c)], dsems.at[q]) for r, n, c in RUNS]

    get_phi = pltpu.make_async_copy(phi_h.at[:, 0, :], phi_v, dsems.at[0])
    get_load = pltpu.make_async_copy(load_h, load_v, dsems.at[1])
    get_di = pltpu.make_async_copy(di_h.at[:, 0, :], di_v, dsems.at[2])
    get_phi.start()
    for c in rows_copies(a_h, arows, 3):
        c.start()
    get_load.start()
    get_di.start()
    for c in rows_copies(n_h, nrows, 4):
        c.start()
    used = pl.ds(0, len(B_IDS))
    get_a = pltpu.make_async_copy(a_h.at[used], arows.at[used], dsems.at[3])
    get_n = pltpu.make_async_copy(n_h.at[used], nrows.at[used], dsems.at[4])
    spare = pl.ds(len(B_IDS), NB - len(B_IDS))
    arows[spare] = jnp.zeros((NB - len(B_IDS), 1, NODES), F32)
    nrows[spare] = jnp.zeros((NB - len(B_IDS), 1, NODES), F32)
    pb, pi, pk = choose(bcol, NODES), choose(icol, NODES), choose(kcol, NB)
    wt = wt_ref[...]

    get_phi.wait()
    phi = jnp.concatenate([phi_v[...], jnp.zeros((4, NODES), F32)], axis=0)
    p24 = pick_cols(phi, pb)
    get_a.wait()
    ab = arows[:, 0, :]
    k24 = dot(p24, dot(ab, phi, 1, 1))
    k64 = dot(dot(s64_ref[...], k24), tile_ref[...]) * tmask_ref[...]
    ksend[...] = dot(k64, spread_ref[...])
    pl.semaphore_wait(sem, len(PARTNERS))
    owner_start(ksend, krecv, sems, 0)

    get_load.wait()
    for i in range(M):
        for j in range(M):
            flat[pl.ds((i * M + j) * M, M), :] = load_v[i, j]
    load = flat[...]
    lb, li = pick(pb, load), pick(pi, load)
    get_di.wait()
    di = di_v[...]
    start = dot(di, li)
    abi = pick_cols(ab, pi)
    c = lb - dot(abi, start)
    cl = jnp.concatenate([c, lb], axis=1)
    send[...] = pick(pk, cl)
    exchange_start(send, recv, sems, 1)
    gather_start(owner_finish(ksend, krecv, sems, 0), kplane, sems, 2)
    k0 = jnp.sum(li * start, axis=0, keepdims=True)
    x = dot(di, abi, 1, 1)
    bulk_wait(send, recv, sems, 1)
    asm = cl + pick(pk, recv[...], 0, 0)
    f = wt * asm[:, 0:RHS]
    hsend[0] = dot(s64_ref[...], dot(p24, f))
    owner_start(hsend.at[0], hrecv.at[0], sems, 4)
    gather_turn(kplane, kfull, sems, 2)
    s = pick_cols(ab, pb) - dot(abi, x)
    get_n.wait()
    nbb = pick_cols(nrows[:, 0, :], pb)
    w = dot(nbb, f)
    gather_start(owner_finish(hsend.at[0], hrecv.at[0], sems, 4), gplane.at[0], sems, 5)
    gather_finish(kfull, sems, 2)

    build_coarse(kfull, kc)
    low = lax.broadcasted_iota(jnp.int32, (64, 128), 1) < 64
    for j in range(2):
        cut = pl.ds(128 * j, 128)
        xo[j] = jnp.where(low, kc[pl.ds(128 * j, 64), cut], kc[pl.ds(128 * j + 64, 64), cut])
    sweep(xo, 64)
    gather_turn(gplane.at[0], gfull.at[0], sems, 5)
    group = lax.broadcasted_iota(jnp.int32, (64, 256), 1) // 64
    both = jnp.concatenate([xo[0], xo[1]], axis=1)
    inv_o = jnp.concatenate([jnp.where(group == g, both, 0.0) for g in range(4)], axis=0)
    koe = kc[pl.ds(0, 256), pl.ds(256, 256)]
    m = dot(inv_o, koe)
    se = kc[pl.ds(256, 256), pl.ds(256, 256)] - dot(koe, m, 0, 0)
    x2[0] = jnp.where(low, se[0:64, 0:128], se[64:128, 0:128])
    sweep(x2, 64)
    inv_2 = jnp.concatenate([jnp.where(low, x2[0], 0.0), jnp.where(low, 0.0, x2[0])], axis=0)
    k2f = se[0:128, 128:256]
    m2 = dot(inv_2, k2f)
    xf[0] = se[128:256, 128:256] - dot(k2f, m2, 0, 0)
    sweep(xf, 128)
    prim = lax.broadcasted_iota(jnp.int32, (24, 512), 0)
    want = jnp.full((24, 512), -1, jnp.int32)
    for q, (t, o) in enumerate(PRIM):
        cx, cy, cz = at(o)
        want = jnp.where(prim == q, place(cz) * 64 + (cx * GY + cy) * 4 + t, want)
    sel = (want == lax.broadcasted_iota(jnp.int32, (24, 512), 1)).astype(F32)
    so = sel[:, 0:256]
    s_e = sel[:, 256:512] - dot(so, m)
    s_2 = s_e[:, 0:128]
    wf = dot(s_e[:, 128:256] - dot(s_2, m2), xf[0])
    w2 = dot(s_2, inv_2) - dot(wf, m2, 1, 1)
    we = jnp.concatenate([w2, wf], axis=1)
    w24 = jnp.concatenate([dot(so, inv_o) - dot(we, m, 1, 1), we], axis=1)

    def swap_start(k, v):
        ssend[k] = pick(pk, v)
        exchange_start(ssend.at[k], srecv.at[k], sems, 7 + k)

    def swap_finish(k, v):
        bulk_wait(ssend.at[k], srecv.at[k], sems, 7 + k)
        return v + pick(pk, srecv[k], 0, 0)

    def apply_coarse(w, g):
        return wt * (w + dot(p24, dot(w24, g), 0, 0))

    part = lambda a, b: jnp.sum(a * b, axis=0, keepdims=True)
    gather_finish(gfull.at[0], sems, 5)
    u = apply_coarse(w, gfull[0])
    swap_start(0, u)
    z1 = swap_finish(0, u)
    t1 = dot(s, z1)
    swap_start(1, t1)
    reduce_start(jnp.concatenate([k0, part(c, z1), part(z1, t1), jnp.zeros((5, RHS), F32)], axis=0), rplane.at[0], sems, 11)
    at1 = swap_finish(1, t1)
    f = wt * at1
    hsend[1] = dot(s64_ref[...], dot(p24, f))
    owner_start(hsend.at[1], hrecv.at[1], sems, 13)
    w = dot(nbb, f)
    reduce_turn(rplane.at[0], rline.at[0], sems, 11)
    gather_start(owner_finish(hsend.at[1], hrecv.at[1], sems, 13), gplane.at[1], sems, 14)
    gather_turn(gplane.at[1], gfull.at[1], sems, 14)
    sums = reduce_finish(rline.at[0], sems, 11)
    k0s = sums[0:1]
    g0 = k0s + sums[1:2]
    s1 = g0 / (k0s + sums[2:3])
    gather_finish(gfull.at[1], sems, 14)
    u = apply_coarse(w, gfull[1])
    swap_start(2, u)
    z2 = swap_finish(2, u)
    t2 = dot(s, z2)
    swap_start(3, t2)
    zp, tp, cp = z1 - s1 * z2, t1 - s1 * t2, c - s1 * t1
    reduce_start(jnp.concatenate([part(cp, zp), part(zp, tp), jnp.zeros((6, RHS), F32)], axis=0), rplane.at[1], sems, 16)
    at2 = swap_finish(3, t2)
    reduce_turn(rplane.at[1], rline.at[1], sems, 16)
    last = reduce_finish(rline.at[1], sems, 16)
    rest = 1.0 - s1
    g1 = rest * rest * k0s + last[0:1]
    beta = g1 / g0
    s2 = g1 / (rest * rest * k0s + last[1:2] - beta * g1 / s1)

    xb = s1 * z1 + s2 * (zp + beta * z1)
    xi = (s1 + s2 * (rest + beta)) * start - dot(x, xb)
    kappa = rest * (1.0 - s2) - s2 * beta
    ac = asm[:, 0:RHS]
    ae = asm[:, RHS : 2 * RHS] - ac
    rb = kappa * ae + (ac - s1 * at1) - s2 * ((at1 - s1 * at2) + beta * at1)
    ri = kappa * li
    out[...] = pick(pb, jnp.concatenate([xb, rb], axis=1), 0, 0) + pick(pi, jnp.concatenate([xi, ri], axis=1), 0, 0)
    for i in range(M):
        for j in range(M):
            rows = pl.ds((i * M + j) * M, M)
            sol_ref[i, j] = out[rows, 0:RHS]
            res_ref[i, j] = out[rows, RHS : 2 * RHS]


def local(load, a, di, n, phi):
    tables = [jnp.asarray(v) for v in (B_COL, I_COL, K_COL, WEIGHT, S64, TILE, TMASK, SPREAD)]
    V = lambda *s: pltpu.VMEM(s, F32)
    shape = jax.ShapeDtypeStruct((M, M, M, RHS), F32)
    return tuple(pl.pallas_call(
        program,
        out_shape=[shape, shape],
        in_specs=[pl.BlockSpec(memory_space=pl.ANY)] * 5 + [VM] * len(tables),
        out_specs=[VM, VM],
        scratch_shapes=[
            V(M, M, M, RHS), V(NB, 1, NODES), V(NB, 1, NODES), V(NI, NI), V(20, NODES), V(NODES, RHS), V(NODES, 2 * RHS),
            V(NS, 2 * RHS), V(NS, 2 * RHS), V(4, NS, RHS), V(4, NS, RHS),
            V(64, 128), V(64, 128), V(2, 64, 128), V(2, 64, 128), V(16, 8, 128), V(2, 16, 8, 128), V(512, 128), V(2, 512, 128),
            V(2, 16, 8, 128), V(2, 8, 8, 128), V(512, 512), V(2, 64, 128), V(1, 64, 128), V(1, 128, 128),
            pltpu.SemaphoreType.DMA((36,)), pltpu.SemaphoreType.DMA((5,)),
        ],
        compiler_params=pltpu.CompilerParams(vmem_limit_bytes=60 * 2**20, collective_id=0, has_side_effects=True),
        name="program",
    )(load, a.reshape(NODES, 1, NODES), di.reshape(NI, 1, NI), n.reshape(NODES, 1, NODES), phi.reshape(20, 1, NODES), *tables))


def solution(mesh):
    spec4, spec5 = P("gx", "gy", "gz", None), P("gx", "gy", "gz", None, None)
    return jax.shard_map(
        local, mesh=mesh, in_specs=(spec4, spec5, spec5, spec5, spec5), out_specs=(spec4, spec4), check_vma=False
    )
```

```python
import functools

import jax
import jax.numpy as jnp
import numpy as np
from jax import lax
from jax.experimental import pallas as pl
from jax.experimental.pallas import tpu as pltpu
from jax.sharding import PartitionSpec as P

MESH = pl.DeviceIdType.MESH
F32, BF16 = jnp.float32, jnp.bfloat16
GX, GY, GZ = 4, 4, 8
M = 9
NODES, NB, NI, RHS = 729, 392, 343, 128
ORDER = (1, 3, 5, 7, 2, 6, 0, 4)
VM = pl.BlockSpec(memory_space=pltpu.VMEM)

_g = np.indices((M, M, M)).reshape(3, -1)
_rim = ((_g == 0) | (_g == M - 1)).sum(0)
B_IDS, I_IDS = np.where(_rim > 0)[0], np.where(_rim == 0)[0]
B_POS = {int(n): r for r, n in enumerate(B_IDS)}
I_POS = {int(n): r for r, n in enumerate(I_IDS)}


def one_hot(rows, cols, shape):
    out = np.zeros(shape, np.float32)
    out[rows, cols] = 1.0
    return out


B_COL = np.full((NB, 1), -1, np.int32)
B_COL[: len(B_IDS), 0] = B_IDS
I_COL = I_IDS.astype(np.int32)[:, None]
RUNS, _r = [], 0
while _r < len(B_IDS):
    _e = _r + 1
    while _e < len(B_IDS) and B_IDS[_e] == B_IDS[_e - 1] + 1:
        _e += 1
    RUNS.append((_r, int(B_IDS[_r]), _e - _r))
    _r = _e
WEIGHT = np.zeros((NB, 1), np.float32)
WEIGHT[: len(B_IDS), 0] = 1.0 / 2.0 ** _rim[B_IDS]
WEIGHT = np.broadcast_to(WEIGHT, (NB, RHS)).copy()

DIRS = sorted(
    ((x, y, z) for x in (-1, 0, 1) for y in (-1, 0, 1) for z in (-1, 0, 1) if (x, y, z) != (0, 0, 0)),
    key=lambda d: (sum(map(abs, d)), d),
)
SIZE = {1: 88, 2: 16, 3: 8}
OFFS, _at = {}, 0
for _d in DIRS:
    OFFS[_d] = (_at, SIZE[sum(map(abs, _d))])
    _at += OFFS[_d][1]
NS, NF = _at, 6 * SIZE[1]
K_COL = np.full((NS, 1), -1, np.int32)
for _d in DIRS:
    _sel = [[0] if v == -1 else [M - 1] if v == 1 else list(range(M)) for v in _d]
    for _r, (_i, _j, _k) in enumerate((i, j, k) for i in _sel[0] for j in _sel[1] for k in _sel[2]):
        K_COL[OFFS[_d][0] + _r, 0] = B_POS[(_i * M + _j) * M + _k]

CORNERS = [(x, y, z) for x in (0, 1) for y in (0, 1) for z in (0, 1)]
PRIM = [(0, o) for o in CORNERS]
PRIM += [(1, (0, y, z)) for y in (0, 1) for z in (0, 1)]
PRIM += [(2, (x, 0, z)) for x in (0, 1) for z in (0, 1)]
PRIM += [(3, (x, y, 0)) for x in (0, 1) for y in (0, 1)]
S64 = one_hot([CORNERS.index(o) * 8 + t for t, o in PRIM], np.arange(20), (64, 24))
TILE = np.tile(np.eye(24, dtype=np.float32), (1, 8))
TMASK = (np.arange(64)[:, None] // 8 == np.arange(192)[None, :] // 24).astype(np.float32)
SPREAD = np.zeros((192, 128), np.float32)
for _c, _o1 in enumerate(CORNERS):
    for _q, (_t, _o2) in enumerate(PRIM):
        _f = [b - a + 1 for a, b in zip(_o1, _o2)]
        SPREAD[_c * 24 + _q, _t * 27 + (_f[0] * 3 + _f[1]) * 3 + _f[2]] = 1.0


def dot(a, b, ca=1, cb=0):
    return lax.dot_general(
        a, b, (((ca,), (cb,)), ((), ())), precision=lax.Precision.HIGHEST, preferred_element_type=F32
    )


def pieces(x):
    h = x.astype(BF16)
    r = x - h.astype(F32)
    m = r.astype(BF16)
    return h, m, (r - m.astype(F32)).astype(BF16)


def mm(a, b, ca=1, cb=0):
    return lax.dot_general(a, b, (((ca,), (cb,)), ((), ())), preferred_element_type=F32)


def pick(sel, x):
    h, m, l = pieces(x)
    if x.shape[1] > 128:
        return mm(sel, h) + mm(sel, m) + mm(sel, l)
    n = x.shape[1]
    d = mm(sel, jnp.concatenate([h, m], axis=1))
    return d[:, :n] + d[:, n:] + mm(sel, l)


def pick_cols(x, sel):
    h, m, l = pieces(x)
    return mm(h, sel, 1, 1) + mm(m, sel, 1, 1) + mm(l, sel, 1, 1)


def dot6(a, b):
    b1, b2, b3 = pieces(b)
    n = b.shape[1]
    b12 = jnp.concatenate([b1, b2], axis=1)
    d = mm(a[1], b12) + mm(a[0], b12)
    return (mm(a[0], b3) + mm(a[2], b1)) + d[:, n:] + d[:, :n]


def here():
    return lax.axis_index("gx"), lax.axis_index("gy"), lax.axis_index("gz")


def at(d):
    x, y, z = here()
    return (lax.rem(x + d[0] + GX, GX), lax.rem(y + d[1] + GY, GY), lax.rem(z + d[2] + GZ, GZ))


PLANE = [(x, y, 0) for x in range(GX) for y in range(GY) if (x, y) != (0, 0)]
LINE = [(0, 0, z) for z in range(1, GZ)]
_norm = lambda d: (d[0] % GX, d[1] % GY, d[2] % GZ)
PARTNERS = sorted({_norm(d) for d in DIRS + PLANE + LINE})


def remote(src, dst, sems, k, d):
    return pltpu.make_async_remote_copy(
        src_ref=src, dst_ref=dst, send_sem=sems.at[2 * k], recv_sem=sems.at[2 * k + 1], device_id=at(d), device_id_type=MESH
    )


def exchange_start(send, recv, sems, k, faces):
    for d in DIRS:
        if (sum(map(abs, d)) == 1) == faces:
            o, n = OFFS[d]
            o2, _ = OFFS[tuple(-v for v in d)]
            remote(send.at[pl.ds(o, n)], recv.at[pl.ds(o2, n)], sems, k, d).start()


FACE_ROWS, REST_ROWS = pl.ds(0, NF), pl.ds(NF, NS - NF)


def swap_start(v, pk, send, recv, sems, k):
    send[REST_ROWS, :] = pick(pk[NF:], v)
    exchange_start(send, recv, sems, k + 1, False)
    send[FACE_ROWS, :] = pick(pk[:NF], v)
    exchange_start(send, recv, sems, k, True)


def swap_finish(v, pkt, send, recv, sems, k):
    bulk_wait(send.at[FACE_ROWS], recv.at[FACE_ROWS], sems, k)
    v = v + pick(pkt[:, :NF], recv[FACE_ROWS, :])
    bulk_wait(send.at[REST_ROWS], recv.at[REST_ROWS], sems, k + 1)
    return v + pick(pkt[:, NF:], recv[REST_ROWS, :])


def bulk_wait(send, recv, sems, k):
    c = remote(send, recv, sems, k, (1, 0, 0))
    c.wait_recv()
    c.wait_send()


def owner_start(send, recv, sems, k):
    for c, o in enumerate(CORNERS):
        if c:
            remote(send.at[pl.ds(8 * c, 8)], recv.at[pl.ds(8 * c, 8)], sems, k, o).start()


def owner_finish(send, recv, sems, k):
    bulk_wait(send.at[pl.ds(8, 56)], recv.at[pl.ds(8, 56)], sems, k)
    out = send[pl.ds(0, 8), :]
    for c in range(1, 8):
        out = out + recv[pl.ds(8 * c, 8), :]
    return out


def gather_start(val, plane, sems, k):
    x, y, _ = here()
    ab = x * GY + y
    odd = lax.rem(y, 2) == 1
    plane[ab] = jnp.where(jnp.full((8, 128), odd), pltpu.roll(val, 4, 0), val)
    for d in PLANE:
        remote(plane.at[ab], plane.at[ab], sems, k, d).start()


def gather_turn(plane, full, sems, k):
    bulk_wait(plane.at[pl.ds(0, 15)], plane.at[pl.ds(0, 15)], sems, k)
    _, _, z = here()
    pos = place(z)
    rows = [plane[2 * i] + plane[2 * i + 1] for i in range(8)]
    mine = pl.ds(pl.multiple_of(pos * 64, 64), 64)
    full[mine, :] = jnp.concatenate(rows, axis=0)
    for d in LINE:
        remote(full.at[mine], full.at[mine], sems, k + 1, d).start()


def gather_finish(full, sems, k):
    bulk_wait(full.at[pl.ds(0, 448)], full.at[pl.ds(0, 448)], sems, k + 1)


def reduce_start(val, plane, sems, k):
    x, y, _ = here()
    ab = x * GY + y
    plane[ab] = val
    for d in PLANE:
        remote(plane.at[ab], plane.at[ab], sems, k, d).start()


def reduce_turn(plane, line, sems, k):
    bulk_wait(plane.at[pl.ds(0, 15)], plane.at[pl.ds(0, 15)], sems, k)
    _, _, z = here()
    line[z] = jnp.sum(plane[...], axis=0)
    for d in LINE:
        remote(line.at[z], line.at[z], sems, k + 1, d).start()


def reduce_finish(line, sems, k):
    bulk_wait(line.at[pl.ds(0, 7)], line.at[pl.ds(0, 7)], sems, k + 1)
    return jnp.sum(line[...], axis=0)


SPLIT = []
for _i in range(M):
    for _j in range(M):
        _n = (_i * M + _j) * M
        if _i in (0, M - 1) or _j in (0, M - 1):
            SPLIT.append((_i, _j, [(False, 0, B_POS[_n], M)]))
        else:
            SPLIT.append((_i, _j, [(False, 0, B_POS[_n], 1), (True, 1, I_POS[_n + 1], M - 2), (False, M - 1, B_POS[_n + M - 1], 1)]))


def choose(ids_ref, n):
    ids = ids_ref[...]
    return (lax.broadcasted_iota(jnp.int32, (ids.shape[0], n), 1) == ids).astype(F32).astype(BF16)


def place(z):
    h = z // 2
    return lax.rem(z, 2) * h + (1 - lax.rem(z, 2)) * (6 - 2 * lax.rem(h, 2) + h // 2)


def coords(m):
    pos = m >> 6
    c = jnp.where(pos < 4, 2 * pos + 1, jnp.where(pos < 6, 4 * pos - 14, 4 * pos - 24))
    return (m >> 4) & 3, (m >> 2) & 3, c, m & 3


def build_coarse(kall_ref, kc):
    kall = kall_ref[...]
    ra, rb, rc, _ = coords(lax.broadcasted_iota(jnp.int32, (512, 128), 0))
    for j in range(4):
        ca, cb, cc, ct = coords(lax.broadcasted_iota(jnp.int32, (1, 128), 1) + 128 * j)
        da, db, dc = (ca + 1 - ra) & 3, (cb + 1 - rb) & 3, (cc + 1 - rc) & 7
        hit = (da < 3) & (db < 3) & (dc < 3)
        slot = jnp.where(hit, ct * 27 + da * 9 + db * 3 + dc, 0)
        v = jnp.take_along_axis(kall, slot, axis=1, mode="promise_in_bounds")
        kc[:, pl.ds(128 * j, 128)] = jnp.where(hit, v, 0.0)


def sweep(ref, n):
    lane = lax.broadcasted_iota(jnp.int32, (n, 128), 1)
    base = lane // n * n
    take = lambda v, idx: jnp.take_along_axis(v, idx, axis=1, mode="promise_in_bounds")

    def body(i, carry):
        k = 2 * i
        i0, i1 = base + k, base + k + 1
        s0, s1 = i0[0:8], i1[0:8]
        for j in range(ref.shape[0]):
            x = ref[j]
            r0 = jnp.broadcast_to(ref[j, pl.ds(k, 1), :], (8, 128))
            r1 = jnp.broadcast_to(ref[j, pl.ds(k + 1, 1), :], (8, 128))
            c0, c1 = take(x, i0), take(x, i1)
            p, q, r = take(r0, s0), take(r0, s1), take(r1, s1)
            d = 1.0 / (p * r - q * q)
            b00, b01, b11 = r * d, -q * d, p * d
            on0, on1 = lane[0:8] == s0, lane[0:8] == s1
            n0 = jnp.where(on0, b00, jnp.where(on1, b01, b00 * r0 + b01 * r1))
            n1 = jnp.where(on0, b01, jnp.where(on1, b11, b01 * r0 + b11 * r1))
            left = jnp.where((lane == i0) | (lane == i1), 0.0, x)
            ref[j] = left - c0 * n0[0:1] - c1 * n1[0:1]
            ref[j, pl.ds(k, 1), :] = n0[0:1]
            ref[j, pl.ds(k + 1, 1), :] = n1[0:1]
        return carry

    lax.fori_loop(0, n // 2, body, 0)


def program(load_h, a_h, di_h, n_h, phi_h, bcol, icol, kcol, krow, wt_ref, s64_ref, tile_ref, tmask_ref, spread_ref,
            xb_ref, xi_ref, rb_ref, ri_ref,
            load_v, a_v, n_v, arows, nrows, di_v, phi_v, lb_v, li_v, send, recv, ssend, srecv,
            ksend, krecv, hsend, hrecv, kplane, gplane, kfull, gfull, rplane, rline, kc, xo, x2, xf, sems, dsems):
    sem = pltpu.get_barrier_semaphore()
    for d in PARTNERS:
        pl.semaphore_signal(sem, inc=1, device_id=at(d), device_id_type=MESH)

    get_phi = pltpu.make_async_copy(phi_h.at[:, 0, :], phi_v, dsems.at[0])
    get_load = pltpu.make_async_copy(load_h, load_v, dsems.at[1])
    get_di = pltpu.make_async_copy(di_h.at[:, 0, :], di_v, dsems.at[2])
    get_phi.start()
    get_a = pltpu.make_async_copy(a_h.at[:, 0, :], a_v, dsems.at[3])
    get_n = pltpu.make_async_copy(n_h.at[:, 0, :], n_v, dsems.at[4])
    get_a.start()
    get_load.start()
    get_di.start()
    get_n.start()

    def border_rows(src, dst):
        dst[pl.ds(NB - 8, 8), :] = jnp.zeros((8, NODES), F32)
        for r, n, c in RUNS:
            dst[pl.ds(r, c), :] = src[pl.ds(n, c), :]

    pb, pi, pk = choose(bcol, NODES), choose(icol, NODES), choose(kcol, NB)
    pkt = (lax.broadcasted_iota(jnp.int32, (NB, NS), 0) == krow[...]).astype(F32).astype(BF16)
    wt = wt_ref[...]

    get_phi.wait()
    phi = jnp.concatenate([phi_v[...], jnp.zeros((4, NODES), F32)], axis=0)
    p24 = pick_cols(phi, pb)
    get_a.wait()
    border_rows(a_v, arows)
    ab = arows[...]
    k24 = dot(p24, dot(ab, phi, 1, 1))
    k64 = dot(dot(s64_ref[...], k24), tile_ref[...]) * tmask_ref[...]
    ksend[...] = dot(k64, spread_ref[...])
    pl.semaphore_wait(sem, len(PARTNERS))
    owner_start(ksend, krecv, sems, 0)

    get_load.wait()
    lb_v[pl.ds(NB - 8, 8), :] = jnp.zeros((8, RHS), F32)
    for i, j, parts in SPLIT:
        for inner, k, r, c in parts:
            (li_v if inner else lb_v)[pl.ds(r, c), :] = load_v[i, j, pl.ds(k, c), :]
    lb, li = lb_v[...], li_v[...]
    get_di.wait()
    di = di_v[...]
    start = dot(di, li)
    abi = pick_cols(ab, pi)
    c = lb - dot(abi, start)
    cl = jnp.concatenate([c, lb], axis=1)
    swap_start(cl, pk, send, recv, sems, 18)
    gather_start(owner_finish(ksend, krecv, sems, 0), kplane, sems, 2)
    k0 = jnp.sum(li * start, axis=0, keepdims=True)
    x = dot(di, abi, 1, 1)
    asm = swap_finish(cl, pkt, send, recv, sems, 18)
    f = wt * asm[:, 0:RHS]
    hsend[0] = dot(s64_ref[...], dot(p24, f))
    owner_start(hsend.at[0], hrecv.at[0], sems, 4)
    gather_turn(kplane, kfull, sems, 2)
    s = pieces(pick_cols(ab, pb) - dot(abi, x))
    get_n.wait()
    border_rows(n_v, nrows)
    nbb = pieces(pick_cols(nrows[...], pb))
    w = dot6(nbb, f)
    gather_start(owner_finish(hsend.at[0], hrecv.at[0], sems, 4), gplane.at[0], sems, 5)
    gather_finish(kfull, sems, 2)

    build_coarse(kfull, kc)
    low = lax.broadcasted_iota(jnp.int32, (64, 128), 1) < 64
    for j in range(2):
        cut = pl.ds(128 * j, 128)
        xo[j] = jnp.where(low, kc[pl.ds(128 * j, 64), cut], kc[pl.ds(128 * j + 64, 64), cut])
    sweep(xo, 64)
    gather_turn(gplane.at[0], gfull.at[0], sems, 5)
    group = lax.broadcasted_iota(jnp.int32, (64, 256), 1) // 64
    both = jnp.concatenate([xo[0], xo[1]], axis=1)
    inv_o = jnp.concatenate([jnp.where(group == g, both, 0.0) for g in range(4)], axis=0)
    koe = kc[pl.ds(0, 256), pl.ds(256, 256)]
    m = dot(inv_o, koe)
    se = kc[pl.ds(256, 256), pl.ds(256, 256)] - dot(koe, m, 0, 0)
    x2[0] = jnp.where(low, se[0:64, 0:128], se[64:128, 0:128])
    sweep(x2, 64)
    inv_2 = jnp.concatenate([jnp.where(low, x2[0], 0.0), jnp.where(low, 0.0, x2[0])], axis=0)
    k2f = se[0:128, 128:256]
    m2 = dot(inv_2, k2f)
    xf[0] = se[128:256, 128:256] - dot(k2f, m2, 0, 0)
    sweep(xf, 128)
    prim = lax.broadcasted_iota(jnp.int32, (24, 512), 0)
    want = jnp.full((24, 512), -1, jnp.int32)
    for q, (t, o) in enumerate(PRIM):
        cx, cy, cz = at(o)
        want = jnp.where(prim == q, place(cz) * 64 + (cx * GY + cy) * 4 + t, want)
    sel = (want == lax.broadcasted_iota(jnp.int32, (24, 512), 1)).astype(F32)
    so = sel[:, 0:256]
    s_e = sel[:, 256:512] - dot(so, m)
    s_2 = s_e[:, 0:128]
    wf = dot(s_e[:, 128:256] - dot(s_2, m2), xf[0])
    w2 = dot(s_2, inv_2) - dot(wf, m2, 1, 1)
    we = jnp.concatenate([w2, wf], axis=1)
    w24 = jnp.concatenate([dot(so, inv_o) - dot(we, m, 1, 1), we], axis=1)

    def apply_coarse(w, g):
        return wt * (w + dot(p24, dot(w24, g), 0, 0))

    part = lambda a, b: jnp.sum(a * b, axis=0, keepdims=True)
    gather_finish(gfull.at[0], sems, 5)
    u = apply_coarse(w, gfull[0])
    swap_start(u, pk, ssend.at[0], srecv.at[0], sems, 20)
    z1 = swap_finish(u, pkt, ssend.at[0], srecv.at[0], sems, 20)
    t1 = dot6(s, z1)
    swap_start(t1, pk, ssend.at[1], srecv.at[1], sems, 22)
    reduce_start(jnp.concatenate([k0, part(c, z1), part(z1, t1), jnp.zeros((5, RHS), F32)], axis=0), rplane.at[0], sems, 11)
    at1 = swap_finish(t1, pkt, ssend.at[1], srecv.at[1], sems, 22)
    f = wt * at1
    hsend[1] = dot(s64_ref[...], dot(p24, f))
    owner_start(hsend.at[1], hrecv.at[1], sems, 13)
    w = dot6(nbb, f)
    reduce_turn(rplane.at[0], rline.at[0], sems, 11)
    gather_start(owner_finish(hsend.at[1], hrecv.at[1], sems, 13), gplane.at[1], sems, 14)
    gather_turn(gplane.at[1], gfull.at[1], sems, 14)
    sums = reduce_finish(rline.at[0], sems, 11)
    k0s = sums[0:1]
    g0 = k0s + sums[1:2]
    s1 = g0 / (k0s + sums[2:3])
    gather_finish(gfull.at[1], sems, 14)
    u = apply_coarse(w, gfull[1])
    swap_start(u, pk, ssend.at[2], srecv.at[2], sems, 24)
    z2 = swap_finish(u, pkt, ssend.at[2], srecv.at[2], sems, 24)
    t2 = dot6(s, z2)
    swap_start(t2, pk, ssend.at[3], srecv.at[3], sems, 26)
    zp, tp, cp = z1 - s1 * z2, t1 - s1 * t2, c - s1 * t1
    reduce_start(jnp.concatenate([part(cp, zp), part(zp, tp), jnp.zeros((6, RHS), F32)], axis=0), rplane.at[1], sems, 16)
    at2 = swap_finish(t2, pkt, ssend.at[3], srecv.at[3], sems, 26)
    reduce_turn(rplane.at[1], rline.at[1], sems, 16)
    last = reduce_finish(rline.at[1], sems, 16)
    rest = 1.0 - s1
    g1 = rest * rest * k0s + last[0:1]
    beta = g1 / g0
    s2 = g1 / (rest * rest * k0s + last[1:2] - beta * g1 / s1)

    xb = s1 * z1 + s2 * (zp + beta * z1)
    xi = (s1 + s2 * (rest + beta)) * start - dot(x, xb)
    kappa = rest * (1.0 - s2) - s2 * beta
    ac = asm[:, 0:RHS]
    ae = asm[:, RHS : 2 * RHS] - ac
    rb = kappa * ae + (ac - s1 * at1) - s2 * ((at1 - s1 * at2) + beta * at1)
    xb_ref[...], xi_ref[...] = xb, xi
    rb_ref[...], ri_ref[...] = rb, kappa * li


def spread(xb_ref, xi_ref, rb_ref, ri_ref, sol_ref, res_ref):
    for i, j, parts in SPLIT:
        for inner, k, r, c in parts:
            rows, there = pl.ds(r, c), pl.ds(k, c)
            sol_ref[i, j, there, :] = (xi_ref if inner else xb_ref)[rows, :]
            res_ref[i, j, there, :] = (ri_ref if inner else rb_ref)[rows, :]


def local(load, a, di, n, phi):
    tables = [jnp.asarray(v) for v in (B_COL, I_COL, K_COL, K_COL.T, WEIGHT, S64, TILE, TMASK, SPREAD)]
    V = lambda *s: pltpu.VMEM(s, F32)
    shape = jax.ShapeDtypeStruct((M, M, M, RHS), F32)
    half = [jax.ShapeDtypeStruct((NB, RHS), F32), jax.ShapeDtypeStruct((NI, RHS), F32)] * 2
    parts = pl.pallas_call(
        program,
        out_shape=half,
        in_specs=[pl.BlockSpec(memory_space=pl.ANY)] * 5 + [VM] * len(tables),
        out_specs=[VM] * 4,
        scratch_shapes=[
            V(M, M, M, RHS), V(NODES, NODES), V(NODES, NODES), V(NB, NODES), V(NB, NODES), V(NI, NI), V(20, NODES), V(NB, RHS), V(NI, RHS),
            V(NS, 2 * RHS), V(NS, 2 * RHS), V(4, NS, RHS), V(4, NS, RHS),
            V(64, 128), V(64, 128), V(2, 64, 128), V(2, 64, 128), V(16, 8, 128), V(2, 16, 8, 128), V(512, 128), V(2, 512, 128),
            V(2, 16, 8, 128), V(2, 8, 8, 128), V(512, 512), V(2, 64, 128), V(1, 64, 128), V(1, 128, 128),
            pltpu.SemaphoreType.DMA((56,)), pltpu.SemaphoreType.DMA((5,)),
        ],
        compiler_params=pltpu.CompilerParams(vmem_limit_bytes=60 * 2**20, collective_id=0, has_side_effects=True),
        name="program",
    )(load, a.reshape(NODES, 1, NODES), di.reshape(NI, 1, NI), n.reshape(NODES, 1, NODES), phi.reshape(20, 1, NODES), *tables)
    return tuple(pl.pallas_call(
        spread, out_shape=[shape, shape], in_specs=[VM] * 4, out_specs=[VM] * 2,
        compiler_params=pltpu.CompilerParams(vmem_limit_bytes=16 * 2**20), name="spread",
    )(*parts))


def solution(mesh):
    spec4, spec5 = P("gx", "gy", "gz", None), P("gx", "gy", "gz", None, None)
    return jax.shard_map(
        local, mesh=mesh, in_specs=(spec4, spec5, spec5, spec5, spec5), out_specs=(spec4, spec4), check_vma=False
    )
```

```python
import functools

import jax
import jax.numpy as jnp
import numpy as np
from jax import lax
from jax.experimental import pallas as pl
from jax.experimental.pallas import tpu as pltpu
from jax.sharding import PartitionSpec as P

MESH = pl.DeviceIdType.MESH
F32, BF16 = jnp.float32, jnp.bfloat16
GX, GY, GZ = 4, 4, 8
M = 9
NODES, NB, NI, RHS = 729, 392, 343, 128
ORDER = (1, 3, 5, 7, 2, 6, 0, 4)
VM = pl.BlockSpec(memory_space=pltpu.VMEM)

_g = np.indices((M, M, M)).reshape(3, -1)
_rim = ((_g == 0) | (_g == M - 1)).sum(0)
B_IDS, I_IDS = np.where(_rim > 0)[0], np.where(_rim == 0)[0]
B_POS = {int(n): r for r, n in enumerate(B_IDS)}
I_POS = {int(n): r for r, n in enumerate(I_IDS)}


def one_hot(rows, cols, shape):
    out = np.zeros(shape, np.float32)
    out[rows, cols] = 1.0
    return out


B_COL = np.full((NB, 1), -1, np.int32)
B_COL[: len(B_IDS), 0] = B_IDS
I_COL = I_IDS.astype(np.int32)[:, None]
RUNS, _r = [], 0
while _r < len(B_IDS):
    _e = _r + 1
    while _e < len(B_IDS) and B_IDS[_e] == B_IDS[_e - 1] + 1:
        _e += 1
    RUNS.append((_r, int(B_IDS[_r]), _e - _r))
    _r = _e
WEIGHT = np.zeros((NB, 1), np.float32)
WEIGHT[: len(B_IDS), 0] = 1.0 / 2.0 ** _rim[B_IDS]
WEIGHT = np.broadcast_to(WEIGHT, (NB, RHS)).copy()

DIRS = sorted(
    ((x, y, z) for x in (-1, 0, 1) for y in (-1, 0, 1) for z in (-1, 0, 1) if (x, y, z) != (0, 0, 0)),
    key=lambda d: (sum(map(abs, d)), d),
)
SIZE = {1: 88, 2: 16, 3: 8}
OFFS, _at = {}, 0
for _d in DIRS:
    OFFS[_d] = (_at, SIZE[sum(map(abs, _d))])
    _at += OFFS[_d][1]
NS, NF = _at, 6 * SIZE[1]
K_COL = np.full((NS, 1), -1, np.int32)
for _d in DIRS:
    _sel = [[0] if v == -1 else [M - 1] if v == 1 else list(range(M)) for v in _d]
    for _r, (_i, _j, _k) in enumerate((i, j, k) for i in _sel[0] for j in _sel[1] for k in _sel[2]):
        K_COL[OFFS[_d][0] + _r, 0] = B_POS[(_i * M + _j) * M + _k]

CORNERS = [(x, y, z) for x in (0, 1) for y in (0, 1) for z in (0, 1)]
PRIM = [(0, o) for o in CORNERS]
PRIM += [(1, (0, y, z)) for y in (0, 1) for z in (0, 1)]
PRIM += [(2, (x, 0, z)) for x in (0, 1) for z in (0, 1)]
PRIM += [(3, (x, y, 0)) for x in (0, 1) for y in (0, 1)]
S64 = one_hot([CORNERS.index(o) * 8 + t for t, o in PRIM], np.arange(20), (64, 24))
TMASK = (np.arange(64)[:, None] // 8 == np.arange(192)[None, :] // 24).astype(np.float32)
SPREAD = np.zeros((192, 128), np.float32)
for _c, _o1 in enumerate(CORNERS):
    for _q, (_t, _o2) in enumerate(PRIM):
        _f = [b - a + 1 for a, b in zip(_o1, _o2)]
        SPREAD[_c * 24 + _q, _t * 27 + (_f[0] * 3 + _f[1]) * 3 + _f[2]] = 1.0


def dot(a, b, ca=1, cb=0):
    return lax.dot_general(
        a, b, (((ca,), (cb,)), ((), ())), precision=lax.Precision.HIGHEST, preferred_element_type=F32
    )


def pieces(x):
    h = x.astype(BF16)
    r = x - h.astype(F32)
    m = r.astype(BF16)
    return h, m, (r - m.astype(F32)).astype(BF16)


def mm(a, b, ca=1, cb=0):
    return lax.dot_general(a, b, (((ca,), (cb,)), ((), ())), preferred_element_type=F32)


def pick(sel, x):
    h, m, l = pieces(x)
    if x.shape[1] > 128:
        return mm(sel, h) + mm(sel, m) + mm(sel, l)
    n = x.shape[1]
    d = mm(sel, jnp.concatenate([h, m], axis=1))
    return d[:, :n] + d[:, n:] + mm(sel, l)


def pick_cols(x, sel):
    h, m, l = pieces(x)
    return mm(h, sel, 1, 1) + mm(m, sel, 1, 1) + mm(l, sel, 1, 1)


def dot6(a, b):
    b1, b2, b3 = pieces(b)
    n = b.shape[1]
    b12 = jnp.concatenate([b1, b2], axis=1)
    d = mm(a[1], b12) + mm(a[0], b12)
    return (mm(a[0], b3) + mm(a[2], b1)) + d[:, n:] + d[:, :n]


def pick_right(x, sel):
    h, m, l = pieces(x)
    return mm(h, sel) + mm(m, sel) + mm(l, sel)


def here():
    return lax.axis_index("gx"), lax.axis_index("gy"), lax.axis_index("gz")


def at(d):
    x, y, z = here()
    return (lax.rem(x + d[0] + GX, GX), lax.rem(y + d[1] + GY, GY), lax.rem(z + d[2] + GZ, GZ))


PLANE = [(x, y, 0) for x in range(GX) for y in range(GY) if (x, y) != (0, 0)]
LINE = [(0, 0, z) for z in range(1, GZ)]
_norm = lambda d: (d[0] % GX, d[1] % GY, d[2] % GZ)
PARTNERS = sorted({_norm(d) for d in DIRS + PLANE + LINE})


def remote(src, dst, sems, k, d):
    return pltpu.make_async_remote_copy(
        src_ref=src, dst_ref=dst, send_sem=sems.at[2 * k], recv_sem=sems.at[2 * k + 1], device_id=at(d), device_id_type=MESH
    )


def exchange_start(send, recv, sems, k, faces):
    for d in DIRS:
        if (sum(map(abs, d)) == 1) == faces:
            o, n = OFFS[d]
            o2, _ = OFFS[tuple(-v for v in d)]
            remote(send.at[pl.ds(o, n)], recv.at[pl.ds(o2, n)], sems, k, d).start()


FACE_ROWS, REST_ROWS = pl.ds(0, NF), pl.ds(NF, NS - NF)


def swap_start(v, pk, send, recv, sems, k):
    send[REST_ROWS, :] = pick(pk[NF:], v)
    exchange_start(send, recv, sems, k + 1, False)
    send[FACE_ROWS, :] = pick(pk[:NF], v)
    exchange_start(send, recv, sems, k, True)


def swap_finish(v, pkt, send, recv, sems, k):
    bulk_wait(send.at[FACE_ROWS], recv.at[FACE_ROWS], sems, k)
    v = v + pick(pkt[:, :NF], recv[FACE_ROWS, :])
    bulk_wait(send.at[REST_ROWS], recv.at[REST_ROWS], sems, k + 1)
    return v + pick(pkt[:, NF:], recv[REST_ROWS, :])


def bulk_wait(send, recv, sems, k):
    c = remote(send, recv, sems, k, (1, 0, 0))
    c.wait_recv()
    c.wait_send()


def owner_start(send, recv, sems, k):
    for c, o in enumerate(CORNERS):
        if c:
            remote(send.at[pl.ds(8 * c, 8)], recv.at[pl.ds(8 * c, 8)], sems, k, o).start()


def owner_finish(send, recv, sems, k):
    bulk_wait(send.at[pl.ds(8, 56)], recv.at[pl.ds(8, 56)], sems, k)
    out = send[pl.ds(0, 8), :]
    for c in range(1, 8):
        out = out + recv[pl.ds(8 * c, 8), :]
    return out


def gather_start(val, plane, sems, k):
    x, y, _ = here()
    ab = x * GY + y
    odd = lax.rem(y, 2) == 1
    plane[ab] = jnp.where(jnp.full((8, 128), odd), pltpu.roll(val, 4, 0), val)
    for d in PLANE:
        remote(plane.at[ab], plane.at[ab], sems, k, d).start()


def gather_turn(plane, full, sems, k):
    bulk_wait(plane.at[pl.ds(0, 15)], plane.at[pl.ds(0, 15)], sems, k)
    _, _, z = here()
    pos = place(z)
    rows = [plane[2 * i] + plane[2 * i + 1] for i in range(8)]
    mine = pl.ds(pl.multiple_of(pos * 64, 64), 64)
    full[mine, :] = jnp.concatenate(rows, axis=0)
    for d in LINE:
        remote(full.at[mine], full.at[mine], sems, k + 1, d).start()


def gather_finish(full, sems, k):
    bulk_wait(full.at[pl.ds(0, 448)], full.at[pl.ds(0, 448)], sems, k + 1)


def reduce_start(val, plane, sems, k):
    x, y, _ = here()
    ab = x * GY + y
    plane[ab] = val
    for d in PLANE:
        remote(plane.at[ab], plane.at[ab], sems, k, d).start()


def reduce_turn(plane, line, sems, k):
    bulk_wait(plane.at[pl.ds(0, 15)], plane.at[pl.ds(0, 15)], sems, k)
    _, _, z = here()
    line[z] = jnp.sum(plane[...], axis=0)
    for d in LINE:
        remote(line.at[z], line.at[z], sems, k + 1, d).start()


def reduce_finish(line, sems, k):
    bulk_wait(line.at[pl.ds(0, 7)], line.at[pl.ds(0, 7)], sems, k + 1)
    return jnp.sum(line[...], axis=0)


SPLIT = []
for _i in range(M):
    for _j in range(M):
        _n = (_i * M + _j) * M
        if _i in (0, M - 1) or _j in (0, M - 1):
            SPLIT.append((_i, _j, [(False, 0, B_POS[_n], M)]))
        else:
            SPLIT.append((_i, _j, [(False, 0, B_POS[_n], 1), (True, 1, I_POS[_n + 1], M - 2), (False, M - 1, B_POS[_n + M - 1], 1)]))


def choose(ids_ref, n):
    ids = ids_ref[...]
    return (lax.broadcasted_iota(jnp.int32, (ids.shape[0], n), 1) == ids).astype(F32).astype(BF16)


def place(z):
    h = z // 2
    return lax.rem(z, 2) * h + (1 - lax.rem(z, 2)) * (6 - 2 * lax.rem(h, 2) + h // 2)


def coords(m):
    pos = m >> 6
    c = jnp.where(pos < 4, 2 * pos + 1, jnp.where(pos < 6, 4 * pos - 14, 4 * pos - 24))
    return (m >> 4) & 3, (m >> 2) & 3, c, m & 3


def build_coarse(kall_ref, kc):
    kall = kall_ref[...]
    ra, rb, rc, _ = coords(lax.broadcasted_iota(jnp.int32, (512, 128), 0))
    for j in range(4):
        ca, cb, cc, ct = coords(lax.broadcasted_iota(jnp.int32, (1, 128), 1) + 128 * j)
        da, db, dc = (ca + 1 - ra) & 3, (cb + 1 - rb) & 3, (cc + 1 - rc) & 7
        hit = (da < 3) & (db < 3) & (dc < 3)
        slot = jnp.where(hit, ct * 27 + da * 9 + db * 3 + dc, 0)
        v = jnp.take_along_axis(kall, slot, axis=1, mode="promise_in_bounds")
        kc[:, pl.ds(128 * j, 128)] = jnp.where(hit, v, 0.0)


def sweep(ref, n):
    lane = lax.broadcasted_iota(jnp.int32, (n, 128), 1)
    base = lane // n * n
    take = lambda v, idx: jnp.take_along_axis(v, idx, axis=1, mode="promise_in_bounds")

    def body(i, carry):
        k = 4 * i
        idx = [base + (k + q) for q in range(4)]
        top = [v[0:8] for v in idx]
        stored = []
        for j in range(ref.shape[0]):
            x = ref[j]
            rows = [jnp.broadcast_to(ref[j, pl.ds(k + q, 1), :], (8, 128)) for q in range(4)]
            a, b, c = take(rows[0], top[0]), take(rows[0], top[1]), take(rows[1], top[1])
            e, f, g, h = take(rows[0], top[2]), take(rows[0], top[3]), take(rows[1], top[2]), take(rows[1], top[3])
            p, q, r = take(rows[2], top[2]), take(rows[2], top[3]), take(rows[3], top[3])
            cols = [take(x, v) for v in idx]
            d = 1.0 / (a * c - b * b)
            a, b, c = c * d, -b * d, a * d
            we, wf, wg, wh = a * e + b * g, a * f + b * h, b * e + c * g, b * f + c * h
            p, q, r = p - (e * we + g * wg), q - (e * wf + g * wh), r - (f * wf + h * wh)
            d = 1.0 / (p * r - q * q)
            p, q, r = r * d, -q * d, p * d
            ue, uf, ug, uh = we * p + wf * q, we * q + wf * r, wg * p + wh * q, wg * q + wh * r
            a, b, c = a + (ue * we + uf * wf), b + (ue * wg + uf * wh), c + (ug * wg + uh * wh)
            inv = [[a, b, -ue, -uf], [b, c, -ug, -uh], [-ue, -ug, p, q], [-uf, -uh, q, r]]
            on = [lane[0:8] == v for v in top]
            new = []
            for m in inv:
                v = (m[0] * rows[0] + m[1] * rows[1]) + (m[2] * rows[2] + m[3] * rows[3])
                for q in range(4):
                    v = jnp.where(on[q], m[q], v)
                new.append(v[0:1])
            left = jnp.where((lane >= idx[0]) & (lane <= idx[3]), 0.0, x)
            stored.append((left - (cols[0] * new[0] + cols[1] * new[1]) - (cols[2] * new[2] + cols[3] * new[3]), new))
        for j, (v, new) in enumerate(stored):
            ref[j] = v
            for q in range(4):
                ref[j, pl.ds(k + q, 1), :] = new[q]
        return carry

    lax.fori_loop(0, n // 4, body, 0)


def program(load_h, a_h, di_h, n_h, phi_h, bcol, icol, kcol, krow, wt_ref, s64_ref, tmask_ref, spread_ref,
            parts_ref,
            load_v, a_v, n_v, arows, nrows, di_v, phi_v, lb_v, li_v, send, recv, ssend, srecv,
            ksend, krecv, hsend, hrecv, kplane, gplane, kfull, gfull, rplane, rline, kc, xo, x2, xf, sems, dsems):
    sem = pltpu.get_barrier_semaphore()
    for d in PARTNERS:
        pl.semaphore_signal(sem, inc=1, device_id=at(d), device_id_type=MESH)

    get_phi = pltpu.make_async_copy(phi_h.at[:, 0, :], phi_v, dsems.at[0])
    get_load = pltpu.make_async_copy(load_h, load_v, dsems.at[1])
    get_di = pltpu.make_async_copy(di_h.at[:, 0, :], di_v, dsems.at[2])
    get_phi.start()
    get_a = pltpu.make_async_copy(a_h.at[:, 0, :], a_v, dsems.at[3])
    get_n = pltpu.make_async_copy(n_h.at[:, 0, :], n_v, dsems.at[4])
    get_a.start()
    get_load.start()
    get_di.start()
    get_n.start()

    def border_rows(src, dst):
        dst[pl.ds(NB - 8, 8), :] = jnp.zeros((8, NODES), F32)
        for r, n, c in RUNS:
            dst[pl.ds(r, c), :] = src[pl.ds(n, c), :]

    pb, pi, pk = choose(bcol, NODES), choose(icol, NODES), choose(kcol, NB)
    pkt = (lax.broadcasted_iota(jnp.int32, (NB, NS), 0) == krow[...]).astype(F32).astype(BF16)
    wt = wt_ref[...]

    get_phi.wait()
    phi = jnp.concatenate([phi_v[...], jnp.zeros((4, NODES), F32)], axis=0)
    phi8 = jnp.concatenate([phi] * 8, axis=0)
    p24 = pick_cols(phi, pb)
    p64 = pick(s64_ref[...].astype(BF16), p24)
    get_a.wait()
    border_rows(a_v, arows)
    ab = arows[...]
    k64 = dot(p64, dot(ab, phi8, 1, 1)) * tmask_ref[...]
    ksend[...] = pick_right(k64, spread_ref[...].astype(BF16))
    pl.semaphore_wait(sem, len(PARTNERS))
    owner_start(ksend, krecv, sems, 0)

    get_load.wait()
    lb_v[pl.ds(NB - 8, 8), :] = jnp.zeros((8, RHS), F32)
    for i, j, parts in SPLIT:
        for inner, k, r, c in parts:
            (li_v if inner else lb_v)[pl.ds(r, c), :] = load_v[i, j, pl.ds(k, c), :]
    lb, li = lb_v[...], li_v[...]
    get_di.wait()
    start = dot6(pieces(di_v[...]), li)
    abi = pick_cols(ab, pi)
    c = lb - dot6(pieces(abi), start)
    cl = jnp.concatenate([c, lb], axis=1)
    swap_start(cl, pk, send, recv, sems, 18)
    gather_start(owner_finish(ksend, krecv, sems, 0), kplane, sems, 2)
    k0 = jnp.sum(li * start, axis=0, keepdims=True)
    p64 = pieces(p64)
    get_n.wait()
    border_rows(n_v, nrows)
    nbb = pieces(pick_cols(nrows[...], pb))
    asm = swap_finish(cl, pkt, send, recv, sems, 18)
    f = wt * asm[:, 0:RHS]
    hsend[0] = dot6(p64, f)
    owner_start(hsend.at[0], hrecv.at[0], sems, 4)
    gather_turn(kplane, kfull, sems, 2)
    w = dot6(nbb, f)
    gather_start(owner_finish(hsend.at[0], hrecv.at[0], sems, 4), gplane.at[0], sems, 5)
    gather_finish(kfull, sems, 2)

    build_coarse(kfull, kc)
    low = lax.broadcasted_iota(jnp.int32, (64, 128), 1) < 64
    for j in range(2):
        cut = pl.ds(128 * j, 128)
        xo[j] = jnp.where(low, kc[pl.ds(128 * j, 64), cut], kc[pl.ds(128 * j + 64, 64), cut])
    sweep(xo, 64)
    gather_turn(gplane.at[0], gfull.at[0], sems, 5)
    group = lax.broadcasted_iota(jnp.int32, (64, 256), 1) // 64
    both = jnp.concatenate([xo[0], xo[1]], axis=1)
    inv_o = jnp.concatenate([jnp.where(group == g, both, 0.0) for g in range(4)], axis=0)
    koe = kc[pl.ds(0, 256), pl.ds(256, 256)]
    m = dot(inv_o, koe)
    se = kc[pl.ds(256, 256), pl.ds(256, 256)] - dot(koe, m, 0, 0)
    x2[0] = jnp.where(low, se[0:64, 0:128], se[64:128, 0:128])
    sweep(x2, 64)
    inv_2 = jnp.concatenate([jnp.where(low, x2[0], 0.0), jnp.where(low, 0.0, x2[0])], axis=0)
    k2f = se[0:128, 128:256]
    m2 = dot(inv_2, k2f)
    xf[0] = se[128:256, 128:256] - dot(k2f, m2, 0, 0)
    sweep(xf, 128)
    prim = lax.broadcasted_iota(jnp.int32, (24, 512), 0)
    want = jnp.full((24, 512), -1, jnp.int32)
    for q, (t, o) in enumerate(PRIM):
        cx, cy, cz = at(o)
        want = jnp.where(prim == q, place(cz) * 64 + (cx * GY + cy) * 4 + t, want)
    sel = (want == lax.broadcasted_iota(jnp.int32, (24, 512), 1)).astype(F32)
    so = sel[:, 0:256]
    s_e = sel[:, 256:512] - dot(so, m)
    s_2 = s_e[:, 0:128]
    wf = dot(s_e[:, 128:256] - dot(s_2, m2), xf[0])
    w2 = dot(s_2, inv_2) - dot(wf, m2, 1, 1)
    we = jnp.concatenate([w2, wf], axis=1)
    w24 = jnp.concatenate([dot(so, inv_o) - dot(we, m, 1, 1), we], axis=1)

    def apply_coarse(w, g):
        return wt * (w + dot(p24, dot(w24, g), 0, 0))

    part = lambda a, b: jnp.sum(a * b, axis=0, keepdims=True)
    gather_finish(gfull.at[0], sems, 5)
    u = apply_coarse(w, gfull[0])
    swap_start(u, pk, ssend.at[0], srecv.at[0], sems, 20)
    x = dot(di_v[...], abi, 1, 1)
    s = pieces(pick_cols(ab, pb) - dot(abi, x))
    z1 = swap_finish(u, pkt, ssend.at[0], srecv.at[0], sems, 20)
    t1 = dot6(s, z1)
    swap_start(t1, pk, ssend.at[1], srecv.at[1], sems, 22)
    reduce_start(jnp.concatenate([k0, part(c, z1), part(z1, t1), jnp.zeros((5, RHS), F32)], axis=0), rplane.at[0], sems, 11)
    at1 = swap_finish(t1, pkt, ssend.at[1], srecv.at[1], sems, 22)
    f = wt * at1
    hsend[1] = dot6(p64, f)
    owner_start(hsend.at[1], hrecv.at[1], sems, 13)
    w = dot6(nbb, f)
    reduce_turn(rplane.at[0], rline.at[0], sems, 11)
    gather_start(owner_finish(hsend.at[1], hrecv.at[1], sems, 13), gplane.at[1], sems, 14)
    gather_turn(gplane.at[1], gfull.at[1], sems, 14)
    sums = reduce_finish(rline.at[0], sems, 11)
    k0s = sums[0:1]
    g0 = k0s + sums[1:2]
    s1 = g0 / (k0s + sums[2:3])
    gather_finish(gfull.at[1], sems, 14)
    u = apply_coarse(w, gfull[1])
    swap_start(u, pk, ssend.at[2], srecv.at[2], sems, 24)
    z2 = swap_finish(u, pkt, ssend.at[2], srecv.at[2], sems, 24)
    t2 = dot6(s, z2)
    swap_start(t2, pk, ssend.at[3], srecv.at[3], sems, 26)
    zp, tp, cp = z1 - s1 * z2, t1 - s1 * t2, c - s1 * t1
    reduce_start(jnp.concatenate([part(cp, zp), part(zp, tp), jnp.zeros((6, RHS), F32)], axis=0), rplane.at[1], sems, 16)
    xz = dot(x, jnp.concatenate([z1, zp], axis=1))
    at2 = swap_finish(t2, pkt, ssend.at[3], srecv.at[3], sems, 26)
    reduce_turn(rplane.at[1], rline.at[1], sems, 16)
    last = reduce_finish(rline.at[1], sems, 16)
    rest = 1.0 - s1
    g1 = rest * rest * k0s + last[0:1]
    beta = g1 / g0
    s2 = g1 / (rest * rest * k0s + last[1:2] - beta * g1 / s1)

    xb = s1 * z1 + s2 * (zp + beta * z1)
    xi = (s1 + s2 * (rest + beta)) * start - (s1 + s2 * beta) * xz[:, :RHS] - s2 * xz[:, RHS:]
    kappa = rest * (1.0 - s2) - s2 * beta
    ac = asm[:, 0:RHS]
    ae = asm[:, RHS : 2 * RHS] - ac
    rb = kappa * ae + (ac - s1 * at1) - s2 * ((at1 - s1 * at2) + beta * at1)
    parts_ref[pl.ds(AT[0], NB), :], parts_ref[pl.ds(AT[1], NI), :] = xb, xi
    parts_ref[pl.ds(AT[2], NB), :], parts_ref[pl.ds(AT[3], NI), :] = rb, kappa * li


AT = (0, NB, NB + 344, 2 * NB + 344)


def spread(parts_ref, sol_ref, res_ref):
    for i, j, parts in SPLIT:
        for inner, k, r, c in parts:
            there = pl.ds(k, c)
            sol_ref[i, j, there, :] = parts_ref[pl.ds(AT[inner] + r, c), :]
            res_ref[i, j, there, :] = parts_ref[pl.ds(AT[2 + inner] + r, c), :]


def local(load, a, di, n, phi):
    tables = [jnp.asarray(v) for v in (B_COL, I_COL, K_COL, K_COL.T, WEIGHT, S64, TMASK, SPREAD)]
    V = lambda *s: pltpu.VMEM(s, F32)
    shape = jax.ShapeDtypeStruct((M, M, M, RHS), F32)
    parts = pl.pallas_call(
        program,
        out_shape=jax.ShapeDtypeStruct((2 * NB + 688, RHS), F32),
        in_specs=[pl.BlockSpec(memory_space=pl.ANY)] * 5 + [VM] * len(tables),
        out_specs=VM,
        scratch_shapes=[
            V(M, M, M, RHS), V(NODES, NODES), V(NODES, NODES), V(NB, NODES), V(NB, NODES), V(NI, NI), V(20, NODES), V(NB, RHS), V(NI, RHS),
            V(NS, 2 * RHS), V(NS, 2 * RHS), V(4, NS, RHS), V(4, NS, RHS),
            V(64, 128), V(64, 128), V(2, 64, 128), V(2, 64, 128), V(16, 8, 128), V(2, 16, 8, 128), V(512, 128), V(2, 512, 128),
            V(2, 16, 8, 128), V(2, 8, 8, 128), V(512, 512), V(2, 64, 128), V(1, 64, 128), V(1, 128, 128),
            pltpu.SemaphoreType.DMA((56,)), pltpu.SemaphoreType.DMA((5,)),
        ],
        compiler_params=pltpu.CompilerParams(vmem_limit_bytes=60 * 2**20, collective_id=0, has_side_effects=True),
        name="program",
    )(load, a.reshape(NODES, 1, NODES), di.reshape(NI, 1, NI), n.reshape(NODES, 1, NODES), phi.reshape(20, 1, NODES), *tables)
    return tuple(pl.pallas_call(
        spread, out_shape=[shape, shape], in_specs=[VM], out_specs=[VM] * 2,
        compiler_params=pltpu.CompilerParams(vmem_limit_bytes=16 * 2**20), name="spread",
    )(parts))


def solution(mesh):
    spec4, spec5 = P("gx", "gy", "gz", None), P("gx", "gy", "gz", None, None)
    return jax.shard_map(
        local, mesh=mesh, in_specs=(spec4, spec5, spec5, spec5, spec5), out_specs=(spec4, spec4), check_vma=False
    )
```

```python
import functools

import jax
import jax.numpy as jnp
import numpy as np
from jax import lax
from jax.experimental import pallas as pl
from jax.experimental.pallas import tpu as pltpu
from jax.sharding import PartitionSpec as P

MESH = pl.DeviceIdType.MESH
F32, BF16 = jnp.float32, jnp.bfloat16
GX, GY, GZ = 4, 4, 8
M = 9
NODES, NB, NI, RHS = 729, 392, 343, 128
ORDER = (1, 3, 5, 7, 2, 6, 0, 4)
VM = pl.BlockSpec(memory_space=pltpu.VMEM)

_g = np.indices((M, M, M)).reshape(3, -1)
_rim = ((_g == 0) | (_g == M - 1)).sum(0)
B_IDS, I_IDS = np.where(_rim > 0)[0], np.where(_rim == 0)[0]
B_POS = {int(n): r for r, n in enumerate(B_IDS)}
I_POS = {int(n): r for r, n in enumerate(I_IDS)}


def one_hot(rows, cols, shape):
    out = np.zeros(shape, np.float32)
    out[rows, cols] = 1.0
    return out


B_COL = np.full((NB, 1), -1, np.int32)
B_COL[: len(B_IDS), 0] = B_IDS
I_COL = I_IDS.astype(np.int32)[:, None]
RUNS, _r = [], 0
while _r < len(B_IDS):
    _e = _r + 1
    while _e < len(B_IDS) and B_IDS[_e] == B_IDS[_e - 1] + 1:
        _e += 1
    RUNS.append((_r, int(B_IDS[_r]), _e - _r))
    _r = _e
WEIGHT = np.zeros((NB, 1), np.float32)
WEIGHT[: len(B_IDS), 0] = 1.0 / 2.0 ** _rim[B_IDS]
WEIGHT = np.broadcast_to(WEIGHT, (NB, RHS)).copy()

DIRS = sorted(
    ((x, y, z) for x in (-1, 0, 1) for y in (-1, 0, 1) for z in (-1, 0, 1) if (x, y, z) != (0, 0, 0)),
    key=lambda d: (sum(map(abs, d)), d),
)
SIZE = {1: 88, 2: 16, 3: 8}
OFFS, _at = {}, 0
for _d in DIRS:
    OFFS[_d] = (_at, SIZE[sum(map(abs, _d))])
    _at += OFFS[_d][1]
NS, NF = _at, 6 * SIZE[1]
K_COL = np.full((NS, 1), -1, np.int32)
for _d in DIRS:
    _sel = [[0] if v == -1 else [M - 1] if v == 1 else list(range(M)) for v in _d]
    for _r, (_i, _j, _k) in enumerate((i, j, k) for i in _sel[0] for j in _sel[1] for k in _sel[2]):
        K_COL[OFFS[_d][0] + _r, 0] = B_POS[(_i * M + _j) * M + _k]

CORNERS = [(x, y, z) for x in (0, 1) for y in (0, 1) for z in (0, 1)]
PRIM = [(0, o) for o in CORNERS]
PRIM += [(1, (0, y, z)) for y in (0, 1) for z in (0, 1)]
PRIM += [(2, (x, 0, z)) for x in (0, 1) for z in (0, 1)]
PRIM += [(3, (x, y, 0)) for x in (0, 1) for y in (0, 1)]
S64 = one_hot([CORNERS.index(o) * 8 + t for t, o in PRIM], np.arange(20), (64, 24))
TMASK = (np.arange(64)[:, None] // 8 == np.arange(192)[None, :] // 24).astype(np.float32)
SPREAD = np.zeros((192, 128), np.float32)
for _c, _o1 in enumerate(CORNERS):
    for _q, (_t, _o2) in enumerate(PRIM):
        _f = [b - a + 1 for a, b in zip(_o1, _o2)]
        SPREAD[_c * 24 + _q, _t * 27 + (_f[0] * 3 + _f[1]) * 3 + _f[2]] = 1.0


def dot(a, b, ca=1, cb=0):
    return lax.dot_general(
        a, b, (((ca,), (cb,)), ((), ())), precision=lax.Precision.HIGHEST, preferred_element_type=F32
    )


def pieces(x):
    h = x.astype(BF16)
    r = x - h.astype(F32)
    m = r.astype(BF16)
    return h, m, (r - m.astype(F32)).astype(BF16)


def mm(a, b, ca=1, cb=0):
    return lax.dot_general(a, b, (((ca,), (cb,)), ((), ())), preferred_element_type=F32)


def pick(sel, x):
    h, m, l = pieces(x)
    if x.shape[1] > 128:
        return mm(sel, h) + mm(sel, m) + mm(sel, l)
    n = x.shape[1]
    d = mm(sel, jnp.concatenate([h, m], axis=1))
    return d[:, :n] + d[:, n:] + mm(sel, l)


def pick_cols(x, sel):
    h, m, l = pieces(x)
    return mm(h, sel, 1, 1) + mm(m, sel, 1, 1) + mm(l, sel, 1, 1)


def dot6(a, b):
    b1, b2, b3 = pieces(b)
    n = b.shape[1]
    b12 = jnp.concatenate([b1, b2], axis=1)
    d = mm(a[1], b12) + mm(a[0], b12)
    return (mm(a[0], b3) + mm(a[2], b1)) + d[:, n:] + d[:, :n]


def pick_right(x, sel):
    h, m, l = pieces(x)
    return mm(h, sel) + mm(m, sel) + mm(l, sel)


def here():
    return lax.axis_index("gx"), lax.axis_index("gy"), lax.axis_index("gz")


def at(d):
    x, y, z = here()
    return (lax.rem(x + d[0] + GX, GX), lax.rem(y + d[1] + GY, GY), lax.rem(z + d[2] + GZ, GZ))


_ring = lambda v, n: min(v, n - v)
PLANE = sorted(
    ((x, y) for x in range(GX) for y in range(GY)), key=lambda d: -_ring(d[0], GX) - _ring(d[1], GY)
)


def everyone(act):
    x, y, z = here()
    rows = [(lax.rem(x + d[0], GX), lax.rem(y + d[1], GY)) for d in PLANE]

    def layer(i, carry):
        up = lax.rem(i, 2)
        there = lax.rem(z + 4 + (i // 2 + up) * (1 - 2 * up), GZ)
        for r in rows:
            act((r[0], r[1], there))
        return carry

    lax.fori_loop(0, GZ - 1, layer, 0)
    for r in rows[:-1]:
        act((r[0], r[1], z))


def copy_to(src, dst, sems, k, device):
    return pltpu.make_async_remote_copy(
        src_ref=src, dst_ref=dst, send_sem=sems.at[2 * k], recv_sem=sems.at[2 * k + 1], device_id=device, device_id_type=MESH
    )


def remote(src, dst, sems, k, d):
    return copy_to(src, dst, sems, k, at(d))


def exchange_start(send, recv, sems, k, faces):
    for d in reversed(DIRS):
        if (sum(map(abs, d)) == 1) == faces:
            o, n = OFFS[d]
            o2, _ = OFFS[tuple(-v for v in d)]
            remote(send.at[pl.ds(o, n)], recv.at[pl.ds(o2, n)], sems, k, d).start()


FACE_ROWS, REST_ROWS = pl.ds(0, NF), pl.ds(NF, NS - NF)


def swap_start(v, pk, send, recv, sems, k):
    send[REST_ROWS, :] = pick(pk[NF:], v)
    exchange_start(send, recv, sems, k + 1, False)
    send[FACE_ROWS, :] = pick(pk[:NF], v)
    exchange_start(send, recv, sems, k, True)


def swap_finish(v, pkt, send, recv, sems, k):
    bulk_wait(send.at[FACE_ROWS], recv.at[FACE_ROWS], sems, k)
    v = v + pick(pkt[:, :NF], recv[FACE_ROWS, :])
    bulk_wait(send.at[REST_ROWS], recv.at[REST_ROWS], sems, k + 1)
    return v + pick(pkt[:, NF:], recv[REST_ROWS, :])


def bulk_wait(send, recv, sems, k):
    c = remote(send, recv, sems, k, (1, 0, 0))
    c.wait_recv()
    c.wait_send()


def owner_start(send, recv, sems, k):
    for c, o in reversed(list(enumerate(CORNERS))):
        if c:
            remote(send.at[pl.ds(8 * c, 8)], recv.at[pl.ds(8 * c, 8)], sems, k, o).start()


def owner_finish(send, recv, sems, k):
    bulk_wait(send.at[pl.ds(8, 56)], recv.at[pl.ds(8, 56)], sems, k)
    out = send[pl.ds(0, 8), :]
    for c in range(1, 8):
        out = out + recv[pl.ds(8 * c, 8), :]
    return out


def place(z):
    h = z // 2
    return lax.rem(z, 2) * h + (1 - lax.rem(z, 2)) * (6 - 2 * lax.rem(h, 2) + h // 2)


def gather_start(val, full, sems, k):
    x, y, z = here()
    slot = place(z) * 16 + x * GY + y
    full[slot] = val
    everyone(lambda device: copy_to(full.at[slot], full.at[slot], sems, k, device).start())


def gather_finish(full, sems, k):
    rest = pl.ds(0, 127)
    bulk_wait(full.at[rest], full.at[rest], sems, k)
    return full[...]


SPLIT = []
for _i in range(M):
    for _j in range(M):
        _n = (_i * M + _j) * M
        if _i in (0, M - 1) or _j in (0, M - 1):
            SPLIT.append((_i, _j, [(False, 0, B_POS[_n], M)]))
        else:
            SPLIT.append((_i, _j, [(False, 0, B_POS[_n], 1), (True, 1, I_POS[_n + 1], M - 2), (False, M - 1, B_POS[_n + M - 1], 1)]))


def choose(ids_ref, n):
    ids = ids_ref[...]
    return (lax.broadcasted_iota(jnp.int32, (ids.shape[0], n), 1) == ids).astype(F32).astype(BF16)


def coords(m):
    pos = m >> 6
    c = jnp.where(pos < 4, 2 * pos + 1, jnp.where(pos < 6, 4 * pos - 14, 4 * pos - 24))
    return (m >> 4) & 3, (m >> 2) & 3, c, m & 3


def build_coarse(kall, kc):
    ra, rb, rc, _ = coords(lax.broadcasted_iota(jnp.int32, (512, 128), 0))
    for j in range(4):
        ca, cb, cc, ct = coords(lax.broadcasted_iota(jnp.int32, (1, 128), 1) + 128 * j)
        da, db, dc = (ca + 1 - ra) & 3, (cb + 1 - rb) & 3, (cc + 1 - rc) & 7
        hit = (da < 3) & (db < 3) & (dc < 3)
        slot = jnp.where(hit, ct * 27 + da * 9 + db * 3 + dc, 0)
        v = jnp.take_along_axis(kall, slot, axis=1, mode="promise_in_bounds")
        kc[:, pl.ds(128 * j, 128)] = jnp.where(hit, v, 0.0)


def sweep(ref, n):
    lane = lax.broadcasted_iota(jnp.int32, (n, 128), 1)
    base = lane // n * n
    take = lambda v, idx: jnp.take_along_axis(v, idx, axis=1, mode="promise_in_bounds")

    def body(i, carry):
        k = 4 * i
        idx = [base + (k + q) for q in range(4)]
        top = [v[0:8] for v in idx]
        stored = []
        for j in range(ref.shape[0]):
            x = ref[j]
            rows = [jnp.broadcast_to(ref[j, pl.ds(k + q, 1), :], (8, 128)) for q in range(4)]
            a, b, c = take(rows[0], top[0]), take(rows[0], top[1]), take(rows[1], top[1])
            e, f, g, h = take(rows[0], top[2]), take(rows[0], top[3]), take(rows[1], top[2]), take(rows[1], top[3])
            p, q, r = take(rows[2], top[2]), take(rows[2], top[3]), take(rows[3], top[3])
            cols = [take(x, v) for v in idx]
            d = 1.0 / (a * c - b * b)
            a, b, c = c * d, -b * d, a * d
            we, wf, wg, wh = a * e + b * g, a * f + b * h, b * e + c * g, b * f + c * h
            p, q, r = p - (e * we + g * wg), q - (e * wf + g * wh), r - (f * wf + h * wh)
            d = 1.0 / (p * r - q * q)
            p, q, r = r * d, -q * d, p * d
            ue, uf, ug, uh = we * p + wf * q, we * q + wf * r, wg * p + wh * q, wg * q + wh * r
            a, b, c = a + (ue * we + uf * wf), b + (ue * wg + uf * wh), c + (ug * wg + uh * wh)
            inv = [[a, b, -ue, -uf], [b, c, -ug, -uh], [-ue, -ug, p, q], [-uf, -uh, q, r]]
            on = [lane[0:8] == v for v in top]
            new = []
            for m in inv:
                v = (m[0] * rows[0] + m[1] * rows[1]) + (m[2] * rows[2] + m[3] * rows[3])
                for q in range(4):
                    v = jnp.where(on[q], m[q], v)
                new.append(v[0:1])
            left = jnp.where((lane >= idx[0]) & (lane <= idx[3]), 0.0, x)
            stored.append((left - (cols[0] * new[0] + cols[1] * new[1]) - (cols[2] * new[2] + cols[3] * new[3]), new))
        for j, (v, new) in enumerate(stored):
            ref[j] = v
            for q in range(4):
                ref[j, pl.ds(k + q, 1), :] = new[q]
        return carry

    lax.fori_loop(0, n // 4, body, 0)


def program(load_h, a_h, di_h, n_h, phi_h, bcol, icol, kcol, krow, wt_ref, s64_ref, tmask_ref, spread_ref,
            parts_ref,
            load_v, a_v, n_v, arows, nrows, di_v, phi_v, lb_v, li_v, send, recv, ssend, srecv,
            ksend, krecv, hsend, hrecv, kfull, gfull, sums1, sums2, kc, xo, x2, xf, mark, sems, dsems):
    sem = pltpu.get_barrier_semaphore()
    everyone(lambda device: pl.semaphore_signal(sem, inc=1, device_id=device, device_id_type=MESH))

    get_phi = pltpu.make_async_copy(phi_h.at[:, 0, :], phi_v, dsems.at[0])
    get_load = pltpu.make_async_copy(load_h, load_v, dsems.at[1])
    get_di = pltpu.make_async_copy(di_h.at[:, 0, :], di_v, dsems.at[2])
    get_phi.start()
    get_a = pltpu.make_async_copy(a_h.at[:, 0, :], a_v, dsems.at[3])
    get_n = pltpu.make_async_copy(n_h.at[:, 0, :], n_v, dsems.at[4])
    get_load.start()
    get_di.start()
    get_a.start()
    get_n.start()

    def border_rows(src, dst):
        dst[pl.ds(NB - 8, 8), :] = jnp.zeros((8, NODES), F32)
        for r, n, c in RUNS:
            dst[pl.ds(r, c), :] = src[pl.ds(n, c), :]

    def fence():
        def note(i, carry):
            mark[i] = jnp.zeros((8, 128), F32)
            return carry

        lax.fori_loop(0, 2, note, 0)

    pb, pi, pk = choose(bcol, NODES), choose(icol, NODES), choose(kcol, NB)
    pkt = (lax.broadcasted_iota(jnp.int32, (NB, NS), 0) == krow[...]).astype(F32).astype(BF16)
    wt = wt_ref[...]

    get_phi.wait()
    phi = jnp.concatenate([phi_v[...], jnp.zeros((4, NODES), F32)], axis=0)
    phi8 = jnp.concatenate([phi] * 8, axis=0)
    p24 = pick_cols(phi, pb)
    p64 = pick(s64_ref[...].astype(BF16), p24)
    get_load.wait()
    lb_v[pl.ds(NB - 8, 8), :] = jnp.zeros((8, RHS), F32)
    for i, j, parts in SPLIT:
        for inner, k, r, c in parts:
            (li_v if inner else lb_v)[pl.ds(r, c), :] = load_v[i, j, pl.ds(k, c), :]
    lb, li = lb_v[...], li_v[...]
    get_di.wait()
    start = dot6(pieces(di_v[...]), li)
    get_a.wait()
    border_rows(a_v, arows)
    ab = arows[...]
    k64 = dot(p64, dot(ab, phi8, 1, 1)) * tmask_ref[...]
    ksend[...] = pick_right(k64, spread_ref[...].astype(BF16))
    pl.semaphore_wait(sem, GX * GY * GZ - 1)
    owner_start(ksend, krecv, sems, 0)
    fence()

    abi = pick_cols(ab, pi)
    c = lb - dot6(pieces(abi), start)
    cl = jnp.concatenate([c, lb], axis=1)
    swap_start(cl, pk, send, recv, sems, 18)
    gather_start(owner_finish(ksend, krecv, sems, 0)[0:4], kfull, sems, 2)
    fence()
    k0 = jnp.sum(li * start, axis=0, keepdims=True)
    p64 = pieces(p64)
    get_n.wait()
    border_rows(n_v, nrows)
    nbb = pieces(pick_cols(nrows[...], pb))
    asm = swap_finish(cl, pkt, send, recv, sems, 18)
    f = wt * asm[:, 0:RHS]
    hsend[0] = dot6(p64, f)
    owner_start(hsend.at[0], hrecv.at[0], sems, 4)
    fence()
    w = dot6(nbb, f)
    build_coarse(gather_finish(kfull, sems, 2).reshape(512, 128), kc)
    low = lax.broadcasted_iota(jnp.int32, (64, 128), 1) < 64
    for j in range(2):
        cut = pl.ds(128 * j, 128)
        xo[j] = jnp.where(low, kc[pl.ds(128 * j, 64), cut], kc[pl.ds(128 * j + 64, 64), cut])
    sweep(xo, 64)
    gather_start(owner_finish(hsend.at[0], hrecv.at[0], sems, 4)[0:4], gfull.at[0], sems, 5)
    fence()
    group = lax.broadcasted_iota(jnp.int32, (64, 256), 1) // 64
    both = jnp.concatenate([xo[0], xo[1]], axis=1)
    inv_o = jnp.concatenate([jnp.where(group == g, both, 0.0) for g in range(4)], axis=0)
    koe = kc[pl.ds(0, 256), pl.ds(256, 256)]
    m = dot(inv_o, koe)
    se = kc[pl.ds(256, 256), pl.ds(256, 256)] - dot(koe, m, 0, 0)
    x2[0] = jnp.where(low, se[0:64, 0:128], se[64:128, 0:128])
    sweep(x2, 64)
    inv_2 = jnp.concatenate([jnp.where(low, x2[0], 0.0), jnp.where(low, 0.0, x2[0])], axis=0)
    k2f = se[0:128, 128:256]
    m2 = dot(inv_2, k2f)
    xf[0] = se[128:256, 128:256] - dot(k2f, m2, 0, 0)
    sweep(xf, 128)
    prim = lax.broadcasted_iota(jnp.int32, (24, 512), 0)
    want = jnp.full((24, 512), -1, jnp.int32)
    for q, (t, o) in enumerate(PRIM):
        cx, cy, cz = at(o)
        want = jnp.where(prim == q, place(cz) * 64 + (cx * GY + cy) * 4 + t, want)
    sel = (want == lax.broadcasted_iota(jnp.int32, (24, 512), 1)).astype(F32)
    so = sel[:, 0:256]
    s_e = sel[:, 256:512] - dot(so, m)
    s_2 = s_e[:, 0:128]
    wf = dot(s_e[:, 128:256] - dot(s_2, m2), xf[0])
    w2 = dot(s_2, inv_2) - dot(wf, m2, 1, 1)
    we = jnp.concatenate([w2, wf], axis=1)
    w24 = jnp.concatenate([dot(so, inv_o) - dot(we, m, 1, 1), we], axis=1)

    def long(v, axis, order):
        q = pieces(v)
        return jnp.concatenate([q[i] for i in order], axis=axis)

    p24t = wt[:, 0:1] * p24.T
    spots = long(p24t, 1, (0, 0, 0, 1, 1, 2))
    packed = mm(pk, spots).astype(BF16)

    def correct_start(w, wpk, g, send, recv, k):
        y = long(dot(w24, g), 0, (0, 1, 2, 0, 1, 0))
        send[REST_ROWS, :] = wpk[NF:] + mm(packed[NF:], y)
        exchange_start(send, recv, sems, k + 1, False)
        send[FACE_ROWS, :] = wpk[:NF] + mm(packed[:NF], y)
        exchange_start(send, recv, sems, k, True)
        return w + mm(spots, y)

    part = lambda a, b: jnp.sum(a * b, axis=0, keepdims=True)
    w = wt * w
    wpk = pick(pk, w)
    g = gather_finish(gfull.at[0], sems, 5).reshape(512, RHS)
    u = correct_start(w, wpk, g, ssend.at[0], srecv.at[0], 20)
    fence()
    x = dot(di_v[...], abi, 1, 1)
    s = pieces(pick_cols(ab, pb) - dot(abi, x))
    z1 = swap_finish(u, pkt, ssend.at[0], srecv.at[0], sems, 20)
    t1 = dot6(s, z1)
    swap_start(t1, pk, ssend.at[1], srecv.at[1], sems, 22)
    fence()
    gather_start(jnp.concatenate([k0, part(c, z1), part(z1, t1), jnp.zeros((1, RHS), F32)], axis=0), sums1, sems, 11)
    at1 = swap_finish(t1, pkt, ssend.at[1], srecv.at[1], sems, 22)
    f = wt * at1
    hsend[1] = dot6(p64, f)
    owner_start(hsend.at[1], hrecv.at[1], sems, 13)
    fence()
    w = wt * dot6(nbb, f)
    wpk = pick(pk, w)
    gather_start(owner_finish(hsend.at[1], hrecv.at[1], sems, 13)[0:4], gfull.at[1], sems, 14)
    fence()
    sums = jnp.sum(gather_finish(sums1, sems, 11), axis=0)
    k0s = sums[0:1]
    g0 = k0s + sums[1:2]
    s1 = g0 / (k0s + sums[2:3])
    g = gather_finish(gfull.at[1], sems, 14).reshape(512, RHS)
    u = correct_start(w, wpk, g, ssend.at[2], srecv.at[2], 24)
    z2 = swap_finish(u, pkt, ssend.at[2], srecv.at[2], sems, 24)
    t2 = dot6(s, z2)
    swap_start(t2, pk, ssend.at[3], srecv.at[3], sems, 26)
    fence()
    zp, tp, cp = z1 - s1 * z2, t1 - s1 * t2, c - s1 * t1
    gather_start(jnp.concatenate([part(cp, zp), part(zp, tp)], axis=0), sums2, sems, 16)
    fence()
    xz = dot(x, jnp.concatenate([z1, zp], axis=1))
    at2 = swap_finish(t2, pkt, ssend.at[3], srecv.at[3], sems, 26)
    last = jnp.sum(gather_finish(sums2, sems, 16), axis=0)
    rest = 1.0 - s1
    g1 = rest * rest * k0s + last[0:1]
    beta = g1 / g0
    s2 = g1 / (rest * rest * k0s + last[1:2] - beta * g1 / s1)

    xb = s1 * z1 + s2 * (zp + beta * z1)
    xi = (s1 + s2 * (rest + beta)) * start - (s1 + s2 * beta) * xz[:, :RHS] - s2 * xz[:, RHS:]
    kappa = rest * (1.0 - s2) - s2 * beta
    ac = asm[:, 0:RHS]
    ae = asm[:, RHS : 2 * RHS] - ac
    rb = kappa * ae + (ac - s1 * at1) - s2 * ((at1 - s1 * at2) + beta * at1)
    parts_ref[pl.ds(AT[0], NB), :], parts_ref[pl.ds(AT[1], NI), :] = xb, xi
    parts_ref[pl.ds(AT[2], NB), :], parts_ref[pl.ds(AT[3], NI), :] = rb, kappa * li


AT = (0, NB, NB + 344, 2 * NB + 344)


def spread(parts_ref, sol_ref, res_ref):
    for i, j, parts in SPLIT:
        for inner, k, r, c in parts:
            there = pl.ds(k, c)
            sol_ref[i, j, there, :] = parts_ref[pl.ds(AT[inner] + r, c), :]
            res_ref[i, j, there, :] = parts_ref[pl.ds(AT[2 + inner] + r, c), :]


def local(load, a, di, n, phi):
    tables = [jnp.asarray(v) for v in (B_COL, I_COL, K_COL, K_COL.T, WEIGHT, S64, TMASK, SPREAD)]
    V = lambda *s: pltpu.VMEM(s, F32)
    shape = jax.ShapeDtypeStruct((M, M, M, RHS), F32)
    parts = pl.pallas_call(
        program,
        out_shape=jax.ShapeDtypeStruct((2 * NB + 688, RHS), F32),
        in_specs=[pl.BlockSpec(memory_space=pl.ANY)] * 5 + [VM] * len(tables),
        out_specs=VM,
        scratch_shapes=[
            V(M, M, M, RHS), V(NODES, NODES), V(NODES, NODES), V(NB, NODES), V(NB, NODES), V(NI, NI), V(20, NODES), V(NB, RHS), V(NI, RHS),
            V(NS, 2 * RHS), V(NS, 2 * RHS), V(4, NS, RHS), V(4, NS, RHS),
            V(64, 128), V(64, 128), V(2, 64, 128), V(2, 64, 128), V(128, 4, 128), V(2, 128, 4, 128),
            V(128, 4, 128), V(128, 2, 128), V(512, 512), V(2, 64, 128), V(1, 64, 128), V(1, 128, 128), V(2, 8, 128),
            pltpu.SemaphoreType.DMA((56,)), pltpu.SemaphoreType.DMA((5,)),
        ],
        compiler_params=pltpu.CompilerParams(vmem_limit_bytes=60 * 2**20, collective_id=0, has_side_effects=True),
        name="program",
    )(load, a.reshape(NODES, 1, NODES), di.reshape(NI, 1, NI), n.reshape(NODES, 1, NODES), phi.reshape(20, 1, NODES), *tables)
    return tuple(pl.pallas_call(
        spread, out_shape=[shape, shape], in_specs=[VM], out_specs=[VM] * 2,
        compiler_params=pltpu.CompilerParams(vmem_limit_bytes=16 * 2**20), name="spread",
    )(parts))


def solution(mesh):
    spec4, spec5 = P("gx", "gy", "gz", None), P("gx", "gy", "gz", None, None)
    return jax.shard_map(
        local, mesh=mesh, in_specs=(spec4, spec5, spec5, spec5, spec5), out_specs=(spec4, spec4), check_vma=False
    )
```

```python
import functools

import jax
import jax.numpy as jnp
import numpy as np
from jax import lax
from jax.experimental import pallas as pl
from jax.experimental.pallas import tpu as pltpu
from jax.sharding import PartitionSpec as P

MESH = pl.DeviceIdType.MESH
F32, BF16 = jnp.float32, jnp.bfloat16
GX, GY, GZ = 4, 4, 8
M = 9
NODES, NB, NI, RHS = 729, 392, 343, 128
ORDER = (1, 3, 5, 7, 2, 6, 0, 4)
VM = pl.BlockSpec(memory_space=pltpu.VMEM)

_g = np.indices((M, M, M)).reshape(3, -1)
_rim = ((_g == 0) | (_g == M - 1)).sum(0)
B_IDS, I_IDS = np.where(_rim > 0)[0], np.where(_rim == 0)[0]
B_POS = {int(n): r for r, n in enumerate(B_IDS)}
I_POS = {int(n): r for r, n in enumerate(I_IDS)}


def one_hot(rows, cols, shape):
    out = np.zeros(shape, np.float32)
    out[rows, cols] = 1.0
    return out


B_COL = np.full((NB, 1), -1, np.int32)
B_COL[: len(B_IDS), 0] = B_IDS
I_COL = I_IDS.astype(np.int32)[:, None]
RUNS, _r = [], 0
while _r < len(B_IDS):
    _e = _r + 1
    while _e < len(B_IDS) and B_IDS[_e] == B_IDS[_e - 1] + 1:
        _e += 1
    RUNS.append((_r, int(B_IDS[_r]), _e - _r))
    _r = _e
WEIGHT = np.zeros((NB, 1), np.float32)
WEIGHT[: len(B_IDS), 0] = 1.0 / 2.0 ** _rim[B_IDS]
WEIGHT = np.broadcast_to(WEIGHT, (NB, RHS)).copy()

DIRS = sorted(
    ((x, y, z) for x in (-1, 0, 1) for y in (-1, 0, 1) for z in (-1, 0, 1) if (x, y, z) != (0, 0, 0)),
    key=lambda d: (sum(map(abs, d)), d),
)
SIZE = {1: 88, 2: 16, 3: 8}
OFFS, _at = {}, 0
for _d in DIRS:
    OFFS[_d] = (_at, SIZE[sum(map(abs, _d))])
    _at += OFFS[_d][1]
NS, NF = _at, 6 * SIZE[1]
K_COL = np.full((NS, 1), -1, np.int32)
for _d in DIRS:
    _sel = [[0] if v == -1 else [M - 1] if v == 1 else list(range(M)) for v in _d]
    for _r, (_i, _j, _k) in enumerate((i, j, k) for i in _sel[0] for j in _sel[1] for k in _sel[2]):
        K_COL[OFFS[_d][0] + _r, 0] = B_POS[(_i * M + _j) * M + _k]

CORNERS = [(x, y, z) for x in (0, 1) for y in (0, 1) for z in (0, 1)]
PRIM = [(0, o) for o in CORNERS]
PRIM += [(1, (0, y, z)) for y in (0, 1) for z in (0, 1)]
PRIM += [(2, (x, 0, z)) for x in (0, 1) for z in (0, 1)]
PRIM += [(3, (x, y, 0)) for x in (0, 1) for y in (0, 1)]
S64 = one_hot([CORNERS.index(o) * 8 + t for t, o in PRIM], np.arange(20), (64, 24))
TMASK = (np.arange(64)[:, None] // 8 == np.arange(192)[None, :] // 24).astype(np.float32)
SPREAD = np.zeros((192, 128), np.float32)
for _c, _o1 in enumerate(CORNERS):
    for _q, (_t, _o2) in enumerate(PRIM):
        _f = [b - a + 1 for a, b in zip(_o1, _o2)]
        SPREAD[_c * 24 + _q, _t * 27 + (_f[0] * 3 + _f[1]) * 3 + _f[2]] = 1.0


def dot(a, b, ca=1, cb=0):
    return lax.dot_general(
        a, b, (((ca,), (cb,)), ((), ())), precision=lax.Precision.HIGHEST, preferred_element_type=F32
    )


def pieces(x):
    h = x.astype(BF16)
    r = x - h.astype(F32)
    m = r.astype(BF16)
    return h, m, (r - m.astype(F32)).astype(BF16)


def mm(a, b, ca=1, cb=0):
    return lax.dot_general(a, b, (((ca,), (cb,)), ((), ())), preferred_element_type=F32)


def pick(sel, x):
    h, m, l = pieces(x)
    if x.shape[1] > 128:
        return mm(sel, h) + mm(sel, m) + mm(sel, l)
    n = x.shape[1]
    d = mm(sel, jnp.concatenate([h, m], axis=1))
    return d[:, :n] + d[:, n:] + mm(sel, l)


def pick_cols(x, sel):
    h, m, l = pieces(x)
    return mm(h, sel, 1, 1) + mm(m, sel, 1, 1) + mm(l, sel, 1, 1)


def dot6(a, b):
    b1, b2, b3 = pieces(b)
    n = b.shape[1]
    b12 = jnp.concatenate([b1, b2], axis=1)
    d = mm(a[1], b12) + mm(a[0], b12)
    return (mm(a[0], b3) + mm(a[2], b1)) + d[:, n:] + d[:, :n]


def pick_right(x, sel):
    h, m, l = pieces(x)
    return mm(h, sel) + mm(m, sel) + mm(l, sel)


def here():
    return lax.axis_index("gx"), lax.axis_index("gy"), lax.axis_index("gz")


def at(d):
    x, y, z = here()
    return (lax.rem(x + d[0] + GX, GX), lax.rem(y + d[1] + GY, GY), lax.rem(z + d[2] + GZ, GZ))


_ring = lambda v, n: min(v, n - v)
PLANE = sorted(
    ((x, y) for x in range(GX) for y in range(GY)), key=lambda d: -_ring(d[0], GX) - _ring(d[1], GY)
)


def everyone(act):
    x, y, z = here()
    rows = [(lax.rem(x + d[0], GX), lax.rem(y + d[1], GY)) for d in PLANE]

    def layer(i, carry):
        up = lax.rem(i, 2)
        there = lax.rem(z + 4 + (i // 2 + up) * (1 - 2 * up), GZ)
        for r in rows:
            act((r[0], r[1], there))
        return carry

    lax.fori_loop(0, GZ - 1, layer, 0)
    for r in rows[:-1]:
        act((r[0], r[1], z))


def copy_to(src, dst, sems, k, device):
    return pltpu.make_async_remote_copy(
        src_ref=src, dst_ref=dst, send_sem=sems.at[2 * k], recv_sem=sems.at[2 * k + 1], device_id=device, device_id_type=MESH
    )


def remote(src, dst, sems, k, d):
    return copy_to(src, dst, sems, k, at(d))


def exchange_start(send, recv, sems, k, faces):
    for d in reversed(DIRS):
        if (sum(map(abs, d)) == 1) == faces:
            o, n = OFFS[d]
            o2, _ = OFFS[tuple(-v for v in d)]
            remote(send.at[pl.ds(o, n)], recv.at[pl.ds(o2, n)], sems, k, d).start()


FACE_ROWS, REST_ROWS = pl.ds(0, NF), pl.ds(NF, NS - NF)


def swap_start(v, pk, send, recv, sems, k):
    send[REST_ROWS, :] = pick(pk[NF:], v)
    exchange_start(send, recv, sems, k + 1, False)
    send[FACE_ROWS, :] = pick(pk[:NF], v)
    exchange_start(send, recv, sems, k, True)


def swap_finish(v, pkt, send, recv, sems, k):
    bulk_wait(send.at[FACE_ROWS], recv.at[FACE_ROWS], sems, k)
    v = v + pick(pkt[:, :NF], recv[FACE_ROWS, :])
    bulk_wait(send.at[REST_ROWS], recv.at[REST_ROWS], sems, k + 1)
    return v + pick(pkt[:, NF:], recv[REST_ROWS, :])


def bulk_wait(send, recv, sems, k):
    c = remote(send, recv, sems, k, (1, 0, 0))
    c.wait_recv()
    c.wait_send()


def owner_start(send, recv, sems, k):
    for c, o in reversed(list(enumerate(CORNERS))):
        if c:
            remote(send.at[pl.ds(8 * c, 8)], recv.at[pl.ds(8 * c, 8)], sems, k, o).start()


def owner_finish(send, recv, sems, k):
    bulk_wait(send.at[pl.ds(8, 56)], recv.at[pl.ds(8, 56)], sems, k)
    out = send[pl.ds(0, 8), :]
    for c in range(1, 8):
        out = out + recv[pl.ds(8 * c, 8), :]
    return out


def place(z):
    h = z // 2
    return lax.rem(z, 2) * h + (1 - lax.rem(z, 2)) * (6 - 2 * lax.rem(h, 2) + h // 2)


def gather_start(val, full, sems, k):
    x, y, z = here()
    slot = place(z) * 16 + x * GY + y
    full[slot] = val
    everyone(lambda device: copy_to(full.at[slot], full.at[slot], sems, k, device).start())


def gather_finish(full, sems, k):
    rest = pl.ds(0, 127)
    bulk_wait(full.at[rest], full.at[rest], sems, k)
    return full[...]


SPLIT = []
for _i in range(M):
    for _j in range(M):
        _n = (_i * M + _j) * M
        if _i in (0, M - 1) or _j in (0, M - 1):
            SPLIT.append((_i, _j, [(False, 0, B_POS[_n], M)]))
        else:
            SPLIT.append((_i, _j, [(False, 0, B_POS[_n], 1), (True, 1, I_POS[_n + 1], M - 2), (False, M - 1, B_POS[_n + M - 1], 1)]))


def choose(ids_ref, n):
    ids = ids_ref[...]
    return (lax.broadcasted_iota(jnp.int32, (ids.shape[0], n), 1) == ids).astype(F32).astype(BF16)


def coords(m):
    pos = m >> 6
    c = jnp.where(pos < 4, 2 * pos + 1, jnp.where(pos < 6, 4 * pos - 14, 4 * pos - 24))
    return (m >> 4) & 3, (m >> 2) & 3, c, m & 3


def build_coarse(kall, kc):
    ra, rb, rc, _ = coords(lax.broadcasted_iota(jnp.int32, (512, 128), 0))
    for j in range(4):
        ca, cb, cc, ct = coords(lax.broadcasted_iota(jnp.int32, (1, 128), 1) + 128 * j)
        da, db, dc = (ca + 1 - ra) & 3, (cb + 1 - rb) & 3, (cc + 1 - rc) & 7
        hit = (da < 3) & (db < 3) & (dc < 3)
        slot = jnp.where(hit, ct * 27 + da * 9 + db * 3 + dc, 0)
        v = jnp.take_along_axis(kall, slot, axis=1, mode="promise_in_bounds")
        kc[:, pl.ds(128 * j, 128)] = jnp.where(hit, v, 0.0)


def sweep(ref, n):
    lane = lax.broadcasted_iota(jnp.int32, (n, 128), 1)
    base = lane // n * n
    take = lambda v, idx: jnp.take_along_axis(v, idx, axis=1, mode="promise_in_bounds")

    def body(i, carry):
        k = 4 * i
        idx = [base + (k + q) for q in range(4)]
        top = [v[0:8] for v in idx]
        stored = []
        for j in range(ref.shape[0]):
            x = ref[j]
            rows = [jnp.broadcast_to(ref[j, pl.ds(k + q, 1), :], (8, 128)) for q in range(4)]
            a, b, c = take(rows[0], top[0]), take(rows[0], top[1]), take(rows[1], top[1])
            e, f, g, h = take(rows[0], top[2]), take(rows[0], top[3]), take(rows[1], top[2]), take(rows[1], top[3])
            p, q, r = take(rows[2], top[2]), take(rows[2], top[3]), take(rows[3], top[3])
            cols = [take(x, v) for v in idx]
            d = 1.0 / (a * c - b * b)
            a, b, c = c * d, -b * d, a * d
            we, wf, wg, wh = a * e + b * g, a * f + b * h, b * e + c * g, b * f + c * h
            p, q, r = p - (e * we + g * wg), q - (e * wf + g * wh), r - (f * wf + h * wh)
            d = 1.0 / (p * r - q * q)
            p, q, r = r * d, -q * d, p * d
            ue, uf, ug, uh = we * p + wf * q, we * q + wf * r, wg * p + wh * q, wg * q + wh * r
            a, b, c = a + (ue * we + uf * wf), b + (ue * wg + uf * wh), c + (ug * wg + uh * wh)
            inv = [[a, b, -ue, -uf], [b, c, -ug, -uh], [-ue, -ug, p, q], [-uf, -uh, q, r]]
            on = [lane[0:8] == v for v in top]
            new = []
            for m in inv:
                v = (m[0] * rows[0] + m[1] * rows[1]) + (m[2] * rows[2] + m[3] * rows[3])
                for q in range(4):
                    v = jnp.where(on[q], m[q], v)
                new.append(v[0:1])
            left = jnp.where((lane >= idx[0]) & (lane <= idx[3]), 0.0, x)
            stored.append((left - (cols[0] * new[0] + cols[1] * new[1]) - (cols[2] * new[2] + cols[3] * new[3]), new))
        for j, (v, new) in enumerate(stored):
            ref[j] = v
            for q in range(4):
                ref[j, pl.ds(k + q, 1), :] = new[q]
        return carry

    lax.fori_loop(0, n // 4, body, 0)


def program(load_h, a_h, di_h, n_h, phi_h, bcol, icol, kcol, krow, wt_ref, s64_ref, tmask_ref, spread_ref,
            parts_ref,
            load_v, a_v, n_v, arows, nrows, di_v, phi_v, lb_v, li_v, send, recv, ssend, srecv,
            ksend, krecv, hsend, hrecv, kfull, gfull, sums1, sums2, kc, xo, x2, xf, mark, sems, dsems):

    get_phi = pltpu.make_async_copy(phi_h.at[:, 0, :], phi_v, dsems.at[0])
    get_load = pltpu.make_async_copy(load_h, load_v, dsems.at[1])
    get_di = pltpu.make_async_copy(di_h.at[:, 0, :], di_v, dsems.at[2])
    get_phi.start()
    get_a = pltpu.make_async_copy(a_h.at[:, 0, :], a_v, dsems.at[3])
    get_n = pltpu.make_async_copy(n_h.at[:, 0, :], n_v, dsems.at[4])
    get_load.start()
    get_di.start()
    get_a.start()
    get_n.start()
    sem = pltpu.get_barrier_semaphore()
    everyone(lambda device: pl.semaphore_signal(sem, inc=1, device_id=device, device_id_type=MESH))

    def border_rows(src, dst):
        dst[pl.ds(NB - 8, 8), :] = jnp.zeros((8, NODES), F32)
        for r, n, c in RUNS:
            dst[pl.ds(r, c), :] = src[pl.ds(n, c), :]

    def fence():
        def note(i, carry):
            mark[i] = jnp.zeros((8, 128), F32)
            return carry

        lax.fori_loop(0, 2, note, 0)

    pb, pi, pk = choose(bcol, NODES), choose(icol, NODES), choose(kcol, NB)
    pkt = (lax.broadcasted_iota(jnp.int32, (NB, NS), 0) == krow[...]).astype(F32).astype(BF16)
    wt = wt_ref[...]

    get_phi.wait()
    phi = jnp.concatenate([phi_v[...], jnp.zeros((4, NODES), F32)], axis=0)
    phi8 = jnp.concatenate([phi] * 8, axis=0)
    p24 = pick_cols(phi, pb)
    p64 = pick(s64_ref[...].astype(BF16), p24)
    get_load.wait()
    lb_v[pl.ds(NB - 8, 8), :] = jnp.zeros((8, RHS), F32)
    for i, j, parts in SPLIT:
        for inner, k, r, c in parts:
            (li_v if inner else lb_v)[pl.ds(r, c), :] = load_v[i, j, pl.ds(k, c), :]
    lb, li = lb_v[...], li_v[...]
    get_di.wait()
    start = dot6(pieces(di_v[...]), li)
    get_a.wait()
    border_rows(a_v, arows)
    ab = arows[...]
    k64 = dot(p64, dot(ab, phi8, 1, 1)) * tmask_ref[...]
    ksend[...] = pick_right(k64, spread_ref[...].astype(BF16))
    pl.semaphore_wait(sem, GX * GY * GZ - 1)
    owner_start(ksend, krecv, sems, 0)
    fence()

    abi = pick_cols(ab, pi)
    c = lb - dot6(pieces(abi), start)
    swap_start(c, pk, send.at[0], recv.at[0], sems, 18)
    gather_start(owner_finish(ksend, krecv, sems, 0)[0:4], kfull, sems, 2)
    fence()
    k0 = jnp.sum(li * start, axis=0, keepdims=True)
    p64 = pieces(p64)
    get_n.wait()
    border_rows(n_v, nrows)
    nbb = pieces(pick_cols(nrows[...], pb))
    ac = swap_finish(c, pkt, send.at[0], recv.at[0], sems, 18)
    f = wt * ac
    hsend[0] = dot6(p64, f)
    owner_start(hsend.at[0], hrecv.at[0], sems, 4)
    fence()
    w = wt * dot6(nbb, f)
    wpk = pick(pk, w)
    build_coarse(gather_finish(kfull, sems, 2).reshape(512, 128), kc)
    low = lax.broadcasted_iota(jnp.int32, (64, 128), 1) < 64
    for j in range(2):
        cut = pl.ds(128 * j, 128)
        xo[j] = jnp.where(low, kc[pl.ds(128 * j, 64), cut], kc[pl.ds(128 * j + 64, 64), cut])
    sweep(xo, 64)
    gather_start(owner_finish(hsend.at[0], hrecv.at[0], sems, 4)[0:4], gfull.at[0], sems, 5)
    fence()
    group = lax.broadcasted_iota(jnp.int32, (64, 256), 1) // 64
    both = jnp.concatenate([xo[0], xo[1]], axis=1)
    inv_o = jnp.concatenate([jnp.where(group == g, both, 0.0) for g in range(4)], axis=0)
    koe = kc[pl.ds(0, 256), pl.ds(256, 256)]
    m = dot(inv_o, koe)
    se = kc[pl.ds(256, 256), pl.ds(256, 256)] - dot(koe, m, 0, 0)
    x2[0] = jnp.where(low, se[0:64, 0:128], se[64:128, 0:128])
    sweep(x2, 64)
    inv_2 = jnp.concatenate([jnp.where(low, x2[0], 0.0), jnp.where(low, 0.0, x2[0])], axis=0)
    k2f = se[0:128, 128:256]
    m2 = dot(inv_2, k2f)
    xf[0] = se[128:256, 128:256] - dot(k2f, m2, 0, 0)
    sweep(xf, 128)
    prim = lax.broadcasted_iota(jnp.int32, (24, 512), 0)
    want = jnp.full((24, 512), -1, jnp.int32)
    for q, (t, o) in enumerate(PRIM):
        cx, cy, cz = at(o)
        want = jnp.where(prim == q, place(cz) * 64 + (cx * GY + cy) * 4 + t, want)
    sel = (want == lax.broadcasted_iota(jnp.int32, (24, 512), 1)).astype(F32)
    so = sel[:, 0:256]
    s_e = sel[:, 256:512] - dot(so, m)
    s_2 = s_e[:, 0:128]
    wf = dot(s_e[:, 128:256] - dot(s_2, m2), xf[0])
    w2 = dot(s_2, inv_2) - dot(wf, m2, 1, 1)
    we = jnp.concatenate([w2, wf], axis=1)
    w24 = jnp.concatenate([dot(so, inv_o) - dot(we, m, 1, 1), we], axis=1)

    def long(v, axis, order):
        q = pieces(v)
        return jnp.concatenate([q[i] for i in order], axis=axis)

    p24t = wt[:, 0:1] * p24.T
    spots = long(p24t, 1, (0, 0, 0, 1, 1, 2))
    packed = mm(pk, spots).astype(BF16)

    def correct_start(w, wpk, g, send, recv, k):
        y = long(dot(w24, g), 0, (0, 1, 2, 0, 1, 0))
        send[REST_ROWS, :] = wpk[NF:] + mm(packed[NF:], y)
        exchange_start(send, recv, sems, k + 1, False)
        send[FACE_ROWS, :] = wpk[:NF] + mm(packed[:NF], y)
        exchange_start(send, recv, sems, k, True)
        return w + mm(spots, y)

    part = lambda a, b: jnp.sum(a * b, axis=0, keepdims=True)
    g = gather_finish(gfull.at[0], sems, 5).reshape(512, RHS)
    u = correct_start(w, wpk, g, ssend.at[0], srecv.at[0], 20)
    fence()
    x = dot(di_v[...], abi, 1, 1)
    s = pieces(pick_cols(ab, pb) - dot(abi, x))
    z1 = swap_finish(u, pkt, ssend.at[0], srecv.at[0], sems, 20)
    t1 = dot6(s, z1)
    swap_start(t1, pk, ssend.at[1], srecv.at[1], sems, 22)
    fence()
    gather_start(jnp.concatenate([k0, part(c, z1), part(z1, t1), jnp.zeros((1, RHS), F32)], axis=0), sums1, sems, 11)
    at1 = swap_finish(t1, pkt, ssend.at[1], srecv.at[1], sems, 22)
    f = wt * at1
    hsend[1] = dot6(p64, f)
    owner_start(hsend.at[1], hrecv.at[1], sems, 13)
    fence()
    w = wt * dot6(nbb, f)
    wpk = pick(pk, w)
    gather_start(owner_finish(hsend.at[1], hrecv.at[1], sems, 13)[0:4], gfull.at[1], sems, 14)
    fence()
    swap_start(lb, pk, send.at[1], recv.at[1], sems, 28)
    sums = jnp.sum(gather_finish(sums1, sems, 11), axis=0)
    k0s = sums[0:1]
    g0 = k0s + sums[1:2]
    s1 = g0 / (k0s + sums[2:3])
    g = gather_finish(gfull.at[1], sems, 14).reshape(512, RHS)
    u = correct_start(w, wpk, g, ssend.at[2], srecv.at[2], 24)
    z2 = swap_finish(u, pkt, ssend.at[2], srecv.at[2], sems, 24)
    t2 = dot6(s, z2)
    zp, tp, cp = z1 - s1 * z2, t1 - s1 * t2, c - s1 * t1
    gather_start(jnp.concatenate([part(cp, zp), part(zp, tp)], axis=0), sums2, sems, 16)
    fence()
    swap_start(t2, pk, ssend.at[3], srecv.at[3], sems, 26)
    fence()
    al = swap_finish(lb, pkt, send.at[1], recv.at[1], sems, 28)
    xz = dot(x, jnp.concatenate([z1, zp], axis=1))
    at2 = swap_finish(t2, pkt, ssend.at[3], srecv.at[3], sems, 26)
    last = jnp.sum(gather_finish(sums2, sems, 16), axis=0)
    rest = 1.0 - s1
    g1 = rest * rest * k0s + last[0:1]
    beta = g1 / g0
    s2 = g1 / (rest * rest * k0s + last[1:2] - beta * g1 / s1)

    xb = s1 * z1 + s2 * (zp + beta * z1)
    xi = (s1 + s2 * (rest + beta)) * start - (s1 + s2 * beta) * xz[:, :RHS] - s2 * xz[:, RHS:]
    kappa = rest * (1.0 - s2) - s2 * beta
    ae = al - ac
    rb = kappa * ae + (ac - s1 * at1) - s2 * ((at1 - s1 * at2) + beta * at1)
    parts_ref[pl.ds(AT[0], NB), :], parts_ref[pl.ds(AT[1], NI), :] = xb, xi
    parts_ref[pl.ds(AT[2], NB), :], parts_ref[pl.ds(AT[3], NI), :] = rb, kappa * li


AT = (0, NB, NB + 344, 2 * NB + 344)


def spread(parts_ref, sol_ref, res_ref):
    for i, j, parts in SPLIT:
        for inner, k, r, c in parts:
            there = pl.ds(k, c)
            sol_ref[i, j, there, :] = parts_ref[pl.ds(AT[inner] + r, c), :]
            res_ref[i, j, there, :] = parts_ref[pl.ds(AT[2 + inner] + r, c), :]


def local(load, a, di, n, phi):
    tables = [jnp.asarray(v) for v in (B_COL, I_COL, K_COL, K_COL.T, WEIGHT, S64, TMASK, SPREAD)]
    V = lambda *s: pltpu.VMEM(s, F32)
    shape = jax.ShapeDtypeStruct((M, M, M, RHS), F32)
    parts = pl.pallas_call(
        program,
        out_shape=jax.ShapeDtypeStruct((2 * NB + 688, RHS), F32),
        in_specs=[pl.BlockSpec(memory_space=pl.ANY)] * 5 + [VM] * len(tables),
        out_specs=VM,
        scratch_shapes=[
            V(M, M, M, RHS), V(NODES, NODES), V(NODES, NODES), V(NB, NODES), V(NB, NODES), V(NI, NI), V(20, NODES), V(NB, RHS), V(NI, RHS),
            V(2, NS, RHS), V(2, NS, RHS), V(4, NS, RHS), V(4, NS, RHS),
            V(64, 128), V(64, 128), V(2, 64, 128), V(2, 64, 128), V(128, 4, 128), V(2, 128, 4, 128),
            V(128, 4, 128), V(128, 2, 128), V(512, 512), V(2, 64, 128), V(1, 64, 128), V(1, 128, 128), V(2, 8, 128),
            pltpu.SemaphoreType.DMA((60,)), pltpu.SemaphoreType.DMA((5,)),
        ],
        compiler_params=pltpu.CompilerParams(vmem_limit_bytes=60 * 2**20, collective_id=0, has_side_effects=True),
        name="program",
    )(load, a.reshape(NODES, 1, NODES), di.reshape(NI, 1, NI), n.reshape(NODES, 1, NODES), phi.reshape(20, 1, NODES), *tables)
    return tuple(pl.pallas_call(
        spread, out_shape=[shape, shape], in_specs=[VM], out_specs=[VM] * 2,
        compiler_params=pltpu.CompilerParams(vmem_limit_bytes=16 * 2**20), name="spread",
    )(parts))


def solution(mesh):
    spec4, spec5 = P("gx", "gy", "gz", None), P("gx", "gy", "gz", None, None)
    return jax.shard_map(
        local, mesh=mesh, in_specs=(spec4, spec5, spec5, spec5, spec5), out_specs=(spec4, spec4), check_vma=False
    )
```

```python
import functools

import jax
import jax.numpy as jnp
import numpy as np
from jax import lax
from jax.experimental import pallas as pl
from jax.experimental.pallas import tpu as pltpu
from jax.sharding import PartitionSpec as P

MESH = pl.DeviceIdType.MESH
F32, BF16 = jnp.float32, jnp.bfloat16
GX, GY, GZ = 4, 4, 8
M = 9
NODES, NB, NI, RHS = 729, 392, 343, 128
ORDER = (1, 3, 5, 7, 2, 6, 0, 4)
VM = pl.BlockSpec(memory_space=pltpu.VMEM)

_g = np.indices((M, M, M)).reshape(3, -1)
_rim = ((_g == 0) | (_g == M - 1)).sum(0)
B_IDS, I_IDS = np.where(_rim > 0)[0], np.where(_rim == 0)[0]
B_POS = {int(n): r for r, n in enumerate(B_IDS)}
I_POS = {int(n): r for r, n in enumerate(I_IDS)}


def one_hot(rows, cols, shape):
    out = np.zeros(shape, np.float32)
    out[rows, cols] = 1.0
    return out


B_COL = np.full((NB, 1), -1, np.int32)
B_COL[: len(B_IDS), 0] = B_IDS
NEAR_NODE = np.full((NB, 1), -1, np.int32)
NEAR = np.full((NB, 1), -1, np.int32)
for _r, _n in enumerate(B_IDS):
    if _rim[_n] == 1:
        _i, _j, _k = (min(max(int(v), 1), M - 2) for v in (_n // 81, _n // 9 % 9, _n % 9))
        NEAR_NODE[_r, 0] = (_i * M + _j) * M + _k
        NEAR[_r, 0] = I_POS[(_i * M + _j) * M + _k]
RUNS, _r = [], 0
while _r < len(B_IDS):
    _e = _r + 1
    while _e < len(B_IDS) and B_IDS[_e] == B_IDS[_e - 1] + 1:
        _e += 1
    RUNS.append((_r, int(B_IDS[_r]), _e - _r))
    _r = _e
WEIGHT = np.zeros((NB, 1), np.float32)
WEIGHT[: len(B_IDS), 0] = 1.0 / 2.0 ** _rim[B_IDS]
WEIGHT = np.broadcast_to(WEIGHT, (NB, RHS)).copy()

DIRS = sorted(
    ((x, y, z) for x in (-1, 0, 1) for y in (-1, 0, 1) for z in (-1, 0, 1) if (x, y, z) != (0, 0, 0)),
    key=lambda d: (sum(map(abs, d)), d),
)
SIZE = {1: 88, 2: 16, 3: 8}
OFFS, _at = {}, 0
for _d in DIRS:
    OFFS[_d] = (_at, SIZE[sum(map(abs, _d))])
    _at += OFFS[_d][1]
NS, NF = _at, 6 * SIZE[1]
K_COL = np.full((NS, 1), -1, np.int32)
for _d in DIRS:
    _sel = [[0] if v == -1 else [M - 1] if v == 1 else list(range(M)) for v in _d]
    for _r, (_i, _j, _k) in enumerate((i, j, k) for i in _sel[0] for j in _sel[1] for k in _sel[2]):
        K_COL[OFFS[_d][0] + _r, 0] = B_POS[(_i * M + _j) * M + _k]

CORNERS = [(x, y, z) for x in (0, 1) for y in (0, 1) for z in (0, 1)]
PRIM = [(0, o) for o in CORNERS]
PRIM += [(1, (0, y, z)) for y in (0, 1) for z in (0, 1)]
PRIM += [(2, (x, 0, z)) for x in (0, 1) for z in (0, 1)]
PRIM += [(3, (x, y, 0)) for x in (0, 1) for y in (0, 1)]
S64 = one_hot([CORNERS.index(o) * 8 + t for t, o in PRIM], np.arange(20), (64, 24))
TMASK = (np.arange(64)[:, None] // 8 == np.arange(192)[None, :] // 24).astype(np.float32)
SPREAD = np.zeros((192, 128), np.float32)
for _c, _o1 in enumerate(CORNERS):
    for _q, (_t, _o2) in enumerate(PRIM):
        _f = [b - a + 1 for a, b in zip(_o1, _o2)]
        SPREAD[_c * 24 + _q, _t * 27 + (_f[0] * 3 + _f[1]) * 3 + _f[2]] = 1.0


def dot(a, b, ca=1, cb=0):
    return lax.dot_general(
        a, b, (((ca,), (cb,)), ((), ())), precision=lax.Precision.HIGHEST, preferred_element_type=F32
    )


def pieces(x):
    h = x.astype(BF16)
    r = x - h.astype(F32)
    m = r.astype(BF16)
    return h, m, (r - m.astype(F32)).astype(BF16)


def mm(a, b, ca=1, cb=0):
    return lax.dot_general(a, b, (((ca,), (cb,)), ((), ())), preferred_element_type=F32)


def pick(sel, x):
    h, m, l = pieces(x)
    if x.shape[1] > 128:
        return mm(sel, h) + mm(sel, m) + mm(sel, l)
    n = x.shape[1]
    d = mm(sel, jnp.concatenate([h, m], axis=1))
    return d[:, :n] + d[:, n:] + mm(sel, l)


def pick_cols(x, sel):
    h, m, l = pieces(x)
    return mm(h, sel, 1, 1) + mm(m, sel, 1, 1) + mm(l, sel, 1, 1)


def dot6(a, b):
    b1, b2, b3 = pieces(b)
    n = b.shape[1]
    b12 = jnp.concatenate([b1, b2], axis=1)
    d = mm(a[1], b12) + mm(a[0], b12)
    return (mm(a[0], b3) + mm(a[2], b1)) + d[:, n:] + d[:, :n]


def pick_right(x, sel):
    h, m, l = pieces(x)
    return mm(h, sel) + mm(m, sel) + mm(l, sel)


def here():
    return lax.axis_index("gx"), lax.axis_index("gy"), lax.axis_index("gz")


def at(d):
    x, y, z = here()
    return (lax.rem(x + d[0] + GX, GX), lax.rem(y + d[1] + GY, GY), lax.rem(z + d[2] + GZ, GZ))


_ring = lambda v, n: min(v, n - v)
PLANE = sorted(
    ((x, y) for x in range(GX) for y in range(GY)), key=lambda d: -_ring(d[0], GX) - _ring(d[1], GY)
)


def everyone(act):
    x, y, z = here()
    rows = [(lax.rem(x + d[0], GX), lax.rem(y + d[1], GY)) for d in PLANE]

    def layer(i, carry):
        up = lax.rem(i, 2)
        there = lax.rem(z + 4 + (i // 2 + up) * (1 - 2 * up), GZ)
        for r in rows:
            act((r[0], r[1], there))
        return carry

    lax.fori_loop(0, GZ - 1, layer, 0)
    for r in rows[:-1]:
        act((r[0], r[1], z))


def copy_to(src, dst, sems, k, device):
    return pltpu.make_async_remote_copy(
        src_ref=src, dst_ref=dst, send_sem=sems.at[2 * k], recv_sem=sems.at[2 * k + 1], device_id=device, device_id_type=MESH
    )


def remote(src, dst, sems, k, d):
    return copy_to(src, dst, sems, k, at(d))


def exchange_start(send, recv, sems, k, faces):
    for d in reversed(DIRS):
        if (sum(map(abs, d)) == 1) == faces:
            o, n = OFFS[d]
            o2, _ = OFFS[tuple(-v for v in d)]
            remote(send.at[pl.ds(o, n)], recv.at[pl.ds(o2, n)], sems, k, d).start()


FACE_ROWS, REST_ROWS = pl.ds(0, NF), pl.ds(NF, NS - NF)


def swap_start(v, pk, send, recv, sems, k):
    send[REST_ROWS, :] = pick(pk[NF:], v)
    exchange_start(send, recv, sems, k + 1, False)
    send[FACE_ROWS, :] = pick(pk[:NF], v)
    exchange_start(send, recv, sems, k, True)


def swap_finish(v, pkt, send, recv, sems, k):
    bulk_wait(send.at[FACE_ROWS], recv.at[FACE_ROWS], sems, k)
    v = v + pick(pkt[:, :NF], recv[FACE_ROWS, :])
    bulk_wait(send.at[REST_ROWS], recv.at[REST_ROWS], sems, k + 1)
    return v + pick(pkt[:, NF:], recv[REST_ROWS, :])


def bulk_wait(send, recv, sems, k):
    c = remote(send, recv, sems, k, (1, 0, 0))
    c.wait_recv()
    c.wait_send()


def owner_start(send, recv, sems, k):
    for c, o in reversed(list(enumerate(CORNERS))):
        if c:
            remote(send.at[pl.ds(8 * c, 8)], recv.at[pl.ds(8 * c, 8)], sems, k, o).start()


def owner_finish(send, recv, sems, k):
    bulk_wait(send.at[pl.ds(8, 56)], recv.at[pl.ds(8, 56)], sems, k)
    out = send[pl.ds(0, 8), :]
    for c in range(1, 8):
        out = out + recv[pl.ds(8 * c, 8), :]
    return out


def place(z):
    h = z // 2
    return lax.rem(z, 2) * h + (1 - lax.rem(z, 2)) * (6 - 2 * lax.rem(h, 2) + h // 2)


def gather_start(val, full, sems, k):
    x, y, z = here()
    slot = place(z) * 16 + x * GY + y
    full[slot] = val
    everyone(lambda device: copy_to(full.at[slot], full.at[slot], sems, k, device).start())


def gather_finish(full, sems, k):
    rest = pl.ds(0, 127)
    bulk_wait(full.at[rest], full.at[rest], sems, k)
    return full[...]


SPLIT = []
for _i in range(M):
    for _j in range(M):
        _n = (_i * M + _j) * M
        if _i in (0, M - 1) or _j in (0, M - 1):
            SPLIT.append((_i, _j, [(False, 0, B_POS[_n], M)]))
        else:
            SPLIT.append((_i, _j, [(False, 0, B_POS[_n], 1), (True, 1, I_POS[_n + 1], M - 2), (False, M - 1, B_POS[_n + M - 1], 1)]))


def choose(ids_ref, n):
    ids = ids_ref[...]
    return (lax.broadcasted_iota(jnp.int32, (ids.shape[0], n), 1) == ids).astype(F32).astype(BF16)


def coords(m):
    pos = m >> 6
    c = jnp.where(pos < 4, 2 * pos + 1, jnp.where(pos < 6, 4 * pos - 14, 4 * pos - 24))
    return (m >> 4) & 3, (m >> 2) & 3, c, m & 3


def build_coarse(kall, kc):
    ra, rb, rc, _ = coords(lax.broadcasted_iota(jnp.int32, (512, 128), 0))
    for j in range(4):
        ca, cb, cc, ct = coords(lax.broadcasted_iota(jnp.int32, (1, 128), 1) + 128 * j)
        da, db, dc = (ca + 1 - ra) & 3, (cb + 1 - rb) & 3, (cc + 1 - rc) & 7
        hit = (da < 3) & (db < 3) & (dc < 3)
        slot = jnp.where(hit, ct * 27 + da * 9 + db * 3 + dc, 0)
        v = jnp.take_along_axis(kall, slot, axis=1, mode="promise_in_bounds")
        kc[:, pl.ds(128 * j, 128)] = jnp.where(hit, v, 0.0)


def sweep(ref, n):
    lane = lax.broadcasted_iota(jnp.int32, (n, 128), 1)
    base = lane // n * n
    take = lambda v, idx: jnp.take_along_axis(v, idx, axis=1, mode="promise_in_bounds")

    def body(i, carry):
        k = 4 * i
        idx = [base + (k + q) for q in range(4)]
        top = [v[0:8] for v in idx]
        stored = []
        for j in range(ref.shape[0]):
            x = ref[j]
            rows = [jnp.broadcast_to(ref[j, pl.ds(k + q, 1), :], (8, 128)) for q in range(4)]
            a, b, c = take(rows[0], top[0]), take(rows[0], top[1]), take(rows[1], top[1])
            e, f, g, h = take(rows[0], top[2]), take(rows[0], top[3]), take(rows[1], top[2]), take(rows[1], top[3])
            p, q, r = take(rows[2], top[2]), take(rows[2], top[3]), take(rows[3], top[3])
            cols = [take(x, v) for v in idx]
            d = 1.0 / (a * c - b * b)
            a, b, c = c * d, -b * d, a * d
            we, wf, wg, wh = a * e + b * g, a * f + b * h, b * e + c * g, b * f + c * h
            p, q, r = p - (e * we + g * wg), q - (e * wf + g * wh), r - (f * wf + h * wh)
            d = 1.0 / (p * r - q * q)
            p, q, r = r * d, -q * d, p * d
            ue, uf, ug, uh = we * p + wf * q, we * q + wf * r, wg * p + wh * q, wg * q + wh * r
            a, b, c = a + (ue * we + uf * wf), b + (ue * wg + uf * wh), c + (ug * wg + uh * wh)
            inv = [[a, b, -ue, -uf], [b, c, -ug, -uh], [-ue, -ug, p, q], [-uf, -uh, q, r]]
            on = [lane[0:8] == v for v in top]
            new = []
            for m in inv:
                v = (m[0] * rows[0] + m[1] * rows[1]) + (m[2] * rows[2] + m[3] * rows[3])
                for q in range(4):
                    v = jnp.where(on[q], m[q], v)
                new.append(v[0:1])
            left = jnp.where((lane >= idx[0]) & (lane <= idx[3]), 0.0, x)
            stored.append((left - (cols[0] * new[0] + cols[1] * new[1]) - (cols[2] * new[2] + cols[3] * new[3]), new))
        for j, (v, new) in enumerate(stored):
            ref[j] = v
            for q in range(4):
                ref[j, pl.ds(k + q, 1), :] = new[q]
        return carry

    lax.fori_loop(0, n // 4, body, 0)


def program(load_h, a_h, di_h, n_h, phi_h, bcol, nearnode, nearcol, kcol, krow, wt_ref, s64_ref, tmask_ref, spread_ref,
            parts_ref,
            load_v, a_v, n_v, arows, nrows, di_v, phi_v, lb_v, li_v, send, recv, ssend, srecv,
            ksend, krecv, hsend, hrecv, kfull, gfull, sums1, sums2, kc, xo, x2, xf, mark, sems, dsems):

    get_phi = pltpu.make_async_copy(phi_h.at[:, 0, :], phi_v, dsems.at[0])
    get_load = pltpu.make_async_copy(load_h, load_v, dsems.at[1])
    get_di = pltpu.make_async_copy(di_h.at[:, 0, :], di_v, dsems.at[2])
    get_phi.start()
    get_a = pltpu.make_async_copy(a_h.at[:, 0, :], a_v, dsems.at[3])
    get_n = pltpu.make_async_copy(n_h.at[:, 0, :], n_v, dsems.at[4])
    get_load.start()
    get_di.start()
    get_a.start()
    get_n.start()
    sem = pltpu.get_barrier_semaphore()
    everyone(lambda device: pl.semaphore_signal(sem, inc=1, device_id=device, device_id_type=MESH))

    def border_rows(src, dst):
        dst[pl.ds(NB - 8, 8), :] = jnp.zeros((8, NODES), F32)
        for r, n, c in RUNS:
            dst[pl.ds(r, c), :] = src[pl.ds(n, c), :]

    def fence():
        def note(i, carry):
            mark[i] = jnp.zeros((8, 128), F32)
            return carry

        lax.fori_loop(0, 2, note, 0)

    pb, near, pk = choose(bcol, NODES), choose(nearcol, NI), choose(kcol, NB)
    pkt = (lax.broadcasted_iota(jnp.int32, (NB, NS), 0) == krow[...]).astype(F32).astype(BF16)
    wt = wt_ref[...]

    get_phi.wait()
    phi = jnp.concatenate([phi_v[...], jnp.zeros((4, NODES), F32)], axis=0)
    phi8 = jnp.concatenate([phi] * 8, axis=0)
    p24 = pick_cols(phi, pb)
    p64 = pick(s64_ref[...].astype(BF16), p24)
    get_load.wait()
    lb_v[pl.ds(NB - 8, 8), :] = jnp.zeros((8, RHS), F32)
    for i, j, parts in SPLIT:
        for inner, k, r, c in parts:
            (li_v if inner else lb_v)[pl.ds(r, c), :] = load_v[i, j, pl.ds(k, c), :]
    lb, li = lb_v[...], li_v[...]
    get_di.wait()
    start = dot6(pieces(di_v[...]), li)
    get_a.wait()
    border_rows(a_v, arows)
    ab = arows[...]
    k64 = dot(p64, dot(ab, phi8, 1, 1)) * tmask_ref[...]
    ksend[...] = pick_right(k64, spread_ref[...].astype(BF16))
    pl.semaphore_wait(sem, GX * GY * GZ - 1)
    owner_start(ksend, krecv, sems, 0)
    fence()

    spot = lax.broadcasted_iota(jnp.int32, (NB, NODES), 1) == nearnode[...]
    tie = jnp.sum(jnp.where(spot, ab, 0.0), axis=1, keepdims=True)
    c = lb - tie * pick(near, start)
    swap_start(c, pk, send.at[0], recv.at[0], sems, 18)
    gather_start(owner_finish(ksend, krecv, sems, 0)[0:4], kfull, sems, 2)
    fence()
    k0 = jnp.sum(li * start, axis=0, keepdims=True)
    p64 = pieces(p64)
    get_n.wait()
    border_rows(n_v, nrows)
    nbb = pieces(pick_cols(nrows[...], pb))
    ac = swap_finish(c, pkt, send.at[0], recv.at[0], sems, 18)
    f = wt * ac
    hsend[0] = dot6(p64, f)
    owner_start(hsend.at[0], hrecv.at[0], sems, 4)
    fence()
    w = wt * dot6(nbb, f)
    wpk = pick(pk, w)
    build_coarse(gather_finish(kfull, sems, 2).reshape(512, 128), kc)
    low = lax.broadcasted_iota(jnp.int32, (64, 128), 1) < 64
    for j in range(2):
        cut = pl.ds(128 * j, 128)
        xo[j] = jnp.where(low, kc[pl.ds(128 * j, 64), cut], kc[pl.ds(128 * j + 64, 64), cut])
    sweep(xo, 64)
    gather_start(owner_finish(hsend.at[0], hrecv.at[0], sems, 4)[0:4], gfull.at[0], sems, 5)
    fence()
    group = lax.broadcasted_iota(jnp.int32, (64, 256), 1) // 64
    both = jnp.concatenate([xo[0], xo[1]], axis=1)
    inv_o = jnp.concatenate([jnp.where(group == g, both, 0.0) for g in range(4)], axis=0)
    koe = kc[pl.ds(0, 256), pl.ds(256, 256)]
    m = dot(inv_o, koe)
    se = kc[pl.ds(256, 256), pl.ds(256, 256)] - dot(koe, m, 0, 0)
    x2[0] = jnp.where(low, se[0:64, 0:128], se[64:128, 0:128])
    sweep(x2, 64)
    inv_2 = jnp.concatenate([jnp.where(low, x2[0], 0.0), jnp.where(low, 0.0, x2[0])], axis=0)
    k2f = se[0:128, 128:256]
    m2 = dot(inv_2, k2f)
    xf[0] = se[128:256, 128:256] - dot(k2f, m2, 0, 0)
    sweep(xf, 128)
    prim = lax.broadcasted_iota(jnp.int32, (24, 512), 0)
    want = jnp.full((24, 512), -1, jnp.int32)
    for q, (t, o) in enumerate(PRIM):
        cx, cy, cz = at(o)
        want = jnp.where(prim == q, place(cz) * 64 + (cx * GY + cy) * 4 + t, want)
    sel = (want == lax.broadcasted_iota(jnp.int32, (24, 512), 1)).astype(F32)
    so = sel[:, 0:256]
    s_e = sel[:, 256:512] - dot(so, m)
    s_2 = s_e[:, 0:128]
    wf = dot(s_e[:, 128:256] - dot(s_2, m2), xf[0])
    w2 = dot(s_2, inv_2) - dot(wf, m2, 1, 1)
    we = jnp.concatenate([w2, wf], axis=1)
    w24 = jnp.concatenate([dot(so, inv_o) - dot(we, m, 1, 1), we], axis=1)

    def long(v, axis, order):
        q = pieces(v)
        return jnp.concatenate([q[i] for i in order], axis=axis)

    p24t = wt[:, 0:1] * p24.T
    spots = long(p24t, 1, (0, 0, 0, 1, 1, 2))
    packed = mm(pk, spots).astype(BF16)

    def correct_start(w, wpk, g, send, recv, k):
        y = long(dot(w24, g), 0, (0, 1, 2, 0, 1, 0))
        send[REST_ROWS, :] = wpk[NF:] + mm(packed[NF:], y)
        exchange_start(send, recv, sems, k + 1, False)
        send[FACE_ROWS, :] = wpk[:NF] + mm(packed[:NF], y)
        exchange_start(send, recv, sems, k, True)
        return w + mm(spots, y)

    part = lambda a, b: jnp.sum(a * b, axis=0, keepdims=True)
    g = gather_finish(gfull.at[0], sems, 5).reshape(512, RHS)
    u = correct_start(w, wpk, g, ssend.at[0], srecv.at[0], 20)
    fence()
    x = pick_cols(di_v[...], near) * jnp.broadcast_to(tie, (NB, 128)).T[0:1, :]
    s = pieces(pick_cols(ab, pb) - tie * pick(near, x))
    z1 = swap_finish(u, pkt, ssend.at[0], srecv.at[0], sems, 20)
    t1 = dot6(s, z1)
    swap_start(t1, pk, ssend.at[1], srecv.at[1], sems, 22)
    fence()
    gather_start(jnp.concatenate([k0, part(c, z1), part(z1, t1), jnp.zeros((1, RHS), F32)], axis=0), sums1, sems, 11)
    at1 = swap_finish(t1, pkt, ssend.at[1], srecv.at[1], sems, 22)
    f = wt * at1
    hsend[1] = dot6(p64, f)
    owner_start(hsend.at[1], hrecv.at[1], sems, 13)
    fence()
    w = wt * dot6(nbb, f)
    wpk = pick(pk, w)
    gather_start(owner_finish(hsend.at[1], hrecv.at[1], sems, 13)[0:4], gfull.at[1], sems, 14)
    fence()
    swap_start(lb, pk, send.at[1], recv.at[1], sems, 28)
    sums = jnp.sum(gather_finish(sums1, sems, 11), axis=0)
    k0s = sums[0:1]
    g0 = k0s + sums[1:2]
    s1 = g0 / (k0s + sums[2:3])
    g = gather_finish(gfull.at[1], sems, 14).reshape(512, RHS)
    u = correct_start(w, wpk, g, ssend.at[2], srecv.at[2], 24)
    z2 = swap_finish(u, pkt, ssend.at[2], srecv.at[2], sems, 24)
    t2 = dot6(s, z2)
    zp, tp, cp = z1 - s1 * z2, t1 - s1 * t2, c - s1 * t1
    gather_start(jnp.concatenate([part(cp, zp), part(zp, tp)], axis=0), sums2, sems, 16)
    fence()
    swap_start(t2, pk, ssend.at[3], srecv.at[3], sems, 26)
    fence()
    al = swap_finish(lb, pkt, send.at[1], recv.at[1], sems, 28)
    x1, x2_, _ = pieces(x)
    both1, both2, _ = pieces(jnp.concatenate([z1, zp], axis=1))
    xz = mm(x1, both1) + (mm(x1, both2) + mm(x2_, both1))
    at2 = swap_finish(t2, pkt, ssend.at[3], srecv.at[3], sems, 26)
    last = jnp.sum(gather_finish(sums2, sems, 16), axis=0)
    rest = 1.0 - s1
    g1 = rest * rest * k0s + last[0:1]
    beta = g1 / g0
    s2 = g1 / (rest * rest * k0s + last[1:2] - beta * g1 / s1)

    xb = s1 * z1 + s2 * (zp + beta * z1)
    xi = (s1 + s2 * (rest + beta)) * start - (s1 + s2 * beta) * xz[:, :RHS] - s2 * xz[:, RHS:]
    kappa = rest * (1.0 - s2) - s2 * beta
    ae = al - ac
    rb = kappa * ae + (ac - s1 * at1) - s2 * ((at1 - s1 * at2) + beta * at1)
    parts_ref[pl.ds(AT[0], NB), :], parts_ref[pl.ds(AT[1], NI), :] = xb, xi
    parts_ref[pl.ds(AT[2], NB), :], parts_ref[pl.ds(AT[3], NI), :] = rb, kappa * li


AT = (0, NB, NB + 344, 2 * NB + 344)


def spread(parts_ref, sol_ref, res_ref):
    for i, j, parts in SPLIT:
        for inner, k, r, c in parts:
            there = pl.ds(k, c)
            sol_ref[i, j, there, :] = parts_ref[pl.ds(AT[inner] + r, c), :]
            res_ref[i, j, there, :] = parts_ref[pl.ds(AT[2 + inner] + r, c), :]


def local(load, a, di, n, phi):
    tables = [jnp.asarray(v) for v in (B_COL, NEAR_NODE, NEAR, K_COL, K_COL.T, WEIGHT, S64, TMASK, SPREAD)]
    V = lambda *s: pltpu.VMEM(s, F32)
    shape = jax.ShapeDtypeStruct((M, M, M, RHS), F32)
    parts = pl.pallas_call(
        program,
        out_shape=jax.ShapeDtypeStruct((2 * NB + 688, RHS), F32),
        in_specs=[pl.BlockSpec(memory_space=pl.ANY)] * 5 + [VM] * len(tables),
        out_specs=VM,
        scratch_shapes=[
            V(M, M, M, RHS), V(NODES, NODES), V(NODES, NODES), V(NB, NODES), V(NB, NODES), V(NI, NI), V(20, NODES), V(NB, RHS), V(NI, RHS),
            V(2, NS, RHS), V(2, NS, RHS), V(4, NS, RHS), V(4, NS, RHS),
            V(64, 128), V(64, 128), V(2, 64, 128), V(2, 64, 128), V(128, 4, 128), V(2, 128, 4, 128),
            V(128, 4, 128), V(128, 2, 128), V(512, 512), V(2, 64, 128), V(1, 64, 128), V(1, 128, 128), V(2, 8, 128),
            pltpu.SemaphoreType.DMA((60,)), pltpu.SemaphoreType.DMA((5,)),
        ],
        compiler_params=pltpu.CompilerParams(vmem_limit_bytes=60 * 2**20, collective_id=0, has_side_effects=True),
        name="program",
    )(load, a.reshape(NODES, 1, NODES), di.reshape(NI, 1, NI), n.reshape(NODES, 1, NODES), phi.reshape(20, 1, NODES), *tables)
    return tuple(pl.pallas_call(
        spread, out_shape=[shape, shape], in_specs=[VM], out_specs=[VM] * 2,
        compiler_params=pltpu.CompilerParams(vmem_limit_bytes=16 * 2**20), name="spread",
    )(parts))


def solution(mesh):
    spec4, spec5 = P("gx", "gy", "gz", None), P("gx", "gy", "gz", None, None)
    return jax.shard_map(
        local, mesh=mesh, in_specs=(spec4, spec5, spec5, spec5, spec5), out_specs=(spec4, spec4), check_vma=False
    )
```

```python
import functools

import jax
import jax.numpy as jnp
import numpy as np
from jax import lax
from jax.experimental import pallas as pl
from jax.experimental.pallas import tpu as pltpu
from jax.sharding import PartitionSpec as P

MESH = pl.DeviceIdType.MESH
F32, BF16 = jnp.float32, jnp.bfloat16
GX, GY, GZ = 4, 4, 8
M = 9
NODES, NB, NI, RHS = 729, 392, 343, 128
ORDER = (1, 3, 5, 7, 2, 6, 0, 4)
VM = pl.BlockSpec(memory_space=pltpu.VMEM)

_g = np.indices((M, M, M)).reshape(3, -1)
_rim = ((_g == 0) | (_g == M - 1)).sum(0)
B_IDS, I_IDS = np.where(_rim > 0)[0], np.where(_rim == 0)[0]
B_POS = {int(n): r for r, n in enumerate(B_IDS)}
I_POS = {int(n): r for r, n in enumerate(I_IDS)}


def one_hot(rows, cols, shape):
    out = np.zeros(shape, np.float32)
    out[rows, cols] = 1.0
    return out


B_COL = np.full((NB, 1), -1, np.int32)
B_COL[: len(B_IDS), 0] = B_IDS
NEAR_NODE = np.full((NB, 1), -1, np.int32)
NEAR = np.full((NB, 1), -1, np.int32)
for _r, _n in enumerate(B_IDS):
    if _rim[_n] == 1:
        _i, _j, _k = (min(max(int(v), 1), M - 2) for v in (_n // 81, _n // 9 % 9, _n % 9))
        NEAR_NODE[_r, 0] = (_i * M + _j) * M + _k
        NEAR[_r, 0] = I_POS[(_i * M + _j) * M + _k]
RUNS, _r = [], 0
while _r < len(B_IDS):
    _e = _r + 1
    while _e < len(B_IDS) and B_IDS[_e] == B_IDS[_e - 1] + 1:
        _e += 1
    RUNS.append((_r, int(B_IDS[_r]), _e - _r))
    _r = _e
WEIGHT = np.zeros((NB, 1), np.float32)
WEIGHT[: len(B_IDS), 0] = 1.0 / 2.0 ** _rim[B_IDS]
WEIGHT = np.broadcast_to(WEIGHT, (NB, RHS)).copy()

DIRS = sorted(
    ((x, y, z) for x in (-1, 0, 1) for y in (-1, 0, 1) for z in (-1, 0, 1) if (x, y, z) != (0, 0, 0)),
    key=lambda d: (sum(map(abs, d)), d),
)
SIZE = {1: 88, 2: 16, 3: 8}
OFFS, _at = {}, 0
for _d in DIRS:
    OFFS[_d] = (_at, SIZE[sum(map(abs, _d))])
    _at += OFFS[_d][1]
NS, NF = _at, 6 * SIZE[1]
K_COL = np.full((NS, 1), -1, np.int32)
for _d in DIRS:
    _sel = [[0] if v == -1 else [M - 1] if v == 1 else list(range(M)) for v in _d]
    for _r, (_i, _j, _k) in enumerate((i, j, k) for i in _sel[0] for j in _sel[1] for k in _sel[2]):
        K_COL[OFFS[_d][0] + _r, 0] = B_POS[(_i * M + _j) * M + _k]

CORNERS = [(x, y, z) for x in (0, 1) for y in (0, 1) for z in (0, 1)]
PRIM = [(0, o) for o in CORNERS]
PRIM += [(1, (0, y, z)) for y in (0, 1) for z in (0, 1)]
PRIM += [(2, (x, 0, z)) for x in (0, 1) for z in (0, 1)]
PRIM += [(3, (x, y, 0)) for x in (0, 1) for y in (0, 1)]
S64 = one_hot([CORNERS.index(o) * 8 + t for t, o in PRIM], np.arange(20), (64, 24))
TMASK = (np.arange(64)[:, None] // 8 == np.arange(192)[None, :] // 24).astype(np.float32)
SPREAD = np.zeros((192, 128), np.float32)
for _c, _o1 in enumerate(CORNERS):
    for _q, (_t, _o2) in enumerate(PRIM):
        _f = [b - a + 1 for a, b in zip(_o1, _o2)]
        SPREAD[_c * 24 + _q, _t * 27 + (_f[0] * 3 + _f[1]) * 3 + _f[2]] = 1.0


def dot(a, b, ca=1, cb=0):
    return lax.dot_general(
        a, b, (((ca,), (cb,)), ((), ())), precision=lax.Precision.HIGHEST, preferred_element_type=F32
    )


def pieces(x):
    h = x.astype(BF16)
    r = x - h.astype(F32)
    m = r.astype(BF16)
    return h, m, (r - m.astype(F32)).astype(BF16)


def mm(a, b, ca=1, cb=0):
    return lax.dot_general(a, b, (((ca,), (cb,)), ((), ())), preferred_element_type=F32)


def pick(sel, x):
    h, m, l = pieces(x)
    if x.shape[1] > 128:
        return mm(sel, h) + mm(sel, m) + mm(sel, l)
    n = x.shape[1]
    d = mm(sel, jnp.concatenate([h, m], axis=1))
    return d[:, :n] + d[:, n:] + mm(sel, l)


def pick_cols(x, sel):
    h, m, l = pieces(x)
    return mm(h, sel, 1, 1) + mm(m, sel, 1, 1) + mm(l, sel, 1, 1)


def dot6(a, b):
    b1, b2, b3 = pieces(b)
    n = b.shape[1]
    b12 = jnp.concatenate([b1, b2], axis=1)
    d = mm(a[1], b12) + mm(a[0], b12)
    return (mm(a[0], b3) + mm(a[2], b1)) + d[:, n:] + d[:, :n]


def pick_right(x, sel):
    h, m, l = pieces(x)
    return mm(h, sel) + mm(m, sel) + mm(l, sel)


def here():
    return lax.axis_index("gx"), lax.axis_index("gy"), lax.axis_index("gz")


def at(d):
    x, y, z = here()
    return (lax.rem(x + d[0] + GX, GX), lax.rem(y + d[1] + GY, GY), lax.rem(z + d[2] + GZ, GZ))


_ring = lambda v, n: min(v, n - v)
PLANE = sorted(
    ((x, y) for x in range(GX) for y in range(GY)), key=lambda d: -_ring(d[0], GX) - _ring(d[1], GY)
)


def everyone(act):
    x, y, z = here()
    rows = [(lax.rem(x + d[0], GX), lax.rem(y + d[1], GY)) for d in PLANE]

    def layer(i, carry):
        up = lax.rem(i, 2)
        there = lax.rem(z + 4 + (i // 2 + up) * (1 - 2 * up), GZ)
        for r in rows:
            act((r[0], r[1], there))
        return carry

    lax.fori_loop(0, GZ - 1, layer, 0)
    for r in rows[:-1]:
        act((r[0], r[1], z))


def copy_to(src, dst, sems, k, device):
    return pltpu.make_async_remote_copy(
        src_ref=src, dst_ref=dst, send_sem=sems.at[2 * k], recv_sem=sems.at[2 * k + 1], device_id=device, device_id_type=MESH
    )


def remote(src, dst, sems, k, d):
    return copy_to(src, dst, sems, k, at(d))


def exchange_start(send, recv, sems, k, faces):
    for d in reversed(DIRS):
        if (sum(map(abs, d)) == 1) == faces:
            o, n = OFFS[d]
            o2, _ = OFFS[tuple(-v for v in d)]
            remote(send.at[pl.ds(o, n)], recv.at[pl.ds(o2, n)], sems, k, d).start()


FACE_ROWS, REST_ROWS = pl.ds(0, NF), pl.ds(NF, NS - NF)


def swap_start(v, pk, send, recv, sems, k):
    send[REST_ROWS, :] = pick(pk[NF:], v)
    exchange_start(send, recv, sems, k + 1, False)
    send[FACE_ROWS, :] = pick(pk[:NF], v)
    exchange_start(send, recv, sems, k, True)


def swap_finish(v, pkt, send, recv, sems, k):
    bulk_wait(send.at[FACE_ROWS], recv.at[FACE_ROWS], sems, k)
    v = v + pick(pkt[:, :NF], recv[FACE_ROWS, :])
    bulk_wait(send.at[REST_ROWS], recv.at[REST_ROWS], sems, k + 1)
    return v + pick(pkt[:, NF:], recv[REST_ROWS, :])


def bulk_wait(send, recv, sems, k):
    c = remote(send, recv, sems, k, (1, 0, 0))
    c.wait_recv()
    c.wait_send()


def owner_start(send, recv, sems, k):
    for c, o in reversed(list(enumerate(CORNERS))):
        if c:
            remote(send.at[pl.ds(8 * c, 8)], recv.at[pl.ds(8 * c, 8)], sems, k, o).start()


def owner_finish(send, recv, sems, k):
    bulk_wait(send.at[pl.ds(8, 56)], recv.at[pl.ds(8, 56)], sems, k)
    out = send[pl.ds(0, 8), :]
    for c in range(1, 8):
        out = out + recv[pl.ds(8 * c, 8), :]
    return out


def place(z):
    h = z // 2
    return lax.rem(z, 2) * h + (1 - lax.rem(z, 2)) * (6 - 2 * lax.rem(h, 2) + h // 2)


def gather_start(val, full, sems, k):
    x, y, z = here()
    slot = place(z) * 16 + x * GY + y
    full[slot] = val
    everyone(lambda device: copy_to(full.at[slot], full.at[slot], sems, k, device).start())


def gather_finish(full, sems, k):
    rest = pl.ds(0, 127)
    bulk_wait(full.at[rest], full.at[rest], sems, k)
    return full[...]


SPLIT = []
for _i in range(M):
    for _j in range(M):
        _n = (_i * M + _j) * M
        if _i in (0, M - 1) or _j in (0, M - 1):
            SPLIT.append((_i, _j, [(False, 0, B_POS[_n], M)]))
        else:
            SPLIT.append((_i, _j, [(False, 0, B_POS[_n], 1), (True, 1, I_POS[_n + 1], M - 2), (False, M - 1, B_POS[_n + M - 1], 1)]))


def choose(ids_ref, n):
    ids = ids_ref[...]
    return (lax.broadcasted_iota(jnp.int32, (ids.shape[0], n), 1) == ids).astype(F32).astype(BF16)


def coords(m):
    pos = m >> 6
    c = jnp.where(pos < 4, 2 * pos + 1, jnp.where(pos < 6, 4 * pos - 14, 4 * pos - 24))
    return (m >> 4) & 3, (m >> 2) & 3, c, m & 3


def build_coarse(kall, kc):
    ra, rb, rc, _ = coords(lax.broadcasted_iota(jnp.int32, (512, 128), 0))
    for j in range(4):
        ca, cb, cc, ct = coords(lax.broadcasted_iota(jnp.int32, (1, 128), 1) + 128 * j)
        da, db, dc = (ca + 1 - ra) & 3, (cb + 1 - rb) & 3, (cc + 1 - rc) & 7
        hit = (da < 3) & (db < 3) & (dc < 3)
        slot = jnp.where(hit, ct * 27 + da * 9 + db * 3 + dc, 0)
        v = jnp.take_along_axis(kall, slot, axis=1, mode="promise_in_bounds")
        kc[:, pl.ds(128 * j, 128)] = jnp.where(hit, v, 0.0)


def sweep(ref, n):
    lane = lax.broadcasted_iota(jnp.int32, (n, 128), 1)
    base = lane // n * n
    take = lambda v, idx: jnp.take_along_axis(v, idx, axis=1, mode="promise_in_bounds")

    def body(i, carry):
        k = 4 * i
        idx = [base + (k + q) for q in range(4)]
        top = [v[0:8] for v in idx]
        stored = []
        for j in range(ref.shape[0]):
            x = ref[j]
            rows = [jnp.broadcast_to(ref[j, pl.ds(k + q, 1), :], (8, 128)) for q in range(4)]
            a, b, c = take(rows[0], top[0]), take(rows[0], top[1]), take(rows[1], top[1])
            e, f, g, h = take(rows[0], top[2]), take(rows[0], top[3]), take(rows[1], top[2]), take(rows[1], top[3])
            p, q, r = take(rows[2], top[2]), take(rows[2], top[3]), take(rows[3], top[3])
            cols = [take(x, v) for v in idx]
            s0, s1, s2 = a * c - b * b, a * g - b * e, a * h - b * f
            s3, s4, s5 = b * g - c * e, b * h - c * f, e * h - g * f
            c5, c4, c3 = p * r - q * q, g * r - h * q, g * q - h * p
            c2, c1, c0 = e * r - f * q, e * q - f * p, e * h - f * g
            d = 1.0 / (((s0 * c5 - s1 * c4) + (s2 * c3 + s3 * c2)) + (s5 * c0 - s4 * c1))
            i00, i01 = (c * c5 - g * c4 + h * c3) * d, (e * c4 - b * c5 - f * c3) * d
            i02, i03 = (h * s5 - q * s4 + r * s3) * d, (p * s4 - g * s5 - q * s3) * d
            i11, i12 = (a * c5 - e * c2 + f * c1) * d, (q * s2 - f * s5 - r * s1) * d
            i13, i22 = (e * s5 - p * s2 + q * s1) * d, (f * s4 - h * s2 + r * s0) * d
            i23, i33 = (g * s2 - e * s4 - q * s0) * d, (e * s3 - g * s1 + p * s0) * d
            inv = [[i00, i01, i02, i03], [i01, i11, i12, i13], [i02, i12, i22, i23], [i03, i13, i23, i33]]
            on = [lane[0:8] == v for v in top]
            new = []
            for m in inv:
                v = (m[0] * rows[0] + m[1] * rows[1]) + (m[2] * rows[2] + m[3] * rows[3])
                for q in range(4):
                    v = jnp.where(on[q], m[q], v)
                new.append(v[0:1])
            left = jnp.where((lane >= idx[0]) & (lane <= idx[3]), 0.0, x)
            stored.append((left - (cols[0] * new[0] + cols[1] * new[1]) - (cols[2] * new[2] + cols[3] * new[3]), new))
        for j, (v, new) in enumerate(stored):
            ref[j] = v
            for q in range(4):
                ref[j, pl.ds(k + q, 1), :] = new[q]
        return carry

    lax.fori_loop(0, n // 4, body, 0)


def program(load_h, a_h, di_h, n_h, phi_h, bcol, nearnode, nearcol, kcol, krow, wt_ref, s64_ref, tmask_ref, spread_ref,
            parts_ref,
            load_v, a_v, n_v, arows, nrows, di_v, phi_v, lb_v, li_v, send, recv, ssend, srecv,
            ksend, krecv, hsend, hrecv, kfull, gfull, sums1, sums2, kc, xo, x2, xf, mark, sems, dsems):

    get_phi = pltpu.make_async_copy(phi_h.at[:, 0, :], phi_v, dsems.at[0])
    get_load = pltpu.make_async_copy(load_h, load_v, dsems.at[1])
    get_di = pltpu.make_async_copy(di_h.at[:, 0, :], di_v, dsems.at[2])
    get_phi.start()
    get_a = pltpu.make_async_copy(a_h.at[:, 0, :], a_v, dsems.at[3])
    get_n = pltpu.make_async_copy(n_h.at[:, 0, :], n_v, dsems.at[4])
    get_load.start()
    get_di.start()
    get_a.start()
    get_n.start()
    sem = pltpu.get_barrier_semaphore()
    everyone(lambda device: pl.semaphore_signal(sem, inc=1, device_id=device, device_id_type=MESH))

    def border_rows(src, dst):
        dst[pl.ds(NB - 8, 8), :] = jnp.zeros((8, NODES), F32)
        for r, n, c in RUNS:
            dst[pl.ds(r, c), :] = src[pl.ds(n, c), :]

    def fence():
        def note(i, carry):
            mark[i] = jnp.zeros((8, 128), F32)
            return carry

        lax.fori_loop(0, 2, note, 0)

    pb, near, pk = choose(bcol, NODES), choose(nearcol, NI), choose(kcol, NB)
    pkt = (lax.broadcasted_iota(jnp.int32, (NB, NS), 0) == krow[...]).astype(F32).astype(BF16)
    wt = wt_ref[...]

    get_phi.wait()
    phi = jnp.concatenate([phi_v[...], jnp.zeros((4, NODES), F32)], axis=0)
    phi8 = jnp.concatenate([phi] * 8, axis=0)
    p24 = pick_cols(phi, pb)
    p64 = pick(s64_ref[...].astype(BF16), p24)
    get_load.wait()
    lb_v[pl.ds(NB - 8, 8), :] = jnp.zeros((8, RHS), F32)
    for i, j, parts in SPLIT:
        for inner, k, r, c in parts:
            (li_v if inner else lb_v)[pl.ds(r, c), :] = load_v[i, j, pl.ds(k, c), :]
    lb, li = lb_v[...], li_v[...]
    get_di.wait()
    start = dot6(pieces(di_v[...]), li)
    get_a.wait()
    border_rows(a_v, arows)
    ab = arows[...]
    k64 = dot(p64, dot(ab, phi8, 1, 1)) * tmask_ref[...]
    ksend[...] = pick_right(k64, spread_ref[...].astype(BF16))
    pl.semaphore_wait(sem, GX * GY * GZ - 1)
    owner_start(ksend, krecv, sems, 0)
    fence()

    spot = lax.broadcasted_iota(jnp.int32, (NB, NODES), 1) == nearnode[...]
    tie = jnp.sum(jnp.where(spot, ab, 0.0), axis=1, keepdims=True)
    c = lb - tie * pick(near, start)
    swap_start(c, pk, send.at[0], recv.at[0], sems, 18)
    gather_start(owner_finish(ksend, krecv, sems, 0)[0:4], kfull, sems, 2)
    fence()
    k0 = jnp.sum(li * start, axis=0, keepdims=True)
    p64 = pieces(p64)
    get_n.wait()
    border_rows(n_v, nrows)
    nbb = pieces(pick_cols(nrows[...], pb))
    ac = swap_finish(c, pkt, send.at[0], recv.at[0], sems, 18)
    f = wt * ac
    hsend[0] = dot6(p64, f)
    owner_start(hsend.at[0], hrecv.at[0], sems, 4)
    fence()
    w = wt * dot6(nbb, f)
    wpk = pick(pk, w)
    swap_start(lb, pk, send.at[1], recv.at[1], sems, 28)
    build_coarse(gather_finish(kfull, sems, 2).reshape(512, 128), kc)
    low = lax.broadcasted_iota(jnp.int32, (64, 128), 1) < 64
    for j in range(2):
        cut = pl.ds(128 * j, 128)
        xo[j] = jnp.where(low, kc[pl.ds(128 * j, 64), cut], kc[pl.ds(128 * j + 64, 64), cut])
    sweep(xo, 64)
    gather_start(owner_finish(hsend.at[0], hrecv.at[0], sems, 4)[0:4], gfull.at[0], sems, 5)
    fence()
    group = lax.broadcasted_iota(jnp.int32, (64, 256), 1) // 64
    both = jnp.concatenate([xo[0], xo[1]], axis=1)
    inv_o = jnp.concatenate([jnp.where(group == g, both, 0.0) for g in range(4)], axis=0)
    koe = kc[pl.ds(0, 256), pl.ds(256, 256)]
    m = dot(inv_o, koe)
    se = kc[pl.ds(256, 256), pl.ds(256, 256)] - dot(koe, m, 0, 0)
    x2[0] = jnp.where(low, se[0:64, 0:128], se[64:128, 0:128])
    sweep(x2, 64)
    inv_2 = jnp.concatenate([jnp.where(low, x2[0], 0.0), jnp.where(low, 0.0, x2[0])], axis=0)
    k2f = se[0:128, 128:256]
    m2 = dot(inv_2, k2f)
    xf[0] = se[128:256, 128:256] - dot(k2f, m2, 0, 0)
    prim = lax.broadcasted_iota(jnp.int32, (24, 512), 0)
    want = jnp.full((24, 512), -1, jnp.int32)
    for q, (t, o) in enumerate(PRIM):
        cx, cy, cz = at(o)
        want = jnp.where(prim == q, place(cz) * 64 + (cx * GY + cy) * 4 + t, want)
    sel = (want == lax.broadcasted_iota(jnp.int32, (24, 512), 1)).astype(F32)
    so = sel[:, 0:256]
    s_e = sel[:, 256:512] - dot(so, m)
    s_2 = s_e[:, 0:128]
    s_f, from_2, from_o = s_e[:, 128:256] - dot(s_2, m2), dot(s_2, inv_2), dot(so, inv_o)
    sweep(xf, 128)
    wf = dot(s_f, xf[0])
    we = jnp.concatenate([from_2 - dot(wf, m2, 1, 1), wf], axis=1)
    w24 = jnp.concatenate([from_o - dot(we, m, 1, 1), we], axis=1)

    def long(v, axis, order):
        q = pieces(v)
        return jnp.concatenate([q[i] for i in order], axis=axis)

    p24t = wt[:, 0:1] * p24.T
    spots = long(p24t, 1, (0, 0, 0, 1, 1, 2))
    packed = mm(pk, spots).astype(BF16)

    def correct_start(w, wpk, g, send, recv, k):
        y = long(dot(w24, g), 0, (0, 1, 2, 0, 1, 0))
        send[REST_ROWS, :] = wpk[NF:] + mm(packed[NF:], y)
        exchange_start(send, recv, sems, k + 1, False)
        send[FACE_ROWS, :] = wpk[:NF] + mm(packed[:NF], y)
        exchange_start(send, recv, sems, k, True)
        return w + mm(spots, y)

    part = lambda a, b: jnp.sum(a * b, axis=0, keepdims=True)
    g = gather_finish(gfull.at[0], sems, 5).reshape(512, RHS)
    u = correct_start(w, wpk, g, ssend.at[0], srecv.at[0], 20)
    fence()
    x = pick_cols(di_v[...], near) * jnp.broadcast_to(tie, (NB, 128)).T[0:1, :]
    s = pieces(pick_cols(ab, pb) - tie * pick(near, x))
    z1 = swap_finish(u, pkt, ssend.at[0], srecv.at[0], sems, 20)
    t1 = dot6(s, z1)
    swap_start(t1, pk, ssend.at[1], srecv.at[1], sems, 22)
    fence()
    gather_start(jnp.concatenate([k0, part(c, z1), part(z1, t1), jnp.zeros((1, RHS), F32)], axis=0), sums1, sems, 11)
    at1 = swap_finish(t1, pkt, ssend.at[1], srecv.at[1], sems, 22)
    f = wt * at1
    hsend[1] = dot6(p64, f)
    owner_start(hsend.at[1], hrecv.at[1], sems, 13)
    fence()
    w = wt * dot6(nbb, f)
    wpk = pick(pk, w)
    gather_start(owner_finish(hsend.at[1], hrecv.at[1], sems, 13)[0:4], gfull.at[1], sems, 14)
    fence()
    sums = jnp.sum(gather_finish(sums1, sems, 11), axis=0)
    k0s = sums[0:1]
    g0 = k0s + sums[1:2]
    s1 = g0 / (k0s + sums[2:3])
    g = gather_finish(gfull.at[1], sems, 14).reshape(512, RHS)
    u = correct_start(w, wpk, g, ssend.at[2], srecv.at[2], 24)
    z2 = swap_finish(u, pkt, ssend.at[2], srecv.at[2], sems, 24)
    t2 = dot6(s, z2)
    zp, tp, cp = z1 - s1 * z2, t1 - s1 * t2, c - s1 * t1
    gather_start(jnp.concatenate([part(cp, zp), part(zp, tp)], axis=0), sums2, sems, 16)
    fence()
    swap_start(t2, pk, ssend.at[3], srecv.at[3], sems, 26)
    fence()
    al = swap_finish(lb, pkt, send.at[1], recv.at[1], sems, 28)
    x1, x2_, _ = pieces(x)
    both1, both2, _ = pieces(jnp.concatenate([z1, zp], axis=1))
    xz = mm(x1, both1) + (mm(x1, both2) + mm(x2_, both1))
    at2 = swap_finish(t2, pkt, ssend.at[3], srecv.at[3], sems, 26)
    last = jnp.sum(gather_finish(sums2, sems, 16), axis=0)
    rest = 1.0 - s1
    g1 = rest * rest * k0s + last[0:1]
    beta = g1 / g0
    s2 = g1 / (rest * rest * k0s + last[1:2] - beta * g1 / s1)

    xb = s1 * z1 + s2 * (zp + beta * z1)
    xi = (s1 + s2 * (rest + beta)) * start - (s1 + s2 * beta) * xz[:, :RHS] - s2 * xz[:, RHS:]
    kappa = rest * (1.0 - s2) - s2 * beta
    ae = al - ac
    rb = kappa * ae + (ac - s1 * at1) - s2 * ((at1 - s1 * at2) + beta * at1)
    parts_ref[pl.ds(AT[0], NB), :], parts_ref[pl.ds(AT[1], NI), :] = xb, xi
    parts_ref[pl.ds(AT[2], NB), :], parts_ref[pl.ds(AT[3], NI), :] = rb, kappa * li


AT = (0, NB, NB + 344, 2 * NB + 344)


def spread(parts_ref, sol_ref, res_ref):
    for i, j, parts in SPLIT:
        for inner, k, r, c in parts:
            there = pl.ds(k, c)
            sol_ref[i, j, there, :] = parts_ref[pl.ds(AT[inner] + r, c), :]
            res_ref[i, j, there, :] = parts_ref[pl.ds(AT[2 + inner] + r, c), :]


def local(load, a, di, n, phi):
    tables = [jnp.asarray(v) for v in (B_COL, NEAR_NODE, NEAR, K_COL, K_COL.T, WEIGHT, S64, TMASK, SPREAD)]
    V = lambda *s: pltpu.VMEM(s, F32)
    shape = jax.ShapeDtypeStruct((M, M, M, RHS), F32)
    parts = pl.pallas_call(
        program,
        out_shape=jax.ShapeDtypeStruct((2 * NB + 688, RHS), F32),
        in_specs=[pl.BlockSpec(memory_space=pl.ANY)] * 5 + [VM] * len(tables),
        out_specs=VM,
        scratch_shapes=[
            V(M, M, M, RHS), V(NODES, NODES), V(NODES, NODES), V(NB, NODES), V(NB, NODES), V(NI, NI), V(20, NODES), V(NB, RHS), V(NI, RHS),
            V(2, NS, RHS), V(2, NS, RHS), V(4, NS, RHS), V(4, NS, RHS),
            V(64, 128), V(64, 128), V(2, 64, 128), V(2, 64, 128), V(128, 4, 128), V(2, 128, 4, 128),
            V(128, 4, 128), V(128, 2, 128), V(512, 512), V(2, 64, 128), V(1, 64, 128), V(1, 128, 128), V(2, 8, 128),
            pltpu.SemaphoreType.DMA((60,)), pltpu.SemaphoreType.DMA((5,)),
        ],
        compiler_params=pltpu.CompilerParams(vmem_limit_bytes=60 * 2**20, collective_id=0, has_side_effects=True),
        name="program",
    )(load, a.reshape(NODES, 1, NODES), di.reshape(NI, 1, NI), n.reshape(NODES, 1, NODES), phi.reshape(20, 1, NODES), *tables)
    return tuple(pl.pallas_call(
        spread, out_shape=[shape, shape], in_specs=[VM], out_specs=[VM] * 2,
        compiler_params=pltpu.CompilerParams(vmem_limit_bytes=16 * 2**20), name="spread",
    )(parts))


def solution(mesh):
    spec4, spec5 = P("gx", "gy", "gz", None), P("gx", "gy", "gz", None, None)
    return jax.shard_map(
        local, mesh=mesh, in_specs=(spec4, spec5, spec5, spec5, spec5), out_specs=(spec4, spec4), check_vma=False
    )
```

```python
import functools

import jax
import jax.numpy as jnp
import numpy as np
from jax import lax
from jax.experimental import pallas as pl
from jax.experimental.pallas import tpu as pltpu
from jax.sharding import PartitionSpec as P

MESH = pl.DeviceIdType.MESH
F32, BF16 = jnp.float32, jnp.bfloat16
GX, GY, GZ = 4, 4, 8
M = 9
NODES, NB, NI, RHS = 729, 392, 343, 128
ORDER = (1, 3, 5, 7, 2, 6, 0, 4)
VM = pl.BlockSpec(memory_space=pltpu.VMEM)

_g = np.indices((M, M, M)).reshape(3, -1)
_rim = ((_g == 0) | (_g == M - 1)).sum(0)
B_IDS, I_IDS = np.where(_rim > 0)[0], np.where(_rim == 0)[0]
B_POS = {int(n): r for r, n in enumerate(B_IDS)}
I_POS = {int(n): r for r, n in enumerate(I_IDS)}


def one_hot(rows, cols, shape):
    out = np.zeros(shape, np.float32)
    out[rows, cols] = 1.0
    return out


B_COL = np.full((NB, 1), -1, np.int32)
B_COL[: len(B_IDS), 0] = B_IDS
NEAR_NODE = np.full((NB, 1), -1, np.int32)
NEAR = np.full((NB, 1), -1, np.int32)
for _r, _n in enumerate(B_IDS):
    if _rim[_n] == 1:
        _i, _j, _k = (min(max(int(v), 1), M - 2) for v in (_n // 81, _n // 9 % 9, _n % 9))
        NEAR_NODE[_r, 0] = (_i * M + _j) * M + _k
        NEAR[_r, 0] = I_POS[(_i * M + _j) * M + _k]
RUNS, _r = [], 0
while _r < len(B_IDS):
    _e = _r + 1
    while _e < len(B_IDS) and B_IDS[_e] == B_IDS[_e - 1] + 1:
        _e += 1
    RUNS.append((_r, int(B_IDS[_r]), _e - _r))
    _r = _e
WEIGHT = np.zeros((NB, 1), np.float32)
WEIGHT[: len(B_IDS), 0] = 1.0 / 2.0 ** _rim[B_IDS]
WEIGHT = np.broadcast_to(WEIGHT, (NB, RHS)).copy()

DIRS = sorted(
    ((x, y, z) for x in (-1, 0, 1) for y in (-1, 0, 1) for z in (-1, 0, 1) if (x, y, z) != (0, 0, 0)),
    key=lambda d: (sum(map(abs, d)), d),
)
SIZE = {1: 88, 2: 16, 3: 8}
OFFS, _at = {}, 0
for _d in DIRS:
    OFFS[_d] = (_at, SIZE[sum(map(abs, _d))])
    _at += OFFS[_d][1]
NS, NF = _at, 6 * SIZE[1]
K_COL = np.full((NS, 1), -1, np.int32)
for _d in DIRS:
    _sel = [[0] if v == -1 else [M - 1] if v == 1 else list(range(M)) for v in _d]
    for _r, (_i, _j, _k) in enumerate((i, j, k) for i in _sel[0] for j in _sel[1] for k in _sel[2]):
        K_COL[OFFS[_d][0] + _r, 0] = B_POS[(_i * M + _j) * M + _k]

CORNERS = [(x, y, z) for x in (0, 1) for y in (0, 1) for z in (0, 1)]
PRIM = [(0, o) for o in CORNERS]
PRIM += [(1, (0, y, z)) for y in (0, 1) for z in (0, 1)]
PRIM += [(2, (x, 0, z)) for x in (0, 1) for z in (0, 1)]
PRIM += [(3, (x, y, 0)) for x in (0, 1) for y in (0, 1)]
S64 = one_hot([CORNERS.index(o) * 8 + t for t, o in PRIM], np.arange(20), (64, 24))
TMASK = (np.arange(64)[:, None] // 8 == np.arange(192)[None, :] // 24).astype(np.float32)
SPREAD = np.zeros((192, 128), np.float32)
for _c, _o1 in enumerate(CORNERS):
    for _q, (_t, _o2) in enumerate(PRIM):
        _f = [b - a + 1 for a, b in zip(_o1, _o2)]
        SPREAD[_c * 24 + _q, _t * 27 + (_f[0] * 3 + _f[1]) * 3 + _f[2]] = 1.0


def dot(a, b, ca=1, cb=0):
    return lax.dot_general(
        a, b, (((ca,), (cb,)), ((), ())), precision=lax.Precision.HIGHEST, preferred_element_type=F32
    )


def pieces(x):
    h = x.astype(BF16)
    r = x - h.astype(F32)
    m = r.astype(BF16)
    return h, m, (r - m.astype(F32)).astype(BF16)


def mm(a, b, ca=1, cb=0):
    return lax.dot_general(a, b, (((ca,), (cb,)), ((), ())), preferred_element_type=F32)


def pick(sel, x):
    h, m, l = pieces(x)
    if x.shape[1] > 128:
        return mm(sel, h) + mm(sel, m) + mm(sel, l)
    n = x.shape[1]
    d = mm(sel, jnp.concatenate([h, m], axis=1))
    return d[:, :n] + d[:, n:] + mm(sel, l)


def pick_cols(x, sel):
    h, m, l = pieces(x)
    return mm(h, sel, 1, 1) + mm(m, sel, 1, 1) + mm(l, sel, 1, 1)


def dot6(a, b):
    b1, b2, b3 = pieces(b)
    n = b.shape[1]
    b12 = jnp.concatenate([b1, b2], axis=1)
    d = mm(a[1], b12) + mm(a[0], b12)
    return (mm(a[0], b3) + mm(a[2], b1)) + d[:, n:] + d[:, :n]


def pick_right(x, sel):
    h, m, l = pieces(x)
    return mm(h, sel) + mm(m, sel) + mm(l, sel)


def here():
    return lax.axis_index("gx"), lax.axis_index("gy"), lax.axis_index("gz")


def at(d):
    x, y, z = here()
    return (lax.rem(x + d[0] + GX, GX), lax.rem(y + d[1] + GY, GY), lax.rem(z + d[2] + GZ, GZ))


_ring = lambda v, n: min(v, n - v)
PLANE = sorted(
    ((x, y) for x in range(GX) for y in range(GY)), key=lambda d: -_ring(d[0], GX) - _ring(d[1], GY)
)


def everyone(act):
    x, y, z = here()
    rows = [(lax.rem(x + d[0], GX), lax.rem(y + d[1], GY)) for d in PLANE]

    def layer(i, carry):
        up = lax.rem(i, 2)
        there = lax.rem(z + 4 + (i // 2 + up) * (1 - 2 * up), GZ)
        for r in rows:
            act((r[0], r[1], there))
        return carry

    lax.fori_loop(0, GZ - 1, layer, 0)
    for r in rows[:-1]:
        act((r[0], r[1], z))


def copy_to(src, dst, sems, k, device):
    return pltpu.make_async_remote_copy(
        src_ref=src, dst_ref=dst, send_sem=sems.at[2 * k], recv_sem=sems.at[2 * k + 1], device_id=device, device_id_type=MESH
    )


def remote(src, dst, sems, k, d):
    return copy_to(src, dst, sems, k, at(d))


def exchange_start(send, recv, sems, k, faces):
    for d in reversed(DIRS):
        if (sum(map(abs, d)) == 1) == faces:
            o, n = OFFS[d]
            o2, _ = OFFS[tuple(-v for v in d)]
            remote(send.at[pl.ds(o, n)], recv.at[pl.ds(o2, n)], sems, k, d).start()


FACE_ROWS, REST_ROWS = pl.ds(0, NF), pl.ds(NF, NS - NF)


def swap_start(v, pk, send, recv, sems, k):
    send[REST_ROWS, :] = pick(pk[NF:], v)
    exchange_start(send, recv, sems, k + 1, False)
    send[FACE_ROWS, :] = pick(pk[:NF], v)
    exchange_start(send, recv, sems, k, True)


def swap_finish(v, pkt, send, recv, sems, k):
    bulk_wait(send.at[FACE_ROWS], recv.at[FACE_ROWS], sems, k)
    v = v + pick(pkt[:, :NF], recv[FACE_ROWS, :])
    bulk_wait(send.at[REST_ROWS], recv.at[REST_ROWS], sems, k + 1)
    return v + pick(pkt[:, NF:], recv[REST_ROWS, :])


def bulk_wait(send, recv, sems, k):
    c = remote(send, recv, sems, k, (1, 0, 0))
    c.wait_recv()
    c.wait_send()


def owner_start(send, recv, sems, k):
    for c, o in reversed(list(enumerate(CORNERS))):
        if c:
            remote(send.at[pl.ds(8 * c, 8)], recv.at[pl.ds(8 * c, 8)], sems, k, o).start()


def owner_finish(send, recv, sems, k):
    bulk_wait(send.at[pl.ds(8, 56)], recv.at[pl.ds(8, 56)], sems, k)
    out = send[pl.ds(0, 8), :]
    for c in range(1, 8):
        out = out + recv[pl.ds(8 * c, 8), :]
    return out


def place(z):
    h = z // 2
    return lax.rem(z, 2) * h + (1 - lax.rem(z, 2)) * (6 - 2 * lax.rem(h, 2) + h // 2)


def gather_start(val, full, sems, k):
    x, y, z = here()
    slot = place(z) * 16 + x * GY + y
    full[slot] = val
    everyone(lambda device: copy_to(full.at[slot], full.at[slot], sems, k, device).start())


def gather_finish(full, sems, k):
    rest = pl.ds(0, 127)
    bulk_wait(full.at[rest], full.at[rest], sems, k)
    return full[...]


SPLIT = []
for _i in range(M):
    for _j in range(M):
        _n = (_i * M + _j) * M
        if _i in (0, M - 1) or _j in (0, M - 1):
            SPLIT.append((_i, _j, [(False, 0, B_POS[_n], M)]))
        else:
            SPLIT.append((_i, _j, [(False, 0, B_POS[_n], 1), (True, 1, I_POS[_n + 1], M - 2), (False, M - 1, B_POS[_n + M - 1], 1)]))


def choose(ids_ref, n):
    ids = ids_ref[...]
    return (lax.broadcasted_iota(jnp.int32, (ids.shape[0], n), 1) == ids).astype(F32).astype(BF16)


def coords(m):
    pos = m >> 6
    c = jnp.where(pos < 4, 2 * pos + 1, jnp.where(pos < 6, 4 * pos - 14, 4 * pos - 24))
    return (m >> 4) & 3, (m >> 2) & 3, c, m & 3


def build_coarse(kall, kc):
    ra, rb, rc, _ = coords(lax.broadcasted_iota(jnp.int32, (512, 128), 0))
    for j in range(4):
        ca, cb, cc, ct = coords(lax.broadcasted_iota(jnp.int32, (1, 128), 1) + 128 * j)
        da, db, dc = (ca + 1 - ra) & 3, (cb + 1 - rb) & 3, (cc + 1 - rc) & 7
        hit = (da < 3) & (db < 3) & (dc < 3)
        slot = jnp.where(hit, ct * 27 + da * 9 + db * 3 + dc, 0)
        v = jnp.take_along_axis(kall, slot, axis=1, mode="promise_in_bounds")
        kc[:, pl.ds(128 * j, 128)] = jnp.where(hit, v, 0.0)


def sweep(ref, n):
    lane = lax.broadcasted_iota(jnp.int32, (n, 128), 1)
    base = lane // n * n
    take = lambda v, idx: jnp.take_along_axis(v, idx, axis=1, mode="promise_in_bounds")

    def body(i, carry):
        k = 4 * i
        idx = [base + (k + q) for q in range(4)]
        top = [v[0:8] for v in idx]
        stored = []
        for j in range(ref.shape[0]):
            x = ref[j]
            rows = [jnp.broadcast_to(ref[j, pl.ds(k + q, 1), :], (8, 128)) for q in range(4)]
            a, b, c = take(rows[0], top[0]), take(rows[0], top[1]), take(rows[1], top[1])
            e, f, g, h = take(rows[0], top[2]), take(rows[0], top[3]), take(rows[1], top[2]), take(rows[1], top[3])
            p, q, r = take(rows[2], top[2]), take(rows[2], top[3]), take(rows[3], top[3])
            cols = [take(x, v) for v in idx]
            d = 1.0 / (a * c - b * b)
            a, b, c = c * d, -b * d, a * d
            we, wf, wg, wh = a * e + b * g, a * f + b * h, b * e + c * g, b * f + c * h
            p, q, r = p - (e * we + g * wg), q - (e * wf + g * wh), r - (f * wf + h * wh)
            d = 1.0 / (p * r - q * q)
            p, q, r = r * d, -q * d, p * d
            ue, uf, ug, uh = we * p + wf * q, we * q + wf * r, wg * p + wh * q, wg * q + wh * r
            a, b, c = a + (ue * we + uf * wf), b + (ue * wg + uf * wh), c + (ug * wg + uh * wh)
            inv = [[a, b, -ue, -uf], [b, c, -ug, -uh], [-ue, -ug, p, q], [-uf, -uh, q, r]]
            on = [lane[0:8] == v for v in top]
            new = []
            for m in inv:
                v = (m[0] * rows[0] + m[1] * rows[1]) + (m[2] * rows[2] + m[3] * rows[3])
                for q in range(4):
                    v = jnp.where(on[q], m[q], v)
                new.append(v[0:1])
            left = jnp.where((lane >= idx[0]) & (lane <= idx[3]), 0.0, x)
            stored.append((left - (cols[0] * new[0] + cols[1] * new[1]) - (cols[2] * new[2] + cols[3] * new[3]), new))
        for j, (v, new) in enumerate(stored):
            ref[j] = v
            for q in range(4):
                ref[j, pl.ds(k + q, 1), :] = new[q]
        return carry

    lax.fori_loop(0, n // 4, body, 0)


def program(load_h, a_h, di_h, n_h, phi_h, bcol, nearnode, nearcol, kcol, krow, wt_ref, s64_ref, tmask_ref, spread_ref,
            parts_ref,
            load_v, a_v, n_v, arows, nrows, di_v, phi_v, lb_v, li_v, send, recv, ssend, srecv,
            ksend, krecv, hsend, hrecv, kfull, gfull, sums1, sums2, kc, xo, x2, xf, mark, sems, dsems):

    get_phi = pltpu.make_async_copy(phi_h.at[:, 0, :], phi_v, dsems.at[0])
    get_load = pltpu.make_async_copy(load_h, load_v, dsems.at[1])
    get_di = pltpu.make_async_copy(di_h.at[:, 0, :], di_v, dsems.at[2])
    get_phi.start()
    get_a = pltpu.make_async_copy(a_h.at[:, 0, :], a_v, dsems.at[3])
    get_n = pltpu.make_async_copy(n_h.at[:, 0, :], n_v, dsems.at[4])
    get_load.start()
    get_di.start()
    get_a.start()
    get_n.start()
    sem = pltpu.get_barrier_semaphore()
    everyone(lambda device: pl.semaphore_signal(sem, inc=1, device_id=device, device_id_type=MESH))

    def border_rows(src, dst):
        dst[pl.ds(NB - 8, 8), :] = jnp.zeros((8, NODES), F32)
        for r, n, c in RUNS:
            dst[pl.ds(r, c), :] = src[pl.ds(n, c), :]

    def fence():
        def note(i, carry):
            mark[i] = jnp.zeros((8, 128), F32)
            return carry

        lax.fori_loop(0, 2, note, 0)

    pb = choose(bcol, NODES)
    wt = wt_ref[...]

    get_phi.wait()
    phi = jnp.concatenate([phi_v[...], jnp.zeros((4, NODES), F32)], axis=0)
    phi8 = jnp.concatenate([phi] * 8, axis=0)
    p24 = pick_cols(phi, pb)
    p64 = pick(s64_ref[...].astype(BF16), p24)
    get_load.wait()
    lb_v[pl.ds(NB - 8, 8), :] = jnp.zeros((8, RHS), F32)
    for i, j, parts in SPLIT:
        for inner, k, r, c in parts:
            (li_v if inner else lb_v)[pl.ds(r, c), :] = load_v[i, j, pl.ds(k, c), :]
    lb, li = lb_v[...], li_v[...]
    get_di.wait()
    start = dot6(pieces(di_v[...]), li)
    get_a.wait()
    border_rows(a_v, arows)
    ab = arows[...]
    k64 = dot(p64, dot(ab, phi8, 1, 1)) * tmask_ref[...]
    ksend[...] = pick_right(k64, spread_ref[...].astype(BF16))
    pl.semaphore_wait(sem, GX * GY * GZ - 1)
    owner_start(ksend, krecv, sems, 0)
    fence()
    near, pk = choose(nearcol, NI), choose(kcol, NB)
    pkt = (lax.broadcasted_iota(jnp.int32, (NB, NS), 0) == krow[...]).astype(F32).astype(BF16)

    spot = lax.broadcasted_iota(jnp.int32, (NB, NODES), 1) == nearnode[...]
    tie = jnp.sum(jnp.where(spot, ab, 0.0), axis=1, keepdims=True)
    c = lb - tie * pick(near, start)
    swap_start(c, pk, send.at[0], recv.at[0], sems, 18)
    gather_start(owner_finish(ksend, krecv, sems, 0)[0:4], kfull, sems, 2)
    fence()
    k0 = jnp.sum(li * start, axis=0, keepdims=True)
    p64 = pieces(p64)
    get_n.wait()
    border_rows(n_v, nrows)
    nbb = pieces(pick_cols(nrows[...], pb))
    ac = swap_finish(c, pkt, send.at[0], recv.at[0], sems, 18)
    f = wt * ac
    hsend[0] = dot6(p64, f)
    owner_start(hsend.at[0], hrecv.at[0], sems, 4)
    fence()
    w = wt * dot6(nbb, f)
    wpk = pick(pk, w)
    build_coarse(gather_finish(kfull, sems, 2).reshape(512, 128), kc)
    low = lax.broadcasted_iota(jnp.int32, (64, 128), 1) < 64
    for j in range(2):
        cut = pl.ds(128 * j, 128)
        xo[j] = jnp.where(low, kc[pl.ds(128 * j, 64), cut], kc[pl.ds(128 * j + 64, 64), cut])
    sweep(xo, 64)
    gather_start(owner_finish(hsend.at[0], hrecv.at[0], sems, 4)[0:4], gfull.at[0], sems, 5)
    fence()
    group = lax.broadcasted_iota(jnp.int32, (64, 256), 1) // 64
    both = jnp.concatenate([xo[0], xo[1]], axis=1)
    inv_o = jnp.concatenate([jnp.where(group == g, both, 0.0) for g in range(4)], axis=0)
    koe = kc[pl.ds(0, 256), pl.ds(256, 256)]
    m = dot(inv_o, koe)
    se = kc[pl.ds(256, 256), pl.ds(256, 256)] - dot(koe, m, 0, 0)
    x2[0] = jnp.where(low, se[0:64, 0:128], se[64:128, 0:128])
    sweep(x2, 64)
    inv_2 = jnp.concatenate([jnp.where(low, x2[0], 0.0), jnp.where(low, 0.0, x2[0])], axis=0)
    k2f = se[0:128, 128:256]
    m2 = dot(inv_2, k2f)
    xf[0] = se[128:256, 128:256] - dot(k2f, m2, 0, 0)
    prim = lax.broadcasted_iota(jnp.int32, (24, 512), 0)
    want = jnp.full((24, 512), -1, jnp.int32)
    for q, (t, o) in enumerate(PRIM):
        cx, cy, cz = at(o)
        want = jnp.where(prim == q, place(cz) * 64 + (cx * GY + cy) * 4 + t, want)
    sel = (want == lax.broadcasted_iota(jnp.int32, (24, 512), 1)).astype(F32)
    so = sel[:, 0:256]
    s_e = sel[:, 256:512] - dot(so, m)
    s_2 = s_e[:, 0:128]
    s_f, from_2, from_o = s_e[:, 128:256] - dot(s_2, m2), dot(s_2, inv_2), dot(so, inv_o)
    sweep(xf, 128)
    wf = dot(s_f, xf[0])
    we = jnp.concatenate([from_2 - dot(wf, m2, 1, 1), wf], axis=1)
    w24 = jnp.concatenate([from_o - dot(we, m, 1, 1), we], axis=1)

    def long(v, axis, order):
        q = pieces(v)
        return jnp.concatenate([q[i] for i in order], axis=axis)

    p24t = wt[:, 0:1] * p24.T
    spots = long(p24t, 1, (0, 0, 0, 1, 1, 2))
    packed = mm(pk, spots).astype(BF16)

    def correct_start(w, wpk, g, send, recv, k):
        y = long(dot(w24, g), 0, (0, 1, 2, 0, 1, 0))
        send[REST_ROWS, :] = wpk[NF:] + mm(packed[NF:], y)
        exchange_start(send, recv, sems, k + 1, False)
        send[FACE_ROWS, :] = wpk[:NF] + mm(packed[:NF], y)
        exchange_start(send, recv, sems, k, True)
        return w + mm(spots, y)

    part = lambda a, b: jnp.sum(a * b, axis=0, keepdims=True)
    g = gather_finish(gfull.at[0], sems, 5).reshape(512, RHS)
    u = correct_start(w, wpk, g, ssend.at[0], srecv.at[0], 20)
    fence()
    x = pick_cols(di_v[...], near) * jnp.broadcast_to(tie, (NB, 128)).T[0:1, :]
    s = pieces(pick_cols(ab, pb) - tie * pick(near, x))
    z1 = swap_finish(u, pkt, ssend.at[0], srecv.at[0], sems, 20)
    t1 = dot6(s, z1)
    swap_start(t1, pk, ssend.at[1], srecv.at[1], sems, 22)
    fence()
    gather_start(jnp.concatenate([k0, part(c, z1), part(z1, t1), jnp.zeros((1, RHS), F32)], axis=0), sums1, sems, 11)
    at1 = swap_finish(t1, pkt, ssend.at[1], srecv.at[1], sems, 22)
    f = wt * at1
    hsend[1] = dot6(p64, f)
    owner_start(hsend.at[1], hrecv.at[1], sems, 13)
    fence()
    w = wt * dot6(nbb, f)
    wpk = pick(pk, w)
    gather_start(owner_finish(hsend.at[1], hrecv.at[1], sems, 13)[0:4], gfull.at[1], sems, 14)
    fence()
    swap_start(lb, pk, send.at[1], recv.at[1], sems, 28)
    sums = jnp.sum(gather_finish(sums1, sems, 11), axis=0)
    k0s = sums[0:1]
    g0 = k0s + sums[1:2]
    s1 = g0 / (k0s + sums[2:3])
    g = gather_finish(gfull.at[1], sems, 14).reshape(512, RHS)
    u = correct_start(w, wpk, g, ssend.at[2], srecv.at[2], 24)
    z2 = swap_finish(u, pkt, ssend.at[2], srecv.at[2], sems, 24)
    t2 = dot6(s, z2)
    zp, tp, cp = z1 - s1 * z2, t1 - s1 * t2, c - s1 * t1
    gather_start(jnp.concatenate([part(cp, zp), part(zp, tp)], axis=0), sums2, sems, 16)
    fence()
    swap_start(t2, pk, ssend.at[3], srecv.at[3], sems, 26)
    fence()
    al = swap_finish(lb, pkt, send.at[1], recv.at[1], sems, 28)
    x1, x2_, _ = pieces(x)
    both1, both2, _ = pieces(jnp.concatenate([z1, zp], axis=1))
    xz = mm(x1, both1) + (mm(x1, both2) + mm(x2_, both1))
    at2 = swap_finish(t2, pkt, ssend.at[3], srecv.at[3], sems, 26)
    last = jnp.sum(gather_finish(sums2, sems, 16), axis=0)
    rest = 1.0 - s1
    g1 = rest * rest * k0s + last[0:1]
    beta = g1 / g0
    s2 = g1 / (rest * rest * k0s + last[1:2] - beta * g1 / s1)

    xb = s1 * z1 + s2 * (zp + beta * z1)
    xi = (s1 + s2 * (rest + beta)) * start - (s1 + s2 * beta) * xz[:, :RHS] - s2 * xz[:, RHS:]
    kappa = rest * (1.0 - s2) - s2 * beta
    ae = al - ac
    rb = kappa * ae + (ac - s1 * at1) - s2 * ((at1 - s1 * at2) + beta * at1)
    parts_ref[pl.ds(AT[0], NB), :], parts_ref[pl.ds(AT[1], NI), :] = xb, xi
    parts_ref[pl.ds(AT[2], NB), :], parts_ref[pl.ds(AT[3], NI), :] = rb, kappa * li


AT = (0, NB, NB + 344, 2 * NB + 344)


def spread(parts_ref, sol_ref, res_ref):
    for i, j, parts in SPLIT:
        for inner, k, r, c in parts:
            there = pl.ds(k, c)
            sol_ref[i, j, there, :] = parts_ref[pl.ds(AT[inner] + r, c), :]
            res_ref[i, j, there, :] = parts_ref[pl.ds(AT[2 + inner] + r, c), :]


def local(load, a, di, n, phi):
    tables = [jnp.asarray(v) for v in (B_COL, NEAR_NODE, NEAR, K_COL, K_COL.T, WEIGHT, S64, TMASK, SPREAD)]
    V = lambda *s: pltpu.VMEM(s, F32)
    shape = jax.ShapeDtypeStruct((M, M, M, RHS), F32)
    parts = pl.pallas_call(
        program,
        out_shape=jax.ShapeDtypeStruct((2 * NB + 688, RHS), F32),
        in_specs=[pl.BlockSpec(memory_space=pl.ANY)] * 5 + [VM] * len(tables),
        out_specs=VM,
        scratch_shapes=[
            V(M, M, M, RHS), V(NODES, NODES), V(NODES, NODES), V(NB, NODES), V(NB, NODES), V(NI, NI), V(20, NODES), V(NB, RHS), V(NI, RHS),
            V(2, NS, RHS), V(2, NS, RHS), V(4, NS, RHS), V(4, NS, RHS),
            V(64, 128), V(64, 128), V(2, 64, 128), V(2, 64, 128), V(128, 4, 128), V(2, 128, 4, 128),
            V(128, 4, 128), V(128, 2, 128), V(512, 512), V(2, 64, 128), V(1, 64, 128), V(1, 128, 128), V(2, 8, 128),
            pltpu.SemaphoreType.DMA((60,)), pltpu.SemaphoreType.DMA((5,)),
        ],
        compiler_params=pltpu.CompilerParams(vmem_limit_bytes=60 * 2**20, collective_id=0, has_side_effects=True),
        name="program",
    )(load, a.reshape(NODES, 1, NODES), di.reshape(NI, 1, NI), n.reshape(NODES, 1, NODES), phi.reshape(20, 1, NODES), *tables)
    return tuple(pl.pallas_call(
        spread, out_shape=[shape, shape], in_specs=[VM], out_specs=[VM] * 2,
        compiler_params=pltpu.CompilerParams(vmem_limit_bytes=16 * 2**20), name="spread",
    )(parts))


def solution(mesh):
    spec4, spec5 = P("gx", "gy", "gz", None), P("gx", "gy", "gz", None, None)
    return jax.shard_map(
        local, mesh=mesh, in_specs=(spec4, spec5, spec5, spec5, spec5), out_specs=(spec4, spec4), check_vma=False
    )
```

```python
import functools

import jax
import jax.numpy as jnp
import numpy as np
from jax import lax
from jax.experimental import pallas as pl
from jax.experimental.pallas import tpu as pltpu
from jax.sharding import PartitionSpec as P

MESH = pl.DeviceIdType.MESH
F32, BF16 = jnp.float32, jnp.bfloat16
GX, GY, GZ = 4, 4, 8
M = 9
NODES, NB, NI, RHS = 729, 392, 343, 128
ORDER = (1, 3, 5, 7, 2, 6, 0, 4)
VM = pl.BlockSpec(memory_space=pltpu.VMEM)

_g = np.indices((M, M, M)).reshape(3, -1)
_rim = ((_g == 0) | (_g == M - 1)).sum(0)
B_IDS, I_IDS = np.where(_rim > 0)[0], np.where(_rim == 0)[0]
B_POS = {int(n): r for r, n in enumerate(B_IDS)}
I_POS = {int(n): r for r, n in enumerate(I_IDS)}


def one_hot(rows, cols, shape):
    out = np.zeros(shape, np.float32)
    out[rows, cols] = 1.0
    return out


B_COL = np.full((NB, 1), -1, np.int32)
B_COL[: len(B_IDS), 0] = B_IDS
NEAR_NODE = np.full((NB, 1), -1, np.int32)
NEAR = np.full((NB, 1), -1, np.int32)
for _r, _n in enumerate(B_IDS):
    if _rim[_n] == 1:
        _i, _j, _k = (min(max(int(v), 1), M - 2) for v in (_n // 81, _n // 9 % 9, _n % 9))
        NEAR_NODE[_r, 0] = (_i * M + _j) * M + _k
        NEAR[_r, 0] = I_POS[(_i * M + _j) * M + _k]
RUNS, _r = [], 0
while _r < len(B_IDS):
    _e = _r + 1
    while _e < len(B_IDS) and B_IDS[_e] == B_IDS[_e - 1] + 1:
        _e += 1
    RUNS.append((_r, int(B_IDS[_r]), _e - _r))
    _r = _e
WEIGHT = np.zeros((NB, 1), np.float32)
WEIGHT[: len(B_IDS), 0] = 1.0 / 2.0 ** _rim[B_IDS]
WEIGHT = np.broadcast_to(WEIGHT, (NB, RHS)).copy()

DIRS = sorted(
    ((x, y, z) for x in (-1, 0, 1) for y in (-1, 0, 1) for z in (-1, 0, 1) if (x, y, z) != (0, 0, 0)),
    key=lambda d: (sum(map(abs, d)), d),
)
SIZE = {1: 88, 2: 16, 3: 8}
OFFS, _at = {}, 0
for _d in DIRS:
    OFFS[_d] = (_at, SIZE[sum(map(abs, _d))])
    _at += OFFS[_d][1]
NS, NF = _at, 6 * SIZE[1]
K_COL = np.full((NS, 1), -1, np.int32)
for _d in DIRS:
    _sel = [[0] if v == -1 else [M - 1] if v == 1 else list(range(M)) for v in _d]
    for _r, (_i, _j, _k) in enumerate((i, j, k) for i in _sel[0] for j in _sel[1] for k in _sel[2]):
        K_COL[OFFS[_d][0] + _r, 0] = B_POS[(_i * M + _j) * M + _k]

CORNERS = [(x, y, z) for x in (0, 1) for y in (0, 1) for z in (0, 1)]
PRIM = [(0, o) for o in CORNERS]
PRIM += [(1, (0, y, z)) for y in (0, 1) for z in (0, 1)]
PRIM += [(2, (x, 0, z)) for x in (0, 1) for z in (0, 1)]
PRIM += [(3, (x, y, 0)) for x in (0, 1) for y in (0, 1)]
S64 = one_hot([CORNERS.index(o) * 8 + t for t, o in PRIM], np.arange(20), (64, 24))
TMASK = (np.arange(64)[:, None] // 8 == np.arange(192)[None, :] // 24).astype(np.float32)
SPREAD = np.zeros((192, 128), np.float32)
for _c, _o1 in enumerate(CORNERS):
    for _q, (_t, _o2) in enumerate(PRIM):
        _f = [b - a + 1 for a, b in zip(_o1, _o2)]
        SPREAD[_c * 24 + _q, _t * 27 + (_f[0] * 3 + _f[1]) * 3 + _f[2]] = 1.0


def dot(a, b, ca=1, cb=0):
    return lax.dot_general(
        a, b, (((ca,), (cb,)), ((), ())), precision=lax.Precision.HIGHEST, preferred_element_type=F32
    )


def pieces(x):
    h = x.astype(BF16)
    r = x - h.astype(F32)
    m = r.astype(BF16)
    return h, m, (r - m.astype(F32)).astype(BF16)


def mm(a, b, ca=1, cb=0):
    return lax.dot_general(a, b, (((ca,), (cb,)), ((), ())), preferred_element_type=F32)


def pick(sel, x):
    h, m, l = pieces(x)
    if x.shape[1] > 128:
        return mm(sel, h) + mm(sel, m) + mm(sel, l)
    n = x.shape[1]
    d = mm(sel, jnp.concatenate([h, m], axis=1))
    return d[:, :n] + d[:, n:] + mm(sel, l)


def pick_cols(x, sel):
    h, m, l = pieces(x)
    return mm(h, sel, 1, 1) + mm(m, sel, 1, 1) + mm(l, sel, 1, 1)


def dot6(a, b):
    b1, b2, b3 = pieces(b)
    n = b.shape[1]
    b12 = jnp.concatenate([b1, b2], axis=1)
    d = mm(a[1], b12) + mm(a[0], b12)
    return (mm(a[0], b3) + mm(a[2], b1)) + d[:, n:] + d[:, :n]


def pick_right(x, sel):
    h, m, l = pieces(x)
    return mm(h, sel) + mm(m, sel) + mm(l, sel)


def here():
    return lax.axis_index("gx"), lax.axis_index("gy"), lax.axis_index("gz")


def at(d):
    x, y, z = here()
    return (lax.rem(x + d[0] + GX, GX), lax.rem(y + d[1] + GY, GY), lax.rem(z + d[2] + GZ, GZ))


_ring = lambda v, n: min(v, n - v)
PLANE = sorted(
    ((x, y) for x in range(GX) for y in range(GY)), key=lambda d: -_ring(d[0], GX) - _ring(d[1], GY)
)


def everyone(act):
    x, y, z = here()
    rows = [(lax.rem(x + d[0], GX), lax.rem(y + d[1], GY)) for d in PLANE]

    def layer(i, carry):
        up = lax.rem(i, 2)
        there = lax.rem(z + 4 + (i // 2 + up) * (1 - 2 * up), GZ)
        for r in rows:
            act((r[0], r[1], there))
        return carry

    lax.fori_loop(0, GZ - 1, layer, 0)
    for r in rows[:-1]:
        act((r[0], r[1], z))


def copy_to(src, dst, sems, k, device):
    return pltpu.make_async_remote_copy(
        src_ref=src, dst_ref=dst, send_sem=sems.at[2 * k], recv_sem=sems.at[2 * k + 1], device_id=device, device_id_type=MESH
    )


def remote(src, dst, sems, k, d):
    return copy_to(src, dst, sems, k, at(d))


def exchange_start(send, recv, sems, k, faces):
    for d in reversed(DIRS):
        if (sum(map(abs, d)) == 1) == faces:
            o, n = OFFS[d]
            o2, _ = OFFS[tuple(-v for v in d)]
            remote(send.at[pl.ds(o, n)], recv.at[pl.ds(o2, n)], sems, k, d).start()


FACE_ROWS, REST_ROWS = pl.ds(0, NF), pl.ds(NF, NS - NF)


def swap_start(v, pk, send, recv, sems, k):
    send[REST_ROWS, :] = pick(pk[NF:], v)
    exchange_start(send, recv, sems, k + 1, False)
    send[FACE_ROWS, :] = pick(pk[:NF], v)
    exchange_start(send, recv, sems, k, True)


def swap_finish(v, pkt, send, recv, sems, k):
    bulk_wait(send.at[FACE_ROWS], recv.at[FACE_ROWS], sems, k)
    v = v + pick(pkt[:, :NF], recv[FACE_ROWS, :])
    bulk_wait(send.at[REST_ROWS], recv.at[REST_ROWS], sems, k + 1)
    return v + pick(pkt[:, NF:], recv[REST_ROWS, :])


def bulk_wait(send, recv, sems, k):
    c = remote(send, recv, sems, k, (1, 0, 0))
    c.wait_recv()
    c.wait_send()


def owner_start(send, recv, sems, k):
    for c, o in reversed(list(enumerate(CORNERS))):
        if c:
            remote(send.at[pl.ds(8 * c, 8)], recv.at[pl.ds(8 * c, 8)], sems, k, o).start()


def owner_finish(send, recv, sems, k):
    bulk_wait(send.at[pl.ds(8, 56)], recv.at[pl.ds(8, 56)], sems, k)
    out = send[pl.ds(0, 8), :]
    for c in range(1, 8):
        out = out + recv[pl.ds(8 * c, 8), :]
    return out


def place(z):
    h = z // 2
    return lax.rem(z, 2) * h + (1 - lax.rem(z, 2)) * (6 - 2 * lax.rem(h, 2) + h // 2)


def gather_start(val, full, sems, k):
    x, y, z = here()
    slot = place(z) * 16 + x * GY + y
    full[slot] = val
    everyone(lambda device: copy_to(full.at[slot], full.at[slot], sems, k, device).start())


def gather_finish(full, sems, k):
    rest = pl.ds(0, 127)
    bulk_wait(full.at[rest], full.at[rest], sems, k)
    return full[...]


SPLIT = []
for _i in range(M):
    for _j in range(M):
        _n = (_i * M + _j) * M
        if _i in (0, M - 1) or _j in (0, M - 1):
            SPLIT.append((_i, _j, [(False, 0, B_POS[_n], M)]))
        else:
            SPLIT.append((_i, _j, [(False, 0, B_POS[_n], 1), (True, 1, I_POS[_n + 1], M - 2), (False, M - 1, B_POS[_n + M - 1], 1)]))


def choose(ids_ref, n):
    ids = ids_ref[...]
    return (lax.broadcasted_iota(jnp.int32, (ids.shape[0], n), 1) == ids).astype(F32).astype(BF16)


def coords(m):
    pos = m >> 6
    c = jnp.where(pos < 4, 2 * pos + 1, jnp.where(pos < 6, 4 * pos - 14, 4 * pos - 24))
    return (m >> 4) & 3, (m >> 2) & 3, c, m & 3


def build_coarse(kall, kc):
    ra, rb, rc, _ = coords(lax.broadcasted_iota(jnp.int32, (512, 128), 0))
    for j in range(4):
        ca, cb, cc, ct = coords(lax.broadcasted_iota(jnp.int32, (1, 128), 1) + 128 * j)
        da, db, dc = (ca + 1 - ra) & 3, (cb + 1 - rb) & 3, (cc + 1 - rc) & 7
        hit = (da < 3) & (db < 3) & (dc < 3)
        slot = jnp.where(hit, ct * 27 + da * 9 + db * 3 + dc, 0)
        v = jnp.take_along_axis(kall, slot, axis=1, mode="promise_in_bounds")
        kc[:, pl.ds(128 * j, 128)] = jnp.where(hit, v, 0.0)


def sweep(ref, n):
    lane = lax.broadcasted_iota(jnp.int32, (n, 128), 1)
    base = lane // n * n
    take = lambda v, idx: jnp.take_along_axis(v, idx, axis=1, mode="promise_in_bounds")

    def body(i, carry):
        k = 4 * i
        idx = [base + (k + q) for q in range(4)]
        top = [v[0:8] for v in idx]
        stored = []
        for j in range(ref.shape[0]):
            x = ref[j]
            rows = [jnp.broadcast_to(ref[j, pl.ds(k + q, 1), :], (8, 128)) for q in range(4)]
            a, b, c = take(rows[0], top[0]), take(rows[0], top[1]), take(rows[1], top[1])
            e, f, g, h = take(rows[0], top[2]), take(rows[0], top[3]), take(rows[1], top[2]), take(rows[1], top[3])
            p, q, r = take(rows[2], top[2]), take(rows[2], top[3]), take(rows[3], top[3])
            cols = [take(x, v) for v in idx]
            d = 1.0 / (a * c - b * b)
            a, b, c = c * d, -b * d, a * d
            we, wf, wg, wh = a * e + b * g, a * f + b * h, b * e + c * g, b * f + c * h
            p, q, r = p - (e * we + g * wg), q - (e * wf + g * wh), r - (f * wf + h * wh)
            d = 1.0 / (p * r - q * q)
            p, q, r = r * d, -q * d, p * d
            ue, uf, ug, uh = we * p + wf * q, we * q + wf * r, wg * p + wh * q, wg * q + wh * r
            a, b, c = a + (ue * we + uf * wf), b + (ue * wg + uf * wh), c + (ug * wg + uh * wh)
            inv = [[a, b, -ue, -uf], [b, c, -ug, -uh], [-ue, -ug, p, q], [-uf, -uh, q, r]]
            on = [lane[0:8] == v for v in top]
            new = []
            for m in inv:
                v = (m[0] * rows[0] + m[1] * rows[1]) + (m[2] * rows[2] + m[3] * rows[3])
                for q in range(4):
                    v = jnp.where(on[q], m[q], v)
                new.append(v[0:1])
            left = jnp.where((lane >= idx[0]) & (lane <= idx[3]), 0.0, x)
            stored.append((left - (cols[0] * new[0] + cols[1] * new[1]) - (cols[2] * new[2] + cols[3] * new[3]), new))
        for j, (v, new) in enumerate(stored):
            ref[j] = v
            for q in range(4):
                ref[j, pl.ds(k + q, 1), :] = new[q]
        return carry

    lax.fori_loop(0, n // 4, body, 0)


def program(load_h, a_h, di_h, n_h, phi_h, bcol, nearnode, nearcol, kcol, krow, wt_ref, s64_ref, tmask_ref, spread_ref,
            parts_ref,
            load_v, a_v, n_v, arows, nrows, di_v, phi_v, lb_v, li_v, send, recv, ssend, srecv,
            ksend, krecv, hsend, hrecv, kfull, gfull, sums1, sums2, kc, xo, x2, xf, mark, sems, dsems):

    get_phi = pltpu.make_async_copy(phi_h.at[:, 0, :], phi_v, dsems.at[0])
    get_load = pltpu.make_async_copy(load_h, load_v, dsems.at[1])
    get_di = pltpu.make_async_copy(di_h.at[:, 0, :], di_v, dsems.at[2])
    get_phi.start()
    get_a = pltpu.make_async_copy(a_h.at[:, 0, :], a_v, dsems.at[3])
    get_n = pltpu.make_async_copy(n_h.at[:, 0, :], n_v, dsems.at[4])
    get_a.start()
    get_load.start()
    get_di.start()
    get_n.start()
    sem = pltpu.get_barrier_semaphore()
    everyone(lambda device: pl.semaphore_signal(sem, inc=1, device_id=device, device_id_type=MESH))

    def border_rows(src, dst):
        dst[pl.ds(NB - 8, 8), :] = jnp.zeros((8, NODES), F32)
        for r, n, c in RUNS:
            dst[pl.ds(r, c), :] = src[pl.ds(n, c), :]

    def fence():
        def note(i, carry):
            mark[i] = jnp.zeros((8, 128), F32)
            return carry

        lax.fori_loop(0, 2, note, 0)

    pb = choose(bcol, NODES)
    wt = wt_ref[...]

    get_phi.wait()
    phi = jnp.concatenate([phi_v[...], jnp.zeros((4, NODES), F32)], axis=0)
    phi8 = jnp.concatenate([phi] * 8, axis=0)
    p24 = pick_cols(phi, pb)
    p64 = pick(s64_ref[...].astype(BF16), p24)
    get_a.wait()
    border_rows(a_v, arows)
    ab = arows[...]
    k64 = dot(p64, dot(ab, phi8, 1, 1)) * tmask_ref[...]
    ksend[...] = pick_right(k64, spread_ref[...].astype(BF16))
    pl.semaphore_wait(sem, GX * GY * GZ - 1)
    owner_start(ksend, krecv, sems, 0)
    fence()
    near, pk = choose(nearcol, NI), choose(kcol, NB)
    pkt = (lax.broadcasted_iota(jnp.int32, (NB, NS), 0) == krow[...]).astype(F32).astype(BF16)
    get_load.wait()
    lb_v[pl.ds(NB - 8, 8), :] = jnp.zeros((8, RHS), F32)
    for i, j, parts in SPLIT:
        for inner, k, r, c in parts:
            (li_v if inner else lb_v)[pl.ds(r, c), :] = load_v[i, j, pl.ds(k, c), :]
    lb, li = lb_v[...], li_v[...]
    get_di.wait()
    start = dot6(pieces(di_v[...]), li)

    spot = lax.broadcasted_iota(jnp.int32, (NB, NODES), 1) == nearnode[...]
    tie = jnp.sum(jnp.where(spot, ab, 0.0), axis=1, keepdims=True)
    c = lb - tie * pick(near, start)
    swap_start(c, pk, send.at[0], recv.at[0], sems, 18)
    gather_start(owner_finish(ksend, krecv, sems, 0)[0:4], kfull, sems, 2)
    fence()
    k0 = jnp.sum(li * start, axis=0, keepdims=True)
    p64 = pieces(p64)
    get_n.wait()
    border_rows(n_v, nrows)
    nbb = pieces(pick_cols(nrows[...], pb))
    ac = swap_finish(c, pkt, send.at[0], recv.at[0], sems, 18)
    f = wt * ac
    hsend[0] = dot6(p64, f)
    owner_start(hsend.at[0], hrecv.at[0], sems, 4)
    fence()
    w = wt * dot6(nbb, f)
    wpk = pick(pk, w)
    build_coarse(gather_finish(kfull, sems, 2).reshape(512, 128), kc)
    low = lax.broadcasted_iota(jnp.int32, (64, 128), 1) < 64
    for j in range(2):
        cut = pl.ds(128 * j, 128)
        xo[j] = jnp.where(low, kc[pl.ds(128 * j, 64), cut], kc[pl.ds(128 * j + 64, 64), cut])
    sweep(xo, 64)
    gather_start(owner_finish(hsend.at[0], hrecv.at[0], sems, 4)[0:4], gfull.at[0], sems, 5)
    fence()
    group = lax.broadcasted_iota(jnp.int32, (64, 256), 1) // 64
    both = jnp.concatenate([xo[0], xo[1]], axis=1)
    inv_o = jnp.concatenate([jnp.where(group == g, both, 0.0) for g in range(4)], axis=0)
    koe = kc[pl.ds(0, 256), pl.ds(256, 256)]
    m = dot(inv_o, koe)
    se = kc[pl.ds(256, 256), pl.ds(256, 256)] - dot(koe, m, 0, 0)
    x2[0] = jnp.where(low, se[0:64, 0:128], se[64:128, 0:128])
    sweep(x2, 64)
    inv_2 = jnp.concatenate([jnp.where(low, x2[0], 0.0), jnp.where(low, 0.0, x2[0])], axis=0)
    k2f = se[0:128, 128:256]
    m2 = dot(inv_2, k2f)
    xf[0] = se[128:256, 128:256] - dot(k2f, m2, 0, 0)
    prim = lax.broadcasted_iota(jnp.int32, (24, 512), 0)
    want = jnp.full((24, 512), -1, jnp.int32)
    for q, (t, o) in enumerate(PRIM):
        cx, cy, cz = at(o)
        want = jnp.where(prim == q, place(cz) * 64 + (cx * GY + cy) * 4 + t, want)
    sel = (want == lax.broadcasted_iota(jnp.int32, (24, 512), 1)).astype(F32)
    so = sel[:, 0:256]
    s_e = sel[:, 256:512] - dot(so, m)
    s_2 = s_e[:, 0:128]
    s_f, from_2, from_o = s_e[:, 128:256] - dot(s_2, m2), dot(s_2, inv_2), dot(so, inv_o)
    sweep(xf, 128)
    wf = dot(s_f, xf[0])
    we = jnp.concatenate([from_2 - dot(wf, m2, 1, 1), wf], axis=1)
    w24 = jnp.concatenate([from_o - dot(we, m, 1, 1), we], axis=1)

    def long(v, axis, order):
        q = pieces(v)
        return jnp.concatenate([q[i] for i in order], axis=axis)

    p24t = wt[:, 0:1] * p24.T
    spots = long(p24t, 1, (0, 0, 0, 1, 1, 2))
    packed = mm(pk, spots).astype(BF16)

    def correct_start(w, wpk, g, send, recv, k):
        y = long(dot(w24, g), 0, (0, 1, 2, 0, 1, 0))
        send[REST_ROWS, :] = wpk[NF:] + mm(packed[NF:], y)
        exchange_start(send, recv, sems, k + 1, False)
        send[FACE_ROWS, :] = wpk[:NF] + mm(packed[:NF], y)
        exchange_start(send, recv, sems, k, True)
        return w + mm(spots, y)

    part = lambda a, b: jnp.sum(a * b, axis=0, keepdims=True)
    g = gather_finish(gfull.at[0], sems, 5).reshape(512, RHS)
    u = correct_start(w, wpk, g, ssend.at[0], srecv.at[0], 20)
    fence()
    x = pick_cols(di_v[...], near) * jnp.broadcast_to(tie, (NB, 128)).T[0:1, :]
    s = pieces(pick_cols(ab, pb) - tie * pick(near, x))
    z1 = swap_finish(u, pkt, ssend.at[0], srecv.at[0], sems, 20)
    t1 = dot6(s, z1)
    swap_start(t1, pk, ssend.at[1], srecv.at[1], sems, 22)
    fence()
    gather_start(jnp.concatenate([k0, part(c, z1), part(z1, t1), jnp.zeros((1, RHS), F32)], axis=0), sums1, sems, 11)
    at1 = swap_finish(t1, pkt, ssend.at[1], srecv.at[1], sems, 22)
    f = wt * at1
    hsend[1] = dot6(p64, f)
    owner_start(hsend.at[1], hrecv.at[1], sems, 13)
    fence()
    w = wt * dot6(nbb, f)
    wpk = pick(pk, w)
    gather_start(owner_finish(hsend.at[1], hrecv.at[1], sems, 13)[0:4], gfull.at[1], sems, 14)
    fence()
    swap_start(lb, pk, send.at[1], recv.at[1], sems, 28)
    sums = jnp.sum(gather_finish(sums1, sems, 11), axis=0)
    k0s = sums[0:1]
    g0 = k0s + sums[1:2]
    s1 = g0 / (k0s + sums[2:3])
    g = gather_finish(gfull.at[1], sems, 14).reshape(512, RHS)
    u = correct_start(w, wpk, g, ssend.at[2], srecv.at[2], 24)
    z2 = swap_finish(u, pkt, ssend.at[2], srecv.at[2], sems, 24)
    t2 = dot6(s, z2)
    zp, tp, cp = z1 - s1 * z2, t1 - s1 * t2, c - s1 * t1
    gather_start(jnp.concatenate([part(cp, zp), part(zp, tp)], axis=0), sums2, sems, 16)
    fence()
    swap_start(t2, pk, ssend.at[3], srecv.at[3], sems, 26)
    fence()
    al = swap_finish(lb, pkt, send.at[1], recv.at[1], sems, 28)
    x1, x2_, _ = pieces(x)
    both1, both2, _ = pieces(jnp.concatenate([z1, zp], axis=1))
    xz = mm(x1, both1) + (mm(x1, both2) + mm(x2_, both1))
    at2 = swap_finish(t2, pkt, ssend.at[3], srecv.at[3], sems, 26)
    last = jnp.sum(gather_finish(sums2, sems, 16), axis=0)
    rest = 1.0 - s1
    g1 = rest * rest * k0s + last[0:1]
    beta = g1 / g0
    s2 = g1 / (rest * rest * k0s + last[1:2] - beta * g1 / s1)

    xb = s1 * z1 + s2 * (zp + beta * z1)
    xi = (s1 + s2 * (rest + beta)) * start - (s1 + s2 * beta) * xz[:, :RHS] - s2 * xz[:, RHS:]
    kappa = rest * (1.0 - s2) - s2 * beta
    ae = al - ac
    rb = kappa * ae + (ac - s1 * at1) - s2 * ((at1 - s1 * at2) + beta * at1)
    parts_ref[pl.ds(AT[0], NB), :], parts_ref[pl.ds(AT[1], NI), :] = xb, xi
    parts_ref[pl.ds(AT[2], NB), :], parts_ref[pl.ds(AT[3], NI), :] = rb, kappa * li


AT = (0, NB, NB + 344, 2 * NB + 344)


def spread(parts_ref, sol_ref, res_ref):
    for i, j, parts in SPLIT:
        for inner, k, r, c in parts:
            there = pl.ds(k, c)
            sol_ref[i, j, there, :] = parts_ref[pl.ds(AT[inner] + r, c), :]
            res_ref[i, j, there, :] = parts_ref[pl.ds(AT[2 + inner] + r, c), :]


def local(load, a, di, n, phi):
    tables = [jnp.asarray(v) for v in (B_COL, NEAR_NODE, NEAR, K_COL, K_COL.T, WEIGHT, S64, TMASK, SPREAD)]
    V = lambda *s: pltpu.VMEM(s, F32)
    shape = jax.ShapeDtypeStruct((M, M, M, RHS), F32)
    parts = pl.pallas_call(
        program,
        out_shape=jax.ShapeDtypeStruct((2 * NB + 688, RHS), F32),
        in_specs=[pl.BlockSpec(memory_space=pl.ANY)] * 5 + [VM] * len(tables),
        out_specs=VM,
        scratch_shapes=[
            V(M, M, M, RHS), V(NODES, NODES), V(NODES, NODES), V(NB, NODES), V(NB, NODES), V(NI, NI), V(20, NODES), V(NB, RHS), V(NI, RHS),
            V(2, NS, RHS), V(2, NS, RHS), V(4, NS, RHS), V(4, NS, RHS),
            V(64, 128), V(64, 128), V(2, 64, 128), V(2, 64, 128), V(128, 4, 128), V(2, 128, 4, 128),
            V(128, 4, 128), V(128, 2, 128), V(512, 512), V(2, 64, 128), V(1, 64, 128), V(1, 128, 128), V(2, 8, 128),
            pltpu.SemaphoreType.DMA((60,)), pltpu.SemaphoreType.DMA((5,)),
        ],
        compiler_params=pltpu.CompilerParams(vmem_limit_bytes=60 * 2**20, collective_id=0, has_side_effects=True),
        name="program",
    )(load, a.reshape(NODES, 1, NODES), di.reshape(NI, 1, NI), n.reshape(NODES, 1, NODES), phi.reshape(20, 1, NODES), *tables)
    return tuple(pl.pallas_call(
        spread, out_shape=[shape, shape], in_specs=[VM], out_specs=[VM] * 2,
        compiler_params=pltpu.CompilerParams(vmem_limit_bytes=16 * 2**20), name="spread",
    )(parts))


def solution(mesh):
    spec4, spec5 = P("gx", "gy", "gz", None), P("gx", "gy", "gz", None, None)
    return jax.shard_map(
        local, mesh=mesh, in_specs=(spec4, spec5, spec5, spec5, spec5), out_specs=(spec4, spec4), check_vma=False
    )
```
